32 devices in a mesh: groups: 2 (over y), slide: 4 (over x, core), band: 4 (over z).
Axes of the slice: x: 2, y: 2, z: 4, core: 2. Of those that a mesh axis runs over, the one named last changes fastest.
Arguments:
- features: bfloat16 [8, 4, 256, 192], P(('groups', 'slide'), 'band'), parts along dimension 0, may hold values from -6 to 6
- tissue: int32 [8, 4, 2], P(('groups', 'slide'), 'band'), parts along dimension 0, may hold values 0 or 1
- cotangent: bfloat16 [8, 4, 256, 192], P(('groups', 'slide'), None, 'band'), parts along dimension 0, may hold values from -6 to 6
- x_proj: float32 [4, 192, 38], replicated, may hold values from -0.4375 to 0.4375
- dt_proj: float32 [4, 6, 192], replicated, may hold values from -2.5 to 2.5
- dt_bias: float32 [4, 192], replicated, may hold values from -6 to -2
- a_log: float32 [4, 16, 192], replicated, may hold values from 0 to 2.77
- d_skip: float32 [4, 192], replicated, may hold values from 0.5 to 1.5
Outputs:
- mixed: bfloat16 [8, 4, 256, 192], P(('groups', 'slide'), None, 'band'), parts along dimension 0
- grad_features: bfloat16 [8, 4, 256, 192], P(('groups', 'slide'), 'band'), parts along dimension 0
- grad_x_proj: float32 [8, 192, 38], P('groups'), parts along dimension 0
- grad_dt_proj: float32 [8, 6, 192], P('groups'), parts along dimension 0
- grad_dt_bias: float32 [8, 192], P('groups'), parts along dimension 0
- grad_a_log: float32 [8, 16, 192], P('groups'), parts along dimension 0
- grad_d_skip: float32 [8, 192], P('groups'), parts along dimension 0
The draws below stay inside these ranges and needn't reach their ends.
There are 2 independent parts, one for each index of `groups`. The reference program is written for one: setup_inputs(seed, part) draws one part's arguments, and reference() takes and returns one part's arrays. A program takes and returns all parts, laid end to end along the dimension named above; an argument that names none is the same for every part. Nothing has to cross between parts.
Inputs may be any that keep to these rules, and one draw needn't show every extreme that they name: 1 marks a tile of 128 tokens of one row that holds tissue, 0 one without.
All inputs are finite; a program needn't handle non-finite values. No bound on the sum of `tissue` on one device may be relied on, other than what follows from the above.
Results may differ from the reference program's by a relative error of at most 0.015.
Values may be sent and summed in bfloat16 or wider, within the bound.
No kernel may reach another device: no remote copies, remote signals or barrier semaphores. Data moves between devices by JAX's collectives and lax.ppermute only.
A program may use at most 192 MiB of HBM per device.

```python
import jax
import jax.numpy as jnp
from jax import lax

C = 192
N = 16
R = 6
K = 4
TILE = 128
W = 256
SLIDES = 4
H = 4
WT = 2


def plant(values, stream_key, least, top_value):
    spot = [jax.random.randint(jax.random.fold_in(stream_key, axis), (), 0, length) for axis, length in enumerate(values.shape)]
    widest = values.shape.index(max(values.shape))
    beside = spot[:widest] + [(spot[widest] + 1) % values.shape[widest]] + spot[widest + 1:]
    return values.at[tuple(spot)].set(least).at[tuple(beside)].set(top_value)


def levels(key, extent, split, least, top_value):
    level, own = 1.0, jax.random.fold_in(key, 6)
    for axis_at, blocks in split:
        heights = jnp.exp(jax.random.uniform(jax.random.fold_in(own, axis_at), (blocks,), jnp.float32, least / len(split), top_value / len(split)))
        level = level * jnp.repeat(heights, extent[axis_at] // blocks).reshape([-1 if axis == axis_at else 1 for axis in range(len(extent))])
    return level


def scatter_about(rng, dims, spread, bound, pieces=(), held_as=jnp.bfloat16):
    array = jax.random.normal(rng, dims, jnp.float32) * spread
    if len(pieces) > 0:
        array = levels(rng, dims, pieces, -0.22, 0.18) * array
    return jnp.clip(array, min=-bound, max=bound).astype(held_as)


def setup_inputs(seed: int = 0, part: int = 0) -> dict:
    streams_of = jax.random.split(jax.random.key(seed), 9)
    part_splits = jax.random.split(jax.random.fold_in(streams_of[8], part), 9)
    return {
        "features": scatter_about(part_splits[0], (SLIDES, H, W, C), 1.0, 6.0, ((0, 4), (1, 4))),
        "tissue": plant((jax.random.randint(part_splits[1], (SLIDES, H, WT), 0, 4) < 3).astype(jnp.int32), jax.random.fold_in(part_splits[1], 1), 0, 1),
        "cotangent": scatter_about(part_splits[2], (SLIDES, H, W, C), 1.0, 6.0, ((0, 4), (2, 4))),
        "x_proj": scatter_about(streams_of[3], (K, C, R + 2 * N), C ** -0.5, 0.4375, (), jnp.float32),
        "dt_proj": scatter_about(streams_of[4], (K, R, C), R ** -0.5, 2.5, (), jnp.float32),
        "dt_bias": jnp.clip(jax.random.uniform(streams_of[5], (K, C), jnp.float32, -6.0, -2.0), -6.0, -2.0),
        "a_log": jnp.clip(jax.random.uniform(streams_of[6], (K, N, C), jnp.float32, 0.0, 2.77), 0.0, 2.77),
        "d_skip": jnp.clip(1.0 + 0.1 * jax.random.normal(streams_of[7], (K, C), jnp.float32), 0.5, 1.5),
    }


def direction_scan(inputs, keep_mask, x_weight, dt_weight, dt_offset, log_rate, skip_gain, reverse):
    masked = inputs * keep_mask[:, :, None]
    projected = jnp.einsum('lbc,cr->lbr', masked, x_weight, precision=lax.Precision.HIGHEST)
    rank_size = dt_weight.shape[0]
    state_size = log_rate.shape[0]
    low_rank = projected[:, :, :rank_size]
    b_coef = projected[:, :, rank_size:rank_size + state_size]
    c_coef = projected[:, :, rank_size + state_size:]
    step_size = jax.nn.softplus(jnp.einsum('lbr,rc->lbc', low_rank, dt_weight, precision=lax.Precision.HIGHEST) + dt_offset) * keep_mask[:, :, None]
    decay_rate = -jnp.exp(log_rate)

    def advance(state_now, item):
        step_now, inputs_now, b_now, c_now = item
        state_now = jnp.exp(step_now[:, None, :] * decay_rate) * state_now + (step_now * inputs_now)[:, None, :] * b_now[:, :, None]
        return (state_now, lax.optimization_barrier(jnp.sum(c_now[:, :, None] * state_now, axis=1)))
    start = jnp.zeros((inputs.shape[1], state_size, inputs.shape[2]), jnp.float32)
    _, outputs = lax.scan(advance, start, (step_size, masked, b_coef, c_coef), reverse=reverse)
    return outputs + skip_gain * masked

def section(field, keep_mask, section_params, scan_axis):
    sequence = jnp.moveaxis(field, scan_axis, 0)
    seq_shape = sequence.shape
    sequence = sequence.reshape(seq_shape[0], -1, seq_shape[-1])
    mask_seq = jnp.moveaxis(keep_mask, scan_axis, 0).reshape(seq_shape[0], -1)
    x_weight, dt_weight, dt_offset, log_rate, skip_gain = section_params
    summed = direction_scan(sequence, mask_seq, x_weight[0], dt_weight[0], dt_offset[0], log_rate[0], skip_gain[0], False)
    summed = summed + direction_scan(sequence, mask_seq, x_weight[1], dt_weight[1], dt_offset[1], log_rate[1], skip_gain[1], True)
    return jnp.moveaxis(summed.reshape(seq_shape), 0, scan_axis)

def reference(features, tissue, cotangent, x_proj, dt_proj, dt_bias, a_log, d_skip):
    keep_mask = jnp.repeat(tissue, TILE, axis=2).astype(jnp.float32)
    weights = (x_proj, dt_proj, dt_bias, a_log, d_skip)
    horiz_params = tuple((weight[:2] for weight in weights))
    vert_params = tuple((weight[2:] for weight in weights))

    def horizontal(feature_in, section_params):
        return section(feature_in.astype(jnp.float32), keep_mask, section_params, 2)

    def vertical(carried_in, section_params):
        return section(carried_in.astype(jnp.float32), keep_mask, section_params, 1)
    rows_out, pull_rows = jax.vjp(horizontal, features, horiz_params)
    carried = rows_out.astype(jnp.bfloat16)
    cols_out, pull_cols = jax.vjp(vertical, carried, vert_params)
    grad_carried, grad_vert = pull_cols(cotangent.astype(jnp.float32))
    grad_features, grad_horiz = pull_rows(grad_carried.astype(jnp.float32))
    joined = tuple((jnp.concatenate([first_part, second_part], axis=0) for first_part, second_part in zip(grad_horiz, grad_vert)))
    return (cols_out.astype(jnp.bfloat16), grad_features, joined[0], joined[1], joined[2], joined[3], joined[4])
```

```python
import functools

import jax
import jax.numpy as jnp
import numpy as np
from jax import lax
from jax.experimental import pallas as pl
from jax.experimental.pallas import tpu as pltpu
from jax.sharding import PartitionSpec as P

F32 = jnp.float32
BF16 = jnp.bfloat16
LANES = 128
SUB = 8
LOG2E = 1.4426950408889634
LN2 = 0.6931471805599453


def dot(a, b, dims=((1,), (0,))):
    return lax.dot_general(a, b, (dims, ((), ())), preferred_element_type=F32)


def split(x):
    hi = x.astype(BF16)
    return hi, (x - hi.astype(F32)).astype(BF16)


def swap64(x):
    return pltpu.roll(x, LANES // 2, axis=1)


def lane_iota(rows):
    return lax.broadcasted_iota(jnp.int32, (rows, LANES), 1)


def pack_tiles(a0, b0, a1, b1):
    low = lane_iota(a0.shape[0]) < LANES // 2
    return [a0, jnp.where(low, b0, swap64(b1)), a1]


class Plan:
    def __init__(self, steps, lines, chunked, channels, states, rank):
        self.steps, self.lines, self.chunked = steps, lines, chunked
        self.rows = steps * lines
        self.groups = lines // SUB
        self.channels, self.states, self.rank = channels, states, rank
        self.half = LANES // 2
        self.unroll = next(k for k in (8, 4, 2, 1) if steps % k == 0)

    def perm(self):
        r = np.arange(self.rows)
        s, j = r // self.lines, r % self.lines
        if self.chunked:
            first = j * self.steps + s
            second = self.rows - 1 - first
        else:
            first = r
            second = (self.steps - 1 - s) * self.lines + j
        hot = np.zeros((self.rows, 2 * self.rows), np.float32)
        hot[r, first] = 1.0
        hot[r, self.rows + second] = 1.0
        back = np.concatenate([hot[:, : self.rows].T, hot[:, self.rows :].T], axis=1)
        return jnp.asarray(hot, BF16), jnp.asarray(back, BF16)


def load_weights(plan, x_ref, dtp_ref, bias_ref, alog_ref, skip_ref, w):
    ch, nst = plan.channels, plan.states
    rest = ch - LANES
    wide = x_ref.shape[2]
    w["x"][...] = jnp.zeros_like(w["x"])
    w["x"][0:ch, 0:wide] = x_ref[0]
    w["x"][LANES + plan.half : LANES + plan.half + rest, plan.half : plan.half + wide] = x_ref[1, LANES:ch, :]
    w["x"][2 * LANES : 3 * LANES, plan.half : plan.half + wide] = x_ref[1, 0:LANES, :]

    def packed(ref, dst, at, count):
        pad = w["pad"]
        pad[0, 0:count, 0:ch] = ref[0]
        pad[1, 0:count, 0:ch] = ref[1]
        rows8 = -(-count // SUB) * SUB
        first, second = pad[0, 0:rows8, :], pad[1, 0:rows8, :]
        tiles = pack_tiles(first[:, :LANES], first[:, LANES:], second[:, :LANES], second[:, LANES:])
        for k in range(3):
            dst[at : at + rows8, k * LANES : (k + 1) * LANES] = tiles[k]

    w["pad"][...] = jnp.zeros_like(w["pad"])
    packed(bias_ref, w["small"], 0, 1)
    packed(skip_ref, w["small"], SUB, 1)
    packed(alog_ref, w["small"], 2 * SUB, nst)
    rates = -jnp.exp(w["small"][2 * SUB : 2 * SUB + nst, :])
    w["small"][2 * SUB : 2 * SUB + nst, :] = rates
    for n in range(nst):
        w["rate"][n] = jnp.broadcast_to(rates[n : n + 1, :] * LOG2E, (SUB, 3 * LANES))
    w["pad"][...] = jnp.zeros_like(w["pad"])
    w["dtp"][...] = jnp.zeros_like(w["dtp"])
    pad = w["pad"]
    pad[0, 0 : plan.rank, 0:ch] = dtp_ref[0]
    pad[1, 0 : plan.rank, 0:ch] = dtp_ref[1]
    a0, b0 = pad[0, 0:SUB, 0:LANES], pad[0, 0:SUB, LANES:]
    a1, b1 = pad[1, 0:SUB, 0:LANES], swap64(pad[1, 0:SUB, LANES:])
    low = lane_iota(SUB) < plan.half
    zero = jnp.zeros_like(b0)
    w["dtp"][0:SUB, 0:LANES] = a0
    w["dtp"][0:SUB, LANES : 2 * LANES] = jnp.where(low, b0, zero)
    w["dtp"][plan.half : plan.half + SUB, LANES : 2 * LANES] = jnp.where(low, zero, b1)
    w["dtp"][plan.half : plan.half + SUB, 2 * LANES :] = a1


def place(plan, perm_ref, x256, dst):
    first = dot(perm_ref[:, : plan.rows], x256)
    second = dot(perm_ref[:, plan.rows :], x256)
    a0, b0, a1, b1 = first[:, :LANES], first[:, LANES:], second[:, :LANES], second[:, LANES:]
    for k, tile in enumerate(pack_tiles(a0, b0, a1, b1)):
        dst[:, k * LANES : (k + 1) * LANES] = tile
    return b0, b1


def unplace(plan, back_ref, packed, stack):
    t0, t1, t2 = packed
    stack[0 : plan.rows, 0:LANES] = t0
    stack[0 : plan.rows, LANES:] = t1
    stack[plan.rows :, 0:LANES] = t2
    stack[plan.rows :, LANES:] = swap64(t1)
    hi, lo = split(stack[...])
    return dot(back_ref[...], hi) + dot(back_ref[...], lo)


def prepare(plan, perm_ref, x256, w, t):
    b0, b1 = place(plan, perm_ref, x256, t["u"])
    low = lane_iota(plan.rows) < plan.half
    m0 = jnp.where(low, swap64(b0), b0)
    m1 = jnp.where(low, swap64(b1), b1)
    masks = [m0, jnp.where(low, m0, m1), m1]
    for k in range(3):
        t["m"][:, k * LANES : (k + 1) * LANES] = masks[k]
    u = t["u"][...].astype(BF16)
    x_hi, x_lo = split(w["x"][...])
    proj = dot(u, x_hi) + dot(u, x_lo)
    t["p"][...] = proj
    p_hi, p_lo = split(proj)
    d_hi, d_lo = split(w["dtp"][...])
    z = dot(p_hi, d_hi) + dot(p_lo, d_hi) + dot(p_hi, d_lo) + w["small"][0:1, :]
    t["z"][...] = z
    soft = jnp.maximum(z, 0.0) + jnp.log1p(jnp.exp(-jnp.abs(z)))
    dt = soft * t["m"][...]
    t["dt"][...] = dt
    t["dtu"][...] = dt * t["u"][...]


def coefs(plan, p8, n, which):
    at = plan.rank + which * plan.states + n
    lo = jnp.broadcast_to(p8[:, at : at + 1], (SUB, LANES))
    hi = jnp.broadcast_to(p8[:, plan.half + at : plan.half + at + 1], (SUB, LANES))
    mid = jnp.where(lane_iota(SUB) < plan.half, lo, hi)
    return jnp.concatenate([lo, mid, hi], axis=1)


def over_steps(plan, g, body, carry, backwards=False):
    u = plan.unroll

    def chunk(i, carry):
        for k in range(u):
            s = i * u + k
            if backwards:
                s = plan.steps - 1 - s
            row = s * plan.lines + g * SUB
            if not isinstance(row, int):
                row = pl.multiple_of(row, SUB)
            carry = body(s, row, carry)
        return carry

    if plan.steps == u:
        return chunk(0, carry)
    return lax.fori_loop(0, plan.steps // u, chunk, carry)


def over_groups(plan, body):
    if plan.groups == 1:
        body(0)
    else:
        lax.fori_loop(0, plan.groups, lambda g, c: (body(g), c)[1], 0)


def chunk_scan(decay, end, backwards):
    at = lax.broadcasted_iota(jnp.int32, end.shape, 0)
    for shift in (1, 2, 4):
        if backwards:
            inside, amount = at < SUB - shift, SUB - shift
        else:
            inside, amount = at >= shift, shift
        prev_end, prev_decay = pltpu.roll(end, amount, axis=0), pltpu.roll(decay, amount, axis=0)
        end = jnp.where(inside, decay * prev_end + end, end)
        decay = jnp.where(inside, decay * prev_decay, decay)
    if backwards:
        return jnp.where(at < SUB - 1, pltpu.roll(end, SUB - 1, axis=0), 0.0)
    return jnp.where(at >= 1, pltpu.roll(end, 1, axis=0), 0.0)


def chunk_decay(plan, w, t, n):
    total = functools.reduce(lambda a, b: a + b, [t["dt"][s * SUB : (s + 1) * SUB, :] for s in range(plan.steps)])
    return [jnp.exp2(total * w["rate"][k]) for k in n]


def forward(plan, w, t, keep_states):
    nst, per = plan.states, 8
    zero = jnp.zeros((SUB, 3 * LANES), F32)
    for n0 in range(0, nst, per):
        ns = list(range(n0, n0 + per))

        def group(g, ns=ns, n0=n0):
            start = tuple(zero for _ in ns)
            if plan.chunked:

                def local(s, row, hs):
                    dt, dtu = t["dt"][pl.ds(row, SUB), :], t["dtu"][pl.ds(row, SUB), :]
                    p8 = t["p"][pl.ds(row, SUB), :]
                    return tuple(
                        jnp.exp2(dt * w["rate"][n]) * h + coefs(plan, p8, n, 0) * dtu for n, h in zip(ns, hs)
                    )

                ends = over_steps(plan, g, local, start)
                start = tuple(chunk_scan(d, e, False) for d, e in zip(chunk_decay(plan, w, t, ns), ends))
            if keep_states:
                for n, h in zip(ns, start):
                    t["h"][0, n, pl.ds(g * SUB, SUB), :] = h

            def full(s, row, hs):
                dt, dtu = t["dt"][pl.ds(row, SUB), :], t["dtu"][pl.ds(row, SUB), :]
                p8 = t["p"][pl.ds(row, SUB), :]
                y = t["u"][pl.ds(row, SUB), :] * w["small"][SUB : SUB + 1, :] if n0 == 0 else t["y"][pl.ds(row, SUB), :]
                new = []
                for n, h in zip(ns, hs):
                    h = jnp.exp2(dt * w["rate"][n]) * h + coefs(plan, p8, n, 0) * dtu
                    y = y + coefs(plan, p8, n, 1) * h
                    if keep_states:
                        t["h"][s + 1, n, pl.ds(g * SUB, SUB), :] = h
                    new.append(h)
                t["y"][pl.ds(row, SUB), :] = y
                return tuple(new)

            over_steps(plan, g, full, start)

        over_groups(plan, group)


def dir_sums(plan, x):
    low = lane_iota(SUB) < plan.half
    mid = x[:, LANES : 2 * LANES]
    mid0 = jnp.where(low, mid, 0.0)
    first = jnp.sum(x[:, :LANES] + mid0, axis=1, keepdims=True)
    second = jnp.sum(x[:, 2 * LANES :] + (mid - mid0), axis=1, keepdims=True)
    return first, second


def backward(plan, w, t):
    nst, per = plan.states, 4
    zero = jnp.zeros((SUB, 3 * LANES), F32)
    lane = lane_iota(SUB)
    for n0 in range(0, nst, per):
        ns = list(range(n0, n0 + per))

        def group(g, ns=ns, n0=n0):
            start = tuple(zero for _ in ns)
            if plan.chunked:

                def local(s, row, gs):
                    dt, gy = t["dt"][pl.ds(row, SUB), :], t["gy"][pl.ds(row, SUB), :]
                    p8 = t["p"][pl.ds(row, SUB), :]
                    return tuple(
                        jnp.exp2(dt * w["rate"][n]) * (coefs(plan, p8, n, 1) * gy + c) for n, c in zip(ns, gs)
                    )

                ends = over_steps(plan, g, local, start, backwards=True)
                start = tuple(chunk_scan(d, e, True) for d, e in zip(chunk_decay(plan, w, t, ns), ends))

            def full(s, row, carry):
                gs, rs = carry
                dt, dtu = t["dt"][pl.ds(row, SUB), :], t["dtu"][pl.ds(row, SUB), :]
                gy = t["gy"][pl.ds(row, SUB), :]
                p8 = t["p"][pl.ds(row, SUB), :]
                if n0 == 0:
                    sb, wq, gp = zero, zero, jnp.zeros((SUB, LANES), F32)
                else:
                    sb, wq = t["sb"][pl.ds(row, SUB), :], t["wq"][pl.ds(row, SUB), :]
                    gp = t["gp"][pl.ds(row, SUB), :]
                new_g, new_r = [], []
                for n, c, r in zip(ns, gs, rs):
                    h_now = t["h"][s + 1, n, pl.ds(g * SUB, SUB), :]
                    h_prev = t["h"][s, n, pl.ds(g * SUB, SUB), :]
                    gh = coefs(plan, p8, n, 1) * gy + c
                    at_b, at_c = plan.rank + n, plan.rank + nst + n
                    c0, c1 = dir_sums(plan, gy * h_now)
                    b0, b1 = dir_sums(plan, gh * dtu)
                    gp = jnp.where(lane == at_b, b0, gp)
                    gp = jnp.where(lane == at_b + plan.half, b1, gp)
                    gp = jnp.where(lane == at_c, c0, gp)
                    gp = jnp.where(lane == at_c + plan.half, c1, gp)
                    sb = sb + gh * coefs(plan, p8, n, 0)
                    c = jnp.exp2(dt * w["rate"][n]) * gh
                    q = c * h_prev
                    wq = wq + q * w["rate"][n]
                    new_g.append(c)
                    new_r.append(r + q * dt)
                t["sb"][pl.ds(row, SUB), :] = sb
                t["wq"][pl.ds(row, SUB), :] = wq
                t["gp"][pl.ds(row, SUB), :] = gp
                return tuple(new_g), tuple(new_r)

            _, rs = over_steps(plan, g, full, (start, tuple(zero for _ in ns)), backwards=True)
            for n, r in zip(ns, rs):
                if plan.groups == 1:
                    t["gr"][n] = r
                else:
                    t["gr"][n] = r + jnp.where(g == 0, 0.0, 1.0) * t["gr"][n]

        if plan.groups > 1:
            for n in ns:
                t["gr"][n] = zero
        over_groups(plan, group)


def finish(plan, back_ref, w, t, grads_ref, natural_mask):
    nst, rank = plan.states, plan.rank
    u, dt, gy, sb = t["u"][...], t["dt"][...], t["gy"][...], t["sb"][...]
    g_dt = t["wq"][...] * LN2 + sb * u
    gz = g_dt * t["m"][...] * (1.0 / (1.0 + jnp.exp(-t["z"][...])))
    gz_b = gz.astype(BF16)
    dtp_b = w["dtp"][...].astype(BF16)
    gp = t["gp"][...] + dot(gz_b, dtp_b, ((1,), (1,)))
    gp_b = gp.astype(BF16)
    u_b = u.astype(BF16)
    g_x = dot(gp_b, u_b, ((0,), (0,)))
    g_d = dot(t["p"][...].astype(BF16), gz_b, ((0,), (0,)))
    lane = lax.broadcasted_iota(jnp.int32, (SUB, 3 * LANES), 1)
    first = lane < plan.channels
    wide = -(-(rank + 2 * nst) // SUB) * SUB
    for r in range(0, wide, SUB):
        grads_ref[r : r + SUB, :] = jnp.where(first, g_x[r : r + SUB, :], g_x[plan.half + r : plan.half + r + SUB, :])
    row = lax.broadcasted_iota(jnp.int32, (SUB, 3 * LANES), 0)
    small = jnp.where(first, g_d[0:SUB, :], g_d[plan.half : plan.half + SUB, :])
    small = jnp.where(row == SUB - 2, jnp.sum(gz, axis=0, keepdims=True), small)
    small = jnp.where(row == SUB - 1, jnp.sum(gy * u, axis=0, keepdims=True), small)
    grads_ref[wide : wide + SUB, :] = small
    for n in range(nst):
        g_rate = jnp.sum(t["gr"][n], axis=0, keepdims=True)
        grads_ref[wide + SUB + n : wide + SUB + n + 1, :] = g_rate * w["small"][2 * SUB + n : 2 * SUB + n + 1, :]
    gu = sb * dt + gy * w["small"][SUB : SUB + 1, :] + dot(gp_b, w["x"][...].astype(BF16), ((1,), (1,)))
    tiles = [gu[:, k * LANES : (k + 1) * LANES] for k in range(3)]
    out = unplace(plan, back_ref, tiles, t["stack"])
    return out * natural_mask


def weight_scratch(plan):
    return {
        "x": pltpu.VMEM((3 * LANES, LANES), F32),
        "pad": pltpu.VMEM((2, max(plan.states, SUB), 2 * LANES), F32),
        "small": pltpu.VMEM((2 * SUB + plan.states, 3 * LANES), F32),
        "rate": pltpu.VMEM((plan.states, SUB, 3 * LANES), F32),
        "dtp": pltpu.VMEM((LANES, 3 * LANES), F32),
    }


def token_scratch(plan, grads):
    wide = pltpu.VMEM((plan.rows, 3 * LANES), F32)
    narrow = pltpu.VMEM((plan.rows, LANES), F32)
    out = {"u": wide, "m": wide, "z": wide, "dt": wide, "dtu": wide, "y": wide, "p": narrow,
           "x256": pltpu.VMEM((plan.rows, 2 * LANES), F32), "stack": pltpu.VMEM((2 * plan.rows, 2 * LANES), F32)}
    if grads:
        out |= {"gy": wide, "sb": wide, "wq": wide, "gp": narrow,
                "h": pltpu.VMEM((plan.steps + 1, plan.states, plan.lines, 3 * LANES), F32),
                "gr": pltpu.VMEM((plan.states, SUB, 3 * LANES), F32)}
    return out


def row_mask(plan, tissue_ref, width):
    tiles = tissue_ref.shape[0]
    per = plan.rows // tiles
    token = lax.broadcasted_iota(jnp.int32, (plan.rows, width), 0)
    mask = jnp.zeros((plan.rows, width), F32)
    for k in range(tiles):
        inside = (token >= k * per) & (token < (k + 1) * per)
        mask = jnp.where(inside, tissue_ref[k].astype(F32), mask)
    return mask


def masked_rows(plan, tissue_ref, feat_ref, x256):
    ch = plan.channels
    x256[:, 0:ch] = feat_ref[...].astype(F32) * row_mask(plan, tissue_ref, ch)
    x256[:, ch:] = row_mask(plan, tissue_ref, 2 * LANES - ch)
    return x256[...].astype(BF16)


def rows_forward_kernel(plan, tissue_ref, feat_ref, perm_ref, back_ref, x_ref, dtp_ref, bias_ref, alog_ref, skip_ref,
                        send_ref, w, t):
    load_weights(plan, x_ref, dtp_ref, bias_ref, alog_ref, skip_ref, w)
    x256 = masked_rows(plan, tissue_ref, feat_ref, t["x256"])
    prepare(plan, perm_ref, x256, w, t)
    forward(plan, w, t, False)
    tiles = [t["y"][:, k * LANES : (k + 1) * LANES] for k in range(3)]
    out = unplace(plan, back_ref, tiles, t["stack"])
    send_ref[...] = out.astype(BF16)
    send_ref[:, plan.channels :] = row_mask(plan, tissue_ref, 2 * LANES - plan.channels).astype(BF16)


def rows_backward_kernel(plan, tissue_ref, feat_ref, gy_ref, perm_ref, back_ref, x_ref, dtp_ref, bias_ref, alog_ref,
                         skip_ref, out_ref, grads_ref, w, t):
    load_weights(plan, x_ref, dtp_ref, bias_ref, alog_ref, skip_ref, w)
    x256 = masked_rows(plan, tissue_ref, feat_ref, t["x256"])
    prepare(plan, perm_ref, x256, w, t)
    t["x256"][:, 0 : plan.channels] = gy_ref[...].astype(F32)
    place(plan, perm_ref, t["x256"][...].astype(BF16), t["gy"])
    forward(plan, w, t, True)
    backward(plan, w, t)
    out = finish(plan, back_ref, w, t, grads_ref, row_mask(plan, tissue_ref, 2 * LANES))
    out_ref[...] = out[:, : plan.channels].astype(BF16)


def columns_kernel(plan, recv_ref, gy_ref, perm_ref, back_ref, x_ref, dtp_ref, bias_ref, alog_ref, skip_ref,
                   mixed_ref, out_ref, grads_ref, w, t):
    ch = plan.channels
    load_weights(plan, x_ref, dtp_ref, bias_ref, alog_ref, skip_ref, w)
    recv = recv_ref[...].astype(F32)
    low = lane_iota(plan.rows) < plan.half
    last = recv[:, LANES:]
    mask = jnp.where(low, swap64(last), last)
    t["x256"][:, 0:LANES] = recv[:, :LANES] * mask
    t["x256"][:, LANES:] = last * mask
    prepare(plan, perm_ref, t["x256"][...].astype(BF16), w, t)
    t["x256"][:, 0:ch] = gy_ref[...].astype(F32)
    place(plan, perm_ref, t["x256"][...].astype(BF16), t["gy"])
    forward(plan, w, t, True)
    tiles = [t["y"][:, k * LANES : (k + 1) * LANES] for k in range(3)]
    mixed = unplace(plan, back_ref, tiles, t["stack"])
    mixed_ref[...] = mixed[:, :ch].astype(BF16)
    backward(plan, w, t)
    out = finish(plan, back_ref, w, t, grads_ref, jnp.concatenate([mask, mask], axis=1))
    out_ref[...] = out[:, :ch].astype(BF16)


def unpack_kernel(plan, rows_ref, cols_ref, gx_ref, gd_ref, gb_ref, ga_ref, gs_ref):
    nst, rank, ch, half = plan.states, plan.rank, plan.channels, plan.half
    wide = rank + 2 * nst
    up = -(-wide // SUB) * SUB
    for side, ref in enumerate((rows_ref, cols_ref)):
        tiles = [ref[:, k * LANES : (k + 1) * LANES] for k in range(3)]
        other = swap64(tiles[1])
        for d, (a, b) in enumerate(((tiles[0], tiles[1]), (tiles[2], other))):
            k = 2 * side + d
            gx_ref[k, 0:LANES, :] = jnp.transpose(a[0:up, :])[:, :wide]
            gx_ref[k, LANES:ch, :] = jnp.transpose(b[0:up, :])[0 : ch - LANES, :wide]
            for lo, hi, part in ((0, LANES, a), (LANES, ch, b[:, : ch - LANES])):
                gd_ref[k, :, lo:hi] = part[up : up + rank, :]
                gb_ref[k : k + 1, lo:hi] = part[up + SUB - 2 : up + SUB - 1, :]
                gs_ref[k : k + 1, lo:hi] = part[up + SUB - 1 : up + SUB, :]
                ga_ref[k, :, lo:hi] = part[up + SUB : up + SUB + nst, :]


def call(kernel, plan, out_shape, ins, side, grads, name):
    specs, args = [], []
    for array, kind in ins:
        args.append(array)
        if kind == "s":
            specs.append(pl.BlockSpec(memory_space=pltpu.SMEM))
        elif kind == "w":
            block = (2,) + array.shape[1:]
            specs.append(pl.BlockSpec(block, functools.partial(lambda nd, i: (side,) + (0,) * (nd - 1), array.ndim)))
        else:
            specs.append(pl.BlockSpec(array.shape, functools.partial(lambda nd, i: (0,) * nd, array.ndim)))
    outs = jax.tree.map(lambda s: pl.BlockSpec(s.shape, functools.partial(lambda nd, i: (0,) * nd, len(s.shape))), out_shape)
    scratch = [weight_scratch(plan), token_scratch(plan, grads)]
    return pl.pallas_call(
        functools.partial(kernel, plan), out_shape=out_shape, grid=(1,), in_specs=specs, out_specs=outs,
        scratch_shapes=scratch, name=name,
    )(*args)


def reduce_all(x, axes):
    for axis in axes:
        size = lax.axis_size(axis)
        step = 1
        while step < size:
            mine = x.astype(BF16)
            theirs = lax.ppermute(mine, axis, [(i, i ^ step) for i in range(size)])
            x = mine.astype(F32) + theirs.astype(F32)
            step *= 2
    return x


def shards(features, tissue, cotangent, x_proj, dt_proj, dt_bias, a_log, d_skip):
    slides, rows_here, width, channels = features.shape
    _, height, cols_here, _ = cotangent.shape
    bands = lax.axis_size("band")
    dirs, rank, states = dt_proj.shape[0], dt_proj.shape[1], a_log.shape[1]
    half = dirs // 2
    rows_plan = Plan(width // SUB, SUB, True, channels, states, rank)
    cols_plan = Plan(height, cols_here, False, channels, states, rank)
    bias3, skip3 = dt_bias.reshape(dirs, 1, channels), d_skip.reshape(dirs, 1, channels)
    weights = [(x_proj, "w"), (dt_proj, "w"), (bias3, "w"), (a_log, "w"), (skip3, "w")]
    feat = features.reshape(width, channels)
    keep = tissue.reshape(-1)
    packed = -(-(rank + 2 * states) // SUB) * SUB + SUB + states
    grads_shape = jax.ShapeDtypeStruct((packed, 3 * LANES), F32)

    perm, back = rows_plan.perm()
    send = call(rows_forward_kernel, rows_plan, jax.ShapeDtypeStruct((width, 2 * LANES), BF16),
                [(keep, "s"), (feat, ""), (perm, ""), (back, "")] + weights, 0, False, "rows_forward")
    moved = lax.all_to_all(send.reshape(bands, cols_here, 2 * LANES), "band", split_axis=0, concat_axis=0, tiled=True)
    cperm, cback = cols_plan.perm()
    tokens = height * cols_here
    token_shape = jax.ShapeDtypeStruct((tokens, channels), BF16)
    mixed, grad_carried, grads_v = call(
        columns_kernel, cols_plan, (token_shape, token_shape, grads_shape),
        [(moved.reshape(tokens, 2 * LANES), ""), (cotangent.reshape(tokens, channels), ""), (cperm, ""), (cback, "")] + weights,
        1, True, "columns")
    returned = lax.all_to_all(grad_carried.reshape(bands, cols_here, channels), "band", split_axis=0, concat_axis=0, tiled=True)
    grad_features, grads_h = call(
        rows_backward_kernel, rows_plan, (jax.ShapeDtypeStruct((width, channels), BF16), grads_shape),
        [(keep, "s"), (feat, ""), (returned.reshape(width, channels), ""), (perm, ""), (back, "")] + weights,
        0, True, "rows_backward")
    both = reduce_all(jnp.stack([grads_h, grads_v]), ("slide", "band"))
    shapes = [(dirs, channels, rank + 2 * states), (dirs, rank, channels), (dirs, channels), (dirs, states, channels), (dirs, channels)]
    outs = pl.pallas_call(
        functools.partial(unpack_kernel, rows_plan), out_shape=[jax.ShapeDtypeStruct(s, F32) for s in shapes], name="unpack",
    )(both[0], both[1])
    return (mixed.reshape(cotangent.shape), grad_features.reshape(features.shape), *outs)


def solution(mesh):
    in_specs = (
        P(("groups", "slide"), "band", None, None),
        P(("groups", "slide"), "band", None),
        P(("groups", "slide"), None, "band", None),
        P(), P(), P(), P(), P(),
    )
    out_specs = (
        P(("groups", "slide"), None, "band", None),
        P(("groups", "slide"), "band", None, None),
        P("groups", None, None),
        P("groups", None, None),
        P("groups", None),
        P("groups", None, None),
        P("groups", None),
    )
    return jax.shard_map(shards, mesh=mesh, in_specs=in_specs, out_specs=out_specs, check_vma=False)
```

```python
import functools

import jax
import jax.numpy as jnp
import numpy as np
from jax import lax
from jax.experimental import pallas as pl
from jax.experimental.pallas import tpu as pltpu
from jax.sharding import PartitionSpec as P

F32 = jnp.float32
BF16 = jnp.bfloat16
LANES = 128
SUB = 8
LOG2E = 1.4426950408889634
LN2 = 0.6931471805599453
VMEM_LIMIT = 34 * 2**20


def dot(a, b, dims=((1,), (0,))):
    return lax.dot_general(a, b, (dims, ((), ())), preferred_element_type=F32)


def split(x):
    hi = x.astype(BF16)
    return hi, (x - hi.astype(F32)).astype(BF16)


def swap64(x):
    return pltpu.roll(x, LANES // 2, axis=1)


def lane_iota(rows):
    return lax.broadcasted_iota(jnp.int32, (rows, LANES), 1)


def pack_tiles(a0, b0, a1, b1):
    low = lane_iota(a0.shape[0]) < LANES // 2
    return [a0, jnp.where(low, b0, swap64(b1)), a1]


class Plan:
    def __init__(self, steps, lines, chunked, channels, states, rank):
        self.steps, self.lines, self.chunked = steps, lines, chunked
        self.rows = steps * lines
        self.groups = lines // SUB
        self.channels, self.states, self.rank = channels, states, rank
        self.half = LANES // 2
        self.unroll = next(k for k in (8, 4, 2, 1) if steps % k == 0)

    def reverse(self, x):
        return jnp.concatenate([x[s * self.lines : (s + 1) * self.lines] for s in reversed(range(self.steps))], axis=0)

    def perm(self):
        r = np.arange(self.rows)
        s, j = r // self.lines, r % self.lines
        first = j * self.steps + s
        second = self.rows - 1 - first
        hot = np.zeros((self.rows, 2 * self.rows), np.float32)
        hot[r, first] = 1.0
        hot[r, self.rows + second] = 1.0
        back = np.concatenate([hot[:, : self.rows].T, hot[:, self.rows :].T], axis=1)
        return jnp.asarray(hot, BF16), jnp.asarray(back, BF16)


def load_weights(plan, side, x_ref, dtp_ref, bias_ref, alog_ref, skip_ref, w):
    ch, nst = plan.channels, plan.states
    pad, half = w["pad"], plan.half
    pad[:, :, ch:] = jnp.zeros((2, pad.shape[1], 2 * LANES - ch), F32)

    def halves(rows):
        first, second = pad[0, 0:rows, :], pad[1, 0:rows, :]
        return first[:, :LANES], first[:, LANES:], second[:, :LANES], second[:, LANES:]

    def diagonal(ref, dst):
        count = ref.shape[0]
        rows = -(-count // SUB) * SUB
        dst[...] = jnp.zeros_like(dst)
        for d in range(2):
            pad[d, rows - SUB : rows, 0:ch] = jnp.zeros((SUB, ch), F32)
            pad[d, 0:count, 0:ch] = ref[:, 2 * side + d, :]
        a0, b0, a1, b1 = halves(rows)
        dst[0:rows, 0:LANES] = a0
        dst[0:rows, LANES : 2 * LANES] = b0
        dst[half : half + rows, LANES : 2 * LANES] = swap64(b1)
        dst[half : half + rows, 2 * LANES :] = a1

    diagonal(x_ref, w["x"])
    diagonal(dtp_ref, w["dtp"])
    for d in range(2):
        pad[d, 0:1, 0:ch] = bias_ref[2 * side + d : 2 * side + d + 1, :]
        pad[d, SUB : SUB + 1, 0:ch] = skip_ref[2 * side + d : 2 * side + d + 1, :]
        pad[d, 2 * SUB : 2 * SUB + nst, 0:ch] = alog_ref[2 * side + d]
    tiles = pack_tiles(*halves(2 * SUB + nst))
    for k in range(3):
        at = slice(k * LANES, (k + 1) * LANES)
        w["small"][0 : 2 * SUB, at] = tiles[k][0 : 2 * SUB]
        rates = -jnp.exp(tiles[k][2 * SUB :])
        w["small"][2 * SUB :, at] = rates
        for n in range(nst):
            w["rate"][n, :, at] = jnp.broadcast_to(rates[n : n + 1, :] * LOG2E, (SUB, LANES))


def place(plan, perm_ref, x, dst, tall=False):
    if plan.chunked:
        dims = ((1,), (1,)) if tall else ((1,), (0,))
        first = dot(perm_ref[:, : plan.rows], x, dims)
        second = dot(perm_ref[:, plan.rows :], x, dims)
    else:
        first, second = x, plan.reverse(x)
    a0, b0, a1, b1 = first[:, :LANES], first[:, LANES:], second[:, :LANES], second[:, LANES:]
    for k, tile in enumerate(pack_tiles(a0, b0, a1, b1)):
        dst[:, k * LANES : (k + 1) * LANES] = tile
    return b0, b1


def unplace(plan, back_ref, packed, stack):
    t0, t1, t2 = packed
    if not plan.chunked:
        return t0 + plan.reverse(t2), t1 + plan.reverse(swap64(t1))
    stack[0 : plan.rows, 0:LANES] = t0
    stack[0 : plan.rows, LANES:] = t1
    stack[plan.rows :, 0:LANES] = t2
    stack[plan.rows :, LANES:] = swap64(t1)
    hi, lo = split(stack[...])
    out = dot(back_ref[...], hi) + dot(back_ref[...], lo)
    return out[:, :LANES], out[:, LANES:]


def prepare(plan, perm_ref, x256, w, t):
    b0, b1 = place(plan, perm_ref, x256, t["u"], plan.chunked)
    low = lane_iota(plan.rows) < plan.half
    m0 = jnp.where(low, swap64(b0), b0)
    m1 = jnp.where(low, swap64(b1), b1)
    masks = [m0, jnp.where(low, m0, m1), m1]
    for k in range(3):
        t["m"][:, k * LANES : (k + 1) * LANES] = masks[k]
    u = t["u"][...].astype(BF16)
    x_hi, x_lo = split(w["x"][...])
    proj = dot(u, x_hi, ((1,), (1,))) + dot(u, x_lo, ((1,), (1,)))
    t["p"][...] = proj
    p_hi, p_lo = split(proj)
    d_hi, d_lo = split(w["dtp"][...])
    z = dot(p_hi, d_hi) + dot(p_lo, d_hi) + dot(p_hi, d_lo) + w["small"][0:1, :]
    t["z"][...] = z
    soft = jnp.maximum(z, 0.0) + jnp.log1p(jnp.exp(-jnp.abs(z)))
    dt = soft * t["m"][...]
    t["dt"][...] = dt
    t["dtu"][...] = dt * t["u"][...]
    spread(plan, t)


def spread(plan, t):
    k = lax.broadcasted_iota(jnp.int32, (2 * LANES, 2 * LANES), 0) % LANES
    l = lax.broadcasted_iota(jnp.int32, (2 * LANES, 2 * LANES), 1)
    ones = jnp.where((k < plan.half) == (l < LANES), 1.0, 0.0).astype(BF16)
    proj = t["p"][...]
    hi = proj.astype(BF16).astype(F32)
    lo = proj - hi
    lane = lane_iota(plan.rows)
    for r in range(2 * plan.states):
        at = plan.rank + r
        mine = (lane == at) | (lane == at + plan.half)
        lhs = jnp.concatenate([jnp.where(mine, hi, 0.0), jnp.where(mine, lo, 0.0)], axis=1).astype(BF16)
        t["bb"][r] = dot(lhs, ones)


def fold(x):
    low = lane_iota(SUB) < LANES // 2
    t0, t1, t2 = x[:, :LANES], x[:, LANES : 2 * LANES], x[:, 2 * LANES :]
    return jnp.concatenate([jnp.where(low, t0, t2) + t1, jnp.where(low, t2, t0)], axis=1)


def gather(plan, t):
    k = lax.broadcasted_iota(jnp.int32, (2 * LANES, LANES), 0)
    l = lax.broadcasted_iota(jnp.int32, (2 * LANES, LANES), 1)
    first = (k < plan.half) | (k >= LANES + plan.half)
    ones = jnp.where(first == (l < plan.half), 1.0, 0.0).astype(BF16)
    lane = lane_iota(plan.rows)
    out = jnp.zeros((plan.rows, LANES), F32)
    for r in range(2 * plan.states):
        at = plan.rank + r
        mine = (lane == at) | (lane == at + plan.half)
        out = jnp.where(mine, dot(t["prod"][r].astype(BF16), ones), out)
    return out


def coefs(plan, t, row, n, which):
    r = which * plan.states + n
    lo = t["bb"][r, pl.ds(row, SUB), 0:LANES]
    hi = t["bb"][r, pl.ds(row, SUB), LANES:]
    mid = jnp.where(lane_iota(SUB) < plan.half, lo, hi)
    return jnp.concatenate([lo, mid, hi], axis=1)


def over_steps(plan, g, body, carry, backwards=False):
    u = plan.unroll

    def chunk(i, carry):
        for k in range(u):
            s = i * u + k
            if backwards:
                s = plan.steps - 1 - s
            row = s * plan.lines + g * SUB
            if not isinstance(row, int):
                row = pl.multiple_of(row, SUB)
            carry = body(s, row, carry)
        return carry

    if plan.steps == u:
        return chunk(0, carry)
    return lax.fori_loop(0, plan.steps // u, chunk, carry)


def over_groups(plan, body):
    if plan.groups == 1:
        body(0)
    else:
        lax.fori_loop(0, plan.groups, lambda g, c: (body(g), c)[1], 0)


def chunk_scan(decay, end, backwards):
    at = lax.broadcasted_iota(jnp.int32, end.shape, 0)
    for shift in (1, 2, 4):
        if backwards:
            inside, amount = at < SUB - shift, SUB - shift
        else:
            inside, amount = at >= shift, shift
        prev_end, prev_decay = pltpu.roll(end, amount, axis=0), pltpu.roll(decay, amount, axis=0)
        end = jnp.where(inside, decay * prev_end + end, end)
        decay = jnp.where(inside, decay * prev_decay, decay)
    if backwards:
        return jnp.where(at < SUB - 1, pltpu.roll(end, SUB - 1, axis=0), 0.0)
    return jnp.where(at >= 1, pltpu.roll(end, 1, axis=0), 0.0)


def chunk_decay(plan, w, t, n):
    total = functools.reduce(lambda a, b: a + b, [t["dt"][s * SUB : (s + 1) * SUB, :] for s in range(plan.steps)])
    return [jnp.exp2(total * w["rate"][k]) for k in n]


def forward(plan, w, t, keep_states):
    nst, per = plan.states, 8
    zero = jnp.zeros((SUB, 3 * LANES), F32)
    for n0 in range(0, nst, per):
        ns = list(range(n0, n0 + per))

        def group(g, ns=ns, n0=n0):
            start = tuple(zero for _ in ns)
            if plan.chunked:

                def local(s, row, hs):
                    dt, dtu = t["dt"][pl.ds(row, SUB), :], t["dtu"][pl.ds(row, SUB), :]
                    return tuple(
                        jnp.exp2(dt * w["rate"][n]) * h + coefs(plan, t, row, n, 0) * dtu for n, h in zip(ns, hs)
                    )

                ends = over_steps(plan, g, local, start)
                start = tuple(chunk_scan(d, e, False) for d, e in zip(chunk_decay(plan, w, t, ns), ends))
            if keep_states:
                for n, h in zip(ns, start):
                    t["h"][0, n, pl.ds(g * SUB, SUB), :] = h

            def full(s, row, hs):
                dt, dtu = t["dt"][pl.ds(row, SUB), :], t["dtu"][pl.ds(row, SUB), :]
                y = t["u"][pl.ds(row, SUB), :] * w["small"][SUB : SUB + 1, :] if n0 == 0 else t["y"][pl.ds(row, SUB), :]
                new = []
                for n, h in zip(ns, hs):
                    h = jnp.exp2(dt * w["rate"][n]) * h + coefs(plan, t, row, n, 0) * dtu
                    y = y + coefs(plan, t, row, n, 1) * h
                    if keep_states:
                        t["h"][s + 1, n, pl.ds(g * SUB, SUB), :] = h
                    new.append(h)
                t["y"][pl.ds(row, SUB), :] = y
                return tuple(new)

            over_steps(plan, g, full, start)

        over_groups(plan, group)


def backward(plan, w, t):
    nst, per = plan.states, 4
    zero = jnp.zeros((SUB, 3 * LANES), F32)
    for n0 in range(0, nst, per):
        ns = list(range(n0, n0 + per))

        def group(g, ns=ns, n0=n0):
            start = tuple(zero for _ in ns)
            if plan.chunked:

                def local(s, row, gs):
                    dt, gy = t["dt"][pl.ds(row, SUB), :], t["gy"][pl.ds(row, SUB), :]
                    return tuple(
                        jnp.exp2(dt * w["rate"][n]) * (coefs(plan, t, row, n, 1) * gy + c) for n, c in zip(ns, gs)
                    )

                ends = over_steps(plan, g, local, start, backwards=True)
                start = tuple(chunk_scan(d, e, True) for d, e in zip(chunk_decay(plan, w, t, ns), ends))

            def full(s, row, carry):
                gs, rs = carry
                dt, dtu = t["dt"][pl.ds(row, SUB), :], t["dtu"][pl.ds(row, SUB), :]
                gy = t["gy"][pl.ds(row, SUB), :]
                if n0 == 0:
                    sb, wq = zero, zero
                else:
                    sb, wq = t["sb"][pl.ds(row, SUB), :], t["wq"][pl.ds(row, SUB), :]
                new_g, new_r = [], []
                for n, c, r in zip(ns, gs, rs):
                    h_now = t["h"][s + 1, n, pl.ds(g * SUB, SUB), :]
                    h_prev = t["h"][s, n, pl.ds(g * SUB, SUB), :]
                    gh = coefs(plan, t, row, n, 1) * gy + c
                    t["prod"][n, pl.ds(row, SUB), :] = fold(gh * dtu)
                    t["prod"][nst + n, pl.ds(row, SUB), :] = fold(gy * h_now)
                    sb = sb + gh * coefs(plan, t, row, n, 0)
                    c = jnp.exp2(dt * w["rate"][n]) * gh
                    q = c * h_prev
                    wq = wq + q * w["rate"][n]
                    new_g.append(c)
                    new_r.append(r + q * dt)
                t["sb"][pl.ds(row, SUB), :] = sb
                t["wq"][pl.ds(row, SUB), :] = wq
                return tuple(new_g), tuple(new_r)

            _, rs = over_steps(plan, g, full, (start, tuple(zero for _ in ns)), backwards=True)
            for n, r in zip(ns, rs):
                t["gr"][n] = r if plan.groups == 1 else t["gr"][n] + r

        if plan.groups > 1:
            for n in ns:
                t["gr"][n] = zero
        over_groups(plan, group)


def finish(plan, back_ref, w, t):
    nst, rank = plan.states, plan.rank
    u, dt, gy, sb = t["u"][...], t["dt"][...], t["gy"][...], t["sb"][...]
    g_dt = t["wq"][...] * LN2 + sb * u
    gz = g_dt * t["m"][...] * (1.0 / (1.0 + jnp.exp(-t["z"][...])))
    gz_b = gz.astype(BF16)
    dtp_b = w["dtp"][...].astype(BF16)
    gp = gather(plan, t) + dot(gz_b, dtp_b, ((1,), (1,)))
    gp_b = gp.astype(BF16)
    u_b = u.astype(BF16)
    g_x = dot(gp_b, u_b, ((0,), (0,)))
    g_d = dot(t["p"][...].astype(BF16), gz_b, ((0,), (0,)))
    lane = lax.broadcasted_iota(jnp.int32, (SUB, 3 * LANES), 1)
    first = lane < plan.channels
    wide = -(-(rank + 2 * nst) // SUB) * SUB
    blocks = [jnp.where(first, g_x[r : r + SUB, :], g_x[plan.half + r : plan.half + r + SUB, :]) for r in range(0, wide, SUB)]
    row = lax.broadcasted_iota(jnp.int32, (SUB, 3 * LANES), 0)
    small = jnp.where(first, g_d[0:SUB, :], g_d[plan.half : plan.half + SUB, :])
    small = jnp.where(row == SUB - 2, jnp.sum(gz, axis=0, keepdims=True), small)
    blocks.append(jnp.where(row == SUB - 1, jnp.sum(gy * u, axis=0, keepdims=True), small))
    for n0 in range(0, nst, SUB):
        part = jnp.zeros((SUB, 3 * LANES), F32)
        for n in range(n0, n0 + SUB):
            part = jnp.where(row == n - n0, jnp.sum(t["gr"][n], axis=0, keepdims=True), part)
        blocks.append(part * w["small"][2 * SUB + n0 : 3 * SUB + n0, :])
    grads = jnp.concatenate(blocks, axis=0)
    gu = sb * dt + gy * w["small"][SUB : SUB + 1, :] + dot(gp_b, w["x"][...].astype(BF16))
    tiles = [gu[:, k * LANES : (k + 1) * LANES] for k in range(3)]
    return grads, unplace(plan, back_ref, tiles, t["stack"])


def weight_shapes(plan):
    up = -(-(plan.rank + 2 * plan.states) // SUB) * SUB
    return {
        "x": (LANES, 3 * LANES),
        "small": (2 * SUB + plan.states, 3 * LANES),
        "rate": (plan.states, SUB, 3 * LANES),
        "dtp": (LANES, 3 * LANES),
    }, {"pad": (2, max(2 * SUB + plan.states, up), 2 * LANES)}


def token_shapes(plan):
    wide, narrow = (plan.rows, 3 * LANES), (plan.rows, LANES)
    kept = {"u": wide, "m": wide, "z": wide, "dt": wide, "dtu": wide, "p": narrow,
            "bb": (2 * plan.states, plan.rows, 2 * LANES),
            "h": (plan.steps + 1, plan.states, plan.lines, 3 * LANES)}
    own = {"y": wide, "stack": (2 * plan.rows, 2 * LANES), "x256": (plan.rows, 2 * LANES)}
    grads = {"gy": wide, "sb": wide, "wq": wide, "prod": (2 * plan.states, plan.rows, 2 * LANES),
             "gr": (plan.states, SUB, 3 * LANES), "x256": (plan.rows, 2 * LANES), "stack": (2 * plan.rows, 2 * LANES)}
    return kept, own, grads


def token_mask(plan, tissue_ref, shape, axis):
    per = plan.rows // tissue_ref.shape[0]
    token = lax.broadcasted_iota(jnp.int32, shape, axis)
    mask = jnp.zeros(shape, F32)
    for k in range(tissue_ref.shape[0]):
        mask = jnp.where((token >= k * per) & (token < (k + 1) * per), tissue_ref[k].astype(F32), mask)
    return mask


def masked_rows(plan, tissue_ref, feat_ref):
    ch = plan.channels
    mask = token_mask(plan, tissue_ref, (SUB, plan.rows), 1)
    tall = jnp.concatenate([mask] * (ch // SUB), axis=0)
    fill = jnp.concatenate([mask] * ((2 * LANES - ch) // SUB), axis=0)
    return jnp.concatenate([feat_ref[...].astype(F32) * tall, fill], axis=0).astype(BF16)


def partner_rows(count, rows, s):
    return pl.ds(pl.multiple_of((lax.axis_index("band") ^ s) * (rows // count), SUB), rows // count)


def send_blocks(refs, tiles, scratch, width):
    scratch[:, :LANES], scratch[:, LANES:] = tiles
    if len(refs) == 1:
        refs[0][...] = scratch[:, :width].astype(BF16)
        return
    for s, ref in enumerate(refs):
        ref[...] = scratch[partner_rows(len(refs), scratch.shape[0], s), :width].astype(BF16)


def receive_blocks(refs, scratch):
    width = refs[0].shape[1]
    if len(refs) == 1:
        scratch[:, :width] = refs[0][...].astype(F32)
        return
    for s, ref in enumerate(refs):
        scratch[partner_rows(len(refs), scratch.shape[0], s), :width] = ref[...].astype(F32)


def rows_forward_kernel(plan, side, *refs):
    count = 9
    far, (send_refs, w, kept, rest, near, sems) = refs[:count], refs[count:]
    copies = [pltpu.make_async_copy(a, b, sems.at[k]) for k, (a, b) in enumerate(zip(far, near))]
    for copy in copies:
        copy.start()
    for copy in copies:
        copy.wait()
    tissue_ref, feat_ref, perm_ref, back_ref, x_ref, dtp_ref, bias_ref, alog_ref, skip_ref = near
    t = kept | rest
    w = w | rest
    load_weights(plan, side, x_ref, dtp_ref, bias_ref, alog_ref, skip_ref, w)
    prepare(plan, perm_ref, masked_rows(plan, tissue_ref, feat_ref), w, t)
    forward(plan, w, t, True)
    tiles = [t["y"][:, k * LANES : (k + 1) * LANES] for k in range(3)]
    a, b = unplace(plan, back_ref, tiles, t["stack"])
    mask = token_mask(plan, tissue_ref, (plan.rows, LANES), 0)
    send_blocks(send_refs, (a, jnp.where(lane_iota(plan.rows) < plan.half, b, mask)), t["x256"], 2 * LANES)


def rows_backward_kernel(plan, side, tissue_ref, gy_refs, perm_ref, back_ref, w, kept, grads_v_ref,
                         out_ref, mine_ref, theirs_ref, rest):
    t = kept | rest
    receive_blocks(gy_refs, t["x256"])
    place(plan, perm_ref, t["x256"][...].astype(BF16), t["gy"])
    backward(plan, w, t)
    grads, (a, b) = finish(plan, back_ref, w, t)
    mask = token_mask(plan, tissue_ref, (plan.rows, LANES), 0)
    out_ref[:, :LANES] = (a * mask).astype(BF16)
    out_ref[:, LANES:] = (b * mask)[:, : plan.channels - LANES].astype(BF16)
    other = grads_v_ref[...].astype(F32)
    odd = lax.axis_index("slide") % 2 == 1
    mine_ref[...] = jnp.where(odd, other, grads).astype(BF16)
    theirs_ref[...] = jnp.where(odd, grads, other).astype(BF16)


def columns_kernel(plan, side, recv_refs, gy_ref, x_ref, dtp_ref, bias_ref, alog_ref, skip_ref,
                   mixed_ref, out_refs, grads_ref, t):
    ch = plan.channels
    w = t
    load_weights(plan, side, x_ref, dtp_ref, bias_ref, alog_ref, skip_ref, w)
    receive_blocks(recv_refs, t["x256"])
    low = lane_iota(plan.rows) < plan.half
    last = t["x256"][:, LANES:]
    mask = jnp.where(low, swap64(last), last)
    prepare(plan, None, jnp.concatenate([t["x256"][:, :LANES] * mask, last * mask], axis=1), w, t)
    t["x256"][:, 0:ch] = gy_ref[...].astype(F32)
    place(plan, None, t["x256"][...], t["gy"])
    forward(plan, w, t, True)
    tiles = [t["y"][:, k * LANES : (k + 1) * LANES] for k in range(3)]
    a, b = unplace(plan, None, tiles, None)
    mixed_ref[:, :LANES] = a.astype(BF16)
    mixed_ref[:, LANES:] = b[:, : ch - LANES].astype(BF16)
    backward(plan, w, t)
    grads, (a, b) = finish(plan, None, w, t)
    grads_ref[...] = grads.astype(BF16)
    mask = t["m"][:, :LANES]
    send_blocks(out_refs, (a * mask, b * mask), t["x256"], ch)


def unpack_kernel(plan, mine_ref, theirs_ref, gx_ref, gd_ref, gb_ref, ga_ref, gs_ref):
    nst, rank, ch = plan.states, plan.rank, plan.channels
    wide = rank + 2 * nst
    up = -(-wide // SUB) * SUB
    odd = lax.axis_index("slide") % 2 == 1
    mine, theirs = mine_ref[...].astype(F32), theirs_ref[...].astype(F32)
    for side, total in enumerate((jnp.where(odd, theirs, mine), jnp.where(odd, mine, theirs))):
        tiles = [total[:, k * LANES : (k + 1) * LANES] for k in range(3)]
        for d, (a, b) in enumerate(((tiles[0], tiles[1]), (tiles[2], swap64(tiles[1])))):
            k = 2 * side + d
            for lo, hi, part in ((0, LANES, a), (LANES, ch, b[:, : ch - LANES])):
                gx_ref[:, k, lo:hi] = part[0:wide, :]
                gd_ref[:, k, lo:hi] = part[up : up + rank, :]
                gb_ref[k : k + 1, lo:hi] = part[up + SUB - 2 : up + SUB - 1, :]
                gs_ref[k : k + 1, lo:hi] = part[up + SUB - 1 : up + SUB, :]
                ga_ref[k, :, lo:hi] = part[up + SUB : up + SUB + nst, :]


def call(kernel, plan, side, out_shape, args, scratch, name, cost, scalars=0, far=()):
    whole = pl.BlockSpec(memory_space=pltpu.VMEM)
    specs = list(jax.tree.map(lambda _: whole, tuple(args)))
    if scalars:
        specs[0] = pl.BlockSpec(memory_space=pltpu.SMEM)
    scratches = [{k: pltpu.VMEM(v, F32) for k, v in scratch.items()}]
    if far:
        args = [pltpu.with_memory_space_constraint(a, pltpu.HBM) if k in far else a for k, a in enumerate(args)]
        for k in far:
            specs[k] = pl.BlockSpec(memory_space=pltpu.HBM)
        scratches += [[(pltpu.SMEM if args[k].ndim == 1 else pltpu.VMEM)(args[k].shape, args[k].dtype) for k in far], pltpu.SemaphoreType.DMA((len(far),))]
    return pl.pallas_call(
        functools.partial(kernel, plan, side), out_shape=out_shape, in_specs=tuple(specs),
        out_specs=jax.tree.map(lambda _: whole, out_shape), scratch_shapes=scratches,
        name=name, cost_estimate=pl.CostEstimate(flops=cost * 10**6, bytes_accessed=4 * 10**6, transcendentals=0),
        compiler_params=pltpu.CompilerParams(vmem_limit_bytes=VMEM_LIMIT),
    )(*args)


def arrays(shapes):
    return {k: jax.ShapeDtypeStruct(v, F32) for k, v in shapes.items()}


def swap(x, axis, step):
    return lax.ppermute(x, axis, [(i, i ^ step) for i in range(lax.axis_size(axis))])


def exchange(x, axis, step):
    return (x.astype(F32) + swap(x, axis, step).astype(F32)).astype(BF16)


def deliver(blocks, rows):
    bands = lax.axis_size("band")
    if len(blocks) == 1:
        block = blocks[0].reshape(bands, rows // bands, -1)
        return [lax.all_to_all(block, "band", split_axis=0, concat_axis=0, tiled=True).reshape(rows, -1)]
    return [blocks[0]] + [swap(blocks[s], "band", s) for s in range(1, bands)]


def shards(features, tissue, cotangent, x_proj, dt_proj, dt_bias, a_log, d_skip):
    _, _, width, channels = features.shape
    _, height, cols_here, _ = cotangent.shape
    bands = lax.axis_size("band")
    dirs, rank, states = dt_proj.shape[0], dt_proj.shape[1], a_log.shape[1]
    rows_plan = Plan(width // SUB, SUB, True, channels, states, rank)
    cols_plan = Plan(height, cols_here, False, channels, states, rank)
    weights = [jnp.transpose(x_proj, (2, 0, 1)), jnp.transpose(dt_proj, (1, 0, 2)), dt_bias, a_log, d_skip]
    feat = jnp.transpose(features.reshape(width, channels))
    keep = tissue.reshape(-1)
    packed = -(-(rank + 2 * states) // SUB) * SUB + SUB + states
    grads_shape = jax.ShapeDtypeStruct((packed, 3 * LANES), BF16)

    perm, back = rows_plan.perm()
    w_kept, w_own = weight_shapes(rows_plan)
    kept, own, grads = token_shapes(rows_plan)
    count = bands if bands in (2, 4) else 1
    tokens = height * cols_here

    def blocks(rows, lanes):
        return [jax.ShapeDtypeStruct((rows // count, lanes), BF16)] * count

    send, w_rows, t_rows = call(
        rows_forward_kernel, rows_plan, 0, (blocks(width, 2 * LANES), arrays(w_kept), arrays(kept)),
        [keep, feat, perm, back] + weights, own | w_own, "rows_forward", 4000, 0, tuple(range(9)))
    moved = deliver(send, width)
    w_kept, w_own = weight_shapes(cols_plan)
    kept_c, own_c, grads_c = token_shapes(cols_plan)
    mixed, grad_carried, grads_v = call(
        columns_kernel, cols_plan, 1,
        (jax.ShapeDtypeStruct((tokens, channels), BF16), blocks(tokens, channels), grads_shape),
        [moved, cotangent.reshape(tokens, channels)] + weights,
        kept_c | own_c | grads_c | w_kept | w_own, "columns", 8000)
    returned = deliver(grad_carried, tokens)
    grad_features, mine, theirs = call(
        rows_backward_kernel, rows_plan, 0, (jax.ShapeDtypeStruct((width, channels), BF16), grads_shape, grads_shape),
        [keep, returned, perm, back, w_rows, t_rows, grads_v], grads, "rows_backward", 8000, 1)
    mine = (mine.astype(F32) + swap(theirs, "slide", 1).astype(F32)).astype(BF16)
    for axis in ("slide", "band"):
        step = 2 if axis == "slide" else 1
        while step < lax.axis_size(axis):
            mine = exchange(mine, axis, step)
            step *= 2
    theirs = swap(mine, "slide", 1)
    shapes = [(rank + 2 * states, dirs, channels), (rank, dirs, channels), (dirs, channels), (dirs, states, channels), (dirs, channels)]
    gx, gd, gb, ga, gs = pl.pallas_call(
        functools.partial(unpack_kernel, rows_plan), out_shape=[jax.ShapeDtypeStruct(s, F32) for s in shapes], name="unpack",
        compiler_params=pltpu.CompilerParams(vmem_limit_bytes=VMEM_LIMIT),
    )(mine, theirs)
    return (mixed.reshape(cotangent.shape), grad_features.reshape(features.shape), jnp.transpose(gx, (1, 2, 0)),
            jnp.transpose(gd, (1, 0, 2)), gb, ga, gs)


def solution(mesh):
    in_specs = (
        P(("groups", "slide"), "band", None, None),
        P(("groups", "slide"), "band", None),
        P(("groups", "slide"), None, "band", None),
        P(), P(), P(), P(), P(),
    )
    out_specs = (
        P(("groups", "slide"), None, "band", None),
        P(("groups", "slide"), "band", None, None),
        P("groups", None, None),
        P("groups", None, None),
        P("groups", None),
        P("groups", None, None),
        P("groups", None),
    )
    return jax.shard_map(shards, mesh=mesh, in_specs=in_specs, out_specs=out_specs, check_vma=False)
```

```python
import functools

import jax
import jax.numpy as jnp
import numpy as np
from jax import lax
from jax.experimental import pallas as pl
from jax.experimental.pallas import tpu as pltpu
from jax.sharding import PartitionSpec as P

F32 = jnp.float32
BF16 = jnp.bfloat16
LANES = 128
SUB = 8
LOG2E = 1.4426950408889634
LN2 = 0.6931471805599453
VMEM_LIMIT = 8 * 2**20
VMEM_SPARE = 4 * 2**20
PER = 8


def dot(a, b, dims=((1,), (0,))):
    return lax.dot_general(a, b, (dims, ((), ())), preferred_element_type=F32)


def split(x):
    hi = x.astype(BF16)
    return hi, (x - hi.astype(F32)).astype(BF16)


def swap64(x):
    return pltpu.roll(x, LANES // 2, axis=1)


def lane_iota(rows):
    return lax.broadcasted_iota(jnp.int32, (rows, LANES), 1)


def pack_tiles(a0, b0, a1, b1):
    low = lane_iota(a0.shape[0]) < LANES // 2
    return [a0, jnp.where(low, b0, swap64(b1)), a1]


class Plan:
    def __init__(self, steps, lines, chunked, channels, states, rank):
        self.steps, self.lines, self.chunked = steps, lines, chunked
        self.rows = steps * lines
        self.groups = lines // SUB
        self.channels, self.states, self.rank = channels, states, rank
        self.half = LANES // 2
        self.unroll = next(k for k in (8, 4, 2, 1) if steps % k == 0)

    def reverse(self, x):
        return jnp.concatenate([x[s * self.lines : (s + 1) * self.lines] for s in reversed(range(self.steps))], axis=0)

    def perm(self):
        r = np.arange(self.rows)
        s, j = r // self.lines, r % self.lines
        first = j * self.steps + s
        second = self.rows - 1 - first
        hot = np.zeros((self.rows, 2 * self.rows), np.float32)
        hot[r, first] = 1.0
        hot[r, self.rows + second] = 1.0
        back = np.concatenate([hot[:, : self.rows].T, hot[:, self.rows :].T], axis=1)
        return jnp.asarray(hot, BF16), jnp.asarray(back, BF16)


def load_weights(plan, side, x_ref, dtp_ref, bias_ref, alog_ref, skip_ref, w):
    ch, nst = plan.channels, plan.states
    pad, half = w["pad"], plan.half
    pad[:, :, ch:] = jnp.zeros((2, pad.shape[1], 2 * LANES - ch), F32)

    def halves(rows):
        first, second = pad[0, 0:rows, :], pad[1, 0:rows, :]
        return first[:, :LANES], first[:, LANES:], second[:, :LANES], second[:, LANES:]

    def diagonal(ref, dst):
        count = ref.shape[0]
        rows = -(-count // SUB) * SUB
        dst[...] = jnp.zeros_like(dst)
        for d in range(2):
            pad[d, rows - SUB : rows, 0:ch] = jnp.zeros((SUB, ch), F32)
            pad[d, 0:count, 0:ch] = ref[:, 2 * side + d, :]
        a0, b0, a1, b1 = halves(rows)
        dst[0:rows, 0:LANES] = a0
        dst[0:rows, LANES : 2 * LANES] = b0
        dst[half : half + rows, LANES : 2 * LANES] = swap64(b1)
        dst[half : half + rows, 2 * LANES :] = a1

    diagonal(x_ref, w["x"])
    diagonal(dtp_ref, w["dtp"])
    for d in range(2):
        pad[d, 0:1, 0:ch] = bias_ref[2 * side + d : 2 * side + d + 1, :]
        pad[d, SUB : SUB + 1, 0:ch] = skip_ref[2 * side + d : 2 * side + d + 1, :]
        pad[d, 2 * SUB : 2 * SUB + nst, 0:ch] = alog_ref[2 * side + d]
    tiles = pack_tiles(*halves(2 * SUB + nst))
    for k in range(3):
        at = slice(k * LANES, (k + 1) * LANES)
        w["small"][0 : 2 * SUB, at] = tiles[k][0 : 2 * SUB]
        rates = -jnp.exp(tiles[k][2 * SUB :])
        w["small"][2 * SUB :, at] = rates
        for n in range(nst):
            w["rate"][n, :, at] = jnp.broadcast_to(rates[n : n + 1, :] * LOG2E, (SUB, LANES))


def place(plan, perm_ref, x, dst, tall=False):
    if plan.chunked:
        dims = ((1,), (1,)) if tall else ((1,), (0,))
        first = dot(perm_ref[:, : plan.rows], x, dims)
        second = dot(perm_ref[:, plan.rows :], x, dims)
    else:
        first, second = x, plan.reverse(x)
    a0, b0, a1, b1 = first[:, :LANES], first[:, LANES:], second[:, :LANES], second[:, LANES:]
    for k, tile in enumerate(pack_tiles(a0, b0, a1, b1)):
        dst[:, k * LANES : (k + 1) * LANES] = tile
    return b0, b1


def unplace(plan, back_ref, packed, stack):
    t0, t1, t2 = packed
    if not plan.chunked:
        return t0 + plan.reverse(t2), t1 + plan.reverse(swap64(t1))
    stack[0 : plan.rows, 0:LANES] = t0
    stack[0 : plan.rows, LANES:] = t1
    stack[plan.rows :, 0:LANES] = t2
    stack[plan.rows :, LANES:] = swap64(t1)
    hi, lo = split(stack[...])
    out = dot(back_ref[...], hi) + dot(back_ref[...], lo)
    return out[:, :LANES], out[:, LANES:]


def prepare(plan, perm_ref, x256, w, t):
    b0, b1 = place(plan, perm_ref, x256, t["u"], plan.chunked)
    low = lane_iota(plan.rows) < plan.half
    m0 = jnp.where(low, swap64(b0), b0)
    m1 = jnp.where(low, swap64(b1), b1)
    masks = [m0, jnp.where(low, m0, m1), m1]
    for k in range(3):
        t["m"][:, k * LANES : (k + 1) * LANES] = masks[k]
    u = t["u"][...].astype(BF16)
    x_hi, x_lo = split(w["x"][...])
    proj = dot(u, x_hi, ((1,), (1,))) + dot(u, x_lo, ((1,), (1,)))
    t["p"][...] = proj
    p_hi, p_lo = split(proj)
    d_hi, d_lo = split(w["dtp"][...])
    z = dot(p_hi, d_hi) + dot(p_lo, d_hi) + dot(p_hi, d_lo) + w["small"][0:1, :]
    t["z"][...] = z
    soft = jnp.maximum(z, 0.0) + jnp.log1p(jnp.exp(-jnp.abs(z)))
    dt = soft * t["m"][...]
    t["dt"][...] = dt
    t["dtu"][...] = dt * t["u"][...]


def own_lanes(plan, r, width):
    lane = lax.broadcasted_iota(jnp.int32, (plan.rows, width), 1) % plan.half
    return lane == plan.rank + r


def spread(plan, t):
    k = lax.broadcasted_iota(jnp.int32, (2 * LANES, 2 * LANES), 0) % LANES
    l = lax.broadcasted_iota(jnp.int32, (2 * LANES, 2 * LANES), 1)
    ones = jnp.where((k < plan.half) == (l < LANES), 1.0, 0.0).astype(BF16)
    hi = t["p"][...].astype(BF16).astype(F32)
    both = jnp.concatenate([hi, t["p"][...] - hi], axis=1)
    for r in range(2 * plan.states):
        t["bc"][r] = dot(jnp.where(own_lanes(plan, r, 2 * LANES), both, 0.0).astype(BF16), ones)


def fold(x):
    low = lane_iota(SUB) < LANES // 2
    t0, t1, t2 = x[:, :LANES], x[:, LANES : 2 * LANES], x[:, 2 * LANES :]
    return jnp.concatenate([jnp.where(low, t0, t2) + t1, jnp.where(low, t2, t0)], axis=1)


def gather(plan, t):
    k = lax.broadcasted_iota(jnp.int32, (2 * LANES, LANES), 0)
    l = lax.broadcasted_iota(jnp.int32, (2 * LANES, LANES), 1)
    first = (k < plan.half) | (k >= LANES + plan.half)
    ones = jnp.where(first == (l < plan.half), 1.0, 0.0).astype(BF16)
    out = jnp.zeros((plan.rows, LANES), F32)
    for r in range(2 * plan.states):
        out = jnp.where(own_lanes(plan, r, LANES), dot(t["prod"][r].astype(BF16), ones), out)
    return out


def coefs(plan, t, row, n, which):
    lo = t["bc"][which * plan.states + n, pl.ds(row, SUB), 0:LANES]
    hi = t["bc"][which * plan.states + n, pl.ds(row, SUB), LANES:]
    mid = jnp.where(lane_iota(SUB) < plan.half, lo, hi)
    return jnp.concatenate([lo, mid, hi], axis=1)


def over_steps(plan, g, body, carry, backwards=False):
    u = plan.unroll

    def chunk(i, carry):
        for k in range(u):
            s = i * u + k
            if backwards:
                s = plan.steps - 1 - s
            row = s * plan.lines + g * SUB
            if not isinstance(row, int):
                row = pl.multiple_of(row, SUB)
            carry = body(s, row, carry)
        return carry

    if plan.steps == u:
        return chunk(0, carry)
    return lax.fori_loop(0, plan.steps // u, chunk, carry)


def over_groups(plan, body):
    if plan.groups == 1:
        body(0)
    else:
        lax.fori_loop(0, plan.groups, lambda g, c: (body(g), c)[1], 0)


def chunk_scan(decay, end, backwards):
    at = lax.broadcasted_iota(jnp.int32, end.shape, 0)
    for shift in (1, 2, 4):
        if backwards:
            inside, amount = at < SUB - shift, SUB - shift
        else:
            inside, amount = at >= shift, shift
        prev_end, prev_decay = pltpu.roll(end, amount, axis=0), pltpu.roll(decay, amount, axis=0)
        end = jnp.where(inside, decay * prev_end + end, end)
        decay = jnp.where(inside, decay * prev_decay, decay)
    if backwards:
        return jnp.where(at < SUB - 1, pltpu.roll(end, SUB - 1, axis=0), 0.0)
    return jnp.where(at >= 1, pltpu.roll(end, 1, axis=0), 0.0)


def chunk_decay(plan, w, t, n):
    total = functools.reduce(lambda a, b: a + b, [t["dt"][s * SUB : (s + 1) * SUB, :] for s in range(plan.steps)])
    return [jnp.exp2(total * w["rate"][k]) for k in n]


def forward(plan, w, t, keep_states):
    nst = plan.states
    zero = jnp.zeros((SUB, 3 * LANES), F32)
    spread(plan, t)
    for n0 in range(0, nst, PER):
        ns = list(range(n0, n0 + PER))

        def group(g, ns=ns, n0=n0):
            start = tuple(zero for _ in ns)
            if plan.chunked:

                def local(s, row, hs):
                    dt, dtu = t["dt"][pl.ds(row, SUB), :], t["dtu"][pl.ds(row, SUB), :]
                    new = []
                    for n, h in zip(ns, hs):
                        a = jnp.exp2(dt * w["rate"][n])
                        t["a"][s, n] = a
                        new.append(a * h + coefs(plan, t, row, n, 0) * dtu)
                    return tuple(new)

                ends = over_steps(plan, g, local, start)
                start = tuple(chunk_scan(d, e, False) for d, e in zip(chunk_decay(plan, w, t, ns), ends))
            if keep_states:
                for n, h in zip(ns, start):
                    t["h"][0, n, pl.ds(g * SUB, SUB), :] = h

            def full(s, row, hs):
                dt, dtu = t["dt"][pl.ds(row, SUB), :], t["dtu"][pl.ds(row, SUB), :]
                y = t["u"][pl.ds(row, SUB), :] * w["small"][SUB : SUB + 1, :] if n0 == 0 else t["y"][pl.ds(row, SUB), :]
                new = []
                for n, h in zip(ns, hs):
                    a = t["a"][s, n] if plan.chunked else jnp.exp2(dt * w["rate"][n])
                    h = a * h + coefs(plan, t, row, n, 0) * dtu
                    y = y + coefs(plan, t, row, n, 1) * h
                    if keep_states:
                        t["h"][s + 1, n, pl.ds(g * SUB, SUB), :] = h
                    new.append(h)
                t["y"][pl.ds(row, SUB), :] = y
                return tuple(new)

            over_steps(plan, g, full, start)

        over_groups(plan, group)


def backward(plan, w, t):
    nst, per = plan.states, 4
    zero = jnp.zeros((SUB, 3 * LANES), F32)
    for n0 in range(0, nst, per):
        ns = list(range(n0, n0 + per))

        def group(g, ns=ns, n0=n0):
            start = tuple(zero for _ in ns)
            if plan.chunked:

                def local(s, row, gs):
                    gy = t["gy"][pl.ds(row, SUB), :]
                    return tuple(t["a"][s, n] * (coefs(plan, t, row, n, 1) * gy + c) for n, c in zip(ns, gs))

                ends = over_steps(plan, g, local, start, backwards=True)
                start = tuple(chunk_scan(d, e, True) for d, e in zip(chunk_decay(plan, w, t, ns), ends))

            def full(s, row, carry):
                gs, rs = carry
                dt, dtu = t["dt"][pl.ds(row, SUB), :], t["dtu"][pl.ds(row, SUB), :]
                gy = t["gy"][pl.ds(row, SUB), :]
                if n0 == 0:
                    sb, wq = zero, zero
                else:
                    sb, wq = t["sb"][pl.ds(row, SUB), :], t["wq"][pl.ds(row, SUB), :]
                new_g, new_r = [], []
                for n, c, r in zip(ns, gs, rs):
                    h_now = t["h"][s + 1, n, pl.ds(g * SUB, SUB), :]
                    h_prev = t["h"][s, n, pl.ds(g * SUB, SUB), :]
                    gh = coefs(plan, t, row, n, 1) * gy + c
                    t["prod"][n, pl.ds(row, SUB), :] = fold(gh * dtu)
                    t["prod"][nst + n, pl.ds(row, SUB), :] = fold(gy * h_now)
                    sb = sb + gh * coefs(plan, t, row, n, 0)
                    a = t["a"][s, n] if plan.chunked else jnp.exp2(dt * w["rate"][n])
                    c = a * gh
                    q = c * h_prev
                    wq = wq + q * w["rate"][n]
                    new_g.append(c)
                    new_r.append(r + q * dt)
                t["sb"][pl.ds(row, SUB), :] = sb
                t["wq"][pl.ds(row, SUB), :] = wq
                return tuple(new_g), tuple(new_r)

            _, rs = over_steps(plan, g, full, (start, tuple(zero for _ in ns)), backwards=True)
            for n, r in zip(ns, rs):
                t["gr"][n] = r if plan.groups == 1 else t["gr"][n] + r

        if plan.groups > 1:
            for n in ns:
                t["gr"][n] = zero
        over_groups(plan, group)


def finish(plan, back_ref, w, t):
    nst, rank = plan.states, plan.rank
    u, dt, gy, sb = t["u"][...], t["dt"][...], t["gy"][...], t["sb"][...]
    g_dt = t["wq"][...] * LN2 + sb * u
    gz = g_dt * t["m"][...] * (1.0 / (1.0 + jnp.exp(-t["z"][...])))
    gz_b = gz.astype(BF16)
    dtp_b = w["dtp"][...].astype(BF16)
    gp = gather(plan, t) + dot(gz_b, dtp_b, ((1,), (1,)))
    gp_b = gp.astype(BF16)
    u_b = u.astype(BF16)
    g_x = dot(gp_b, u_b, ((0,), (0,)))
    g_d = dot(t["p"][...].astype(BF16), gz_b, ((0,), (0,)))
    lane = lax.broadcasted_iota(jnp.int32, (SUB, 3 * LANES), 1)
    first = lane < plan.channels
    wide = -(-(rank + 2 * nst) // SUB) * SUB
    blocks = [jnp.where(first, g_x[r : r + SUB, :], g_x[plan.half + r : plan.half + r + SUB, :]) for r in range(0, wide, SUB)]
    row = lax.broadcasted_iota(jnp.int32, (SUB, 3 * LANES), 0)
    small = jnp.where(first, g_d[0:SUB, :], g_d[plan.half : plan.half + SUB, :])
    small = jnp.where(row == SUB - 2, jnp.sum(gz, axis=0, keepdims=True), small)
    blocks.append(jnp.where(row == SUB - 1, jnp.sum(gy * u, axis=0, keepdims=True), small))
    for n0 in range(0, nst, SUB):
        part = jnp.zeros((SUB, 3 * LANES), F32)
        for n in range(n0, n0 + SUB):
            part = jnp.where(row == n - n0, jnp.sum(t["gr"][n], axis=0, keepdims=True), part)
        blocks.append(part * w["small"][2 * SUB + n0 : 3 * SUB + n0, :])
    grads = jnp.concatenate(blocks, axis=0)
    gu = sb * dt + gy * w["small"][SUB : SUB + 1, :] + dot(gp_b, w["x"][...].astype(BF16))
    tiles = [gu[:, k * LANES : (k + 1) * LANES] for k in range(3)]
    return grads, unplace(plan, back_ref, tiles, t.get("stack"))


def weight_shapes(plan):
    up = -(-(plan.rank + 2 * plan.states) // SUB) * SUB
    return {
        "x": (LANES, 3 * LANES),
        "small": (2 * SUB + plan.states, 3 * LANES),
        "rate": (plan.states, SUB, 3 * LANES),
        "dtp": (LANES, 3 * LANES),
    }, {"pad": (2, max(2 * SUB + plan.states, up), 2 * LANES)}


def token_shapes(plan):
    wide, narrow, double = (plan.rows, 3 * LANES), (plan.rows, LANES), (plan.rows, 2 * LANES)
    kept = {"u": wide, "m": wide, "z": wide, "dt": wide, "dtu": wide, "p": narrow,
            "bc": (2 * plan.states,) + double,
            "h": (plan.steps + 1, plan.states, plan.lines, 3 * LANES)}
    if plan.chunked:
        kept["a"] = (plan.steps, plan.states, plan.lines, 3 * LANES)
    own = {"y": wide, "x256": double}
    grads = {"gy": wide, "sb": wide, "wq": wide, "prod": (2 * plan.states,) + double,
             "gr": (plan.states, SUB, 3 * LANES), "x256": double}
    if plan.chunked:
        own["stack"] = grads["stack"] = (2 * plan.rows, 2 * LANES)
    return kept, own, grads


def token_mask(plan, tissue_ref, shape, axis):
    per = plan.rows // tissue_ref.shape[0]
    token = lax.broadcasted_iota(jnp.int32, shape, axis)
    mask = jnp.zeros(shape, F32)
    for k in range(tissue_ref.shape[0]):
        mask = jnp.where((token >= k * per) & (token < (k + 1) * per), tissue_ref[k].astype(F32), mask)
    return mask


def masked_rows(plan, tissue_ref, feat_ref):
    ch = plan.channels
    mask = token_mask(plan, tissue_ref, (SUB, plan.rows), 1)
    tall = jnp.concatenate([mask] * (ch // SUB), axis=0)
    fill = jnp.concatenate([mask] * ((2 * LANES - ch) // SUB), axis=0)
    return jnp.concatenate([feat_ref[...].astype(F32) * tall, fill], axis=0).astype(BF16)


def partner_rows(count, rows, s):
    return pl.ds(pl.multiple_of((lax.axis_index("band") ^ s) * (rows // count), SUB), rows // count)


def send_blocks(refs, tiles, scratch, width):
    scratch[:, :LANES], scratch[:, LANES:] = tiles
    if len(refs) == 1:
        refs[0][...] = scratch[:, :width].astype(BF16)
        return
    for s, ref in enumerate(refs):
        ref[...] = scratch[partner_rows(len(refs), scratch.shape[0], s), :width].astype(BF16)


def receive_blocks(refs, scratch):
    width = refs[0].shape[1]
    if len(refs) == 1:
        scratch[:, :width] = refs[0][...].astype(F32)
        return
    for s, ref in enumerate(refs):
        scratch[partner_rows(len(refs), scratch.shape[0], s), :width] = ref[...].astype(F32)


def rows_forward_kernel(plan, side, *refs):
    count = 9
    far, (send_refs, w, kept, rest, near, sems) = refs[:count], refs[count:]
    copies = [pltpu.make_async_copy(a, b, sems.at[k]) for k, (a, b) in enumerate(zip(far, near))]
    for copy in copies:
        copy.start()
    for copy in copies:
        copy.wait()
    tissue_ref, feat_ref, perm_ref, back_ref, x_ref, dtp_ref, bias_ref, alog_ref, skip_ref = near
    t = kept | rest
    w = w | rest
    load_weights(plan, side, x_ref, dtp_ref, bias_ref, alog_ref, skip_ref, w)
    prepare(plan, perm_ref, masked_rows(plan, tissue_ref, feat_ref), w, t)
    forward(plan, w, t, True)
    tiles = [t["y"][:, k * LANES : (k + 1) * LANES] for k in range(3)]
    a, b = unplace(plan, back_ref, tiles, t.get("stack"))
    mask = token_mask(plan, tissue_ref, (plan.rows, LANES), 0)
    send_blocks(send_refs, (a, jnp.where(lane_iota(plan.rows) < plan.half, b, mask)), t["x256"], 2 * LANES)


def rows_backward_kernel(plan, side, tissue_ref, gy_refs, perm_ref, back_ref, w, kept, grads_v_ref,
                         out_ref, mine_ref, theirs_ref, rest):
    t = kept | rest
    receive_blocks(gy_refs, t["x256"])
    place(plan, perm_ref, t["x256"][...].astype(BF16), t["gy"])
    backward(plan, w, t)
    grads, (a, b) = finish(plan, back_ref, w, t)
    mask = token_mask(plan, tissue_ref, (plan.rows, LANES), 0)
    out_ref[:, :LANES] = (a * mask).astype(BF16)
    out_ref[:, LANES:] = (b * mask)[:, : plan.channels - LANES].astype(BF16)
    other = grads_v_ref[...].astype(F32)
    odd = lax.axis_index("slide") % 2 == 1
    mine_ref[...] = jnp.where(odd, other, grads).astype(BF16)
    theirs_ref[...] = jnp.where(odd, grads, other).astype(BF16)


def columns_kernel(plan, side, recv_refs, gy_ref, x_ref, dtp_ref, bias_ref, alog_ref, skip_ref,
                   mixed_ref, out_refs, grads_ref, t):
    ch = plan.channels
    w = t
    load_weights(plan, side, x_ref, dtp_ref, bias_ref, alog_ref, skip_ref, w)
    receive_blocks(recv_refs, t["x256"])
    low = lane_iota(plan.rows) < plan.half
    last = t["x256"][:, LANES:]
    mask = jnp.where(low, swap64(last), last)
    prepare(plan, None, jnp.concatenate([t["x256"][:, :LANES] * mask, last * mask], axis=1), w, t)
    t["x256"][:, 0:ch] = gy_ref[...].astype(F32)
    place(plan, None, t["x256"][...], t["gy"])
    forward(plan, w, t, True)
    tiles = [t["y"][:, k * LANES : (k + 1) * LANES] for k in range(3)]
    a, b = unplace(plan, None, tiles, None)
    mixed_ref[:, :LANES] = a.astype(BF16)
    mixed_ref[:, LANES:] = b[:, : ch - LANES].astype(BF16)
    backward(plan, w, t)
    grads, (a, b) = finish(plan, None, w, t)
    grads_ref[...] = grads.astype(BF16)
    mask = t["m"][:, :LANES]
    send_blocks(out_refs, (a * mask, b * mask), t["x256"], ch)


def unpack_kernel(plan, mine_ref, theirs_ref, gx_ref, gd_ref, gb_ref, ga_ref, gs_ref):
    nst, rank, ch = plan.states, plan.rank, plan.channels
    wide = rank + 2 * nst
    up = -(-wide // SUB) * SUB
    odd = lax.axis_index("slide") % 2 == 1
    mine, theirs = mine_ref[...].astype(F32), theirs_ref[...].astype(F32)
    for side, total in enumerate((jnp.where(odd, theirs, mine), jnp.where(odd, mine, theirs))):
        tiles = [total[:, k * LANES : (k + 1) * LANES] for k in range(3)]
        for d, (a, b) in enumerate(((tiles[0], tiles[1]), (tiles[2], swap64(tiles[1])))):
            k = 2 * side + d
            for lo, hi, part in ((0, LANES, a), (LANES, ch, b[:, : ch - LANES])):
                gx_ref[:, k, lo:hi] = part[0:wide, :]
                gd_ref[:, k, lo:hi] = part[up : up + rank, :]
                gb_ref[k : k + 1, lo:hi] = part[up + SUB - 2 : up + SUB - 1, :]
                gs_ref[k : k + 1, lo:hi] = part[up + SUB - 1 : up + SUB, :]
                ga_ref[k, :, lo:hi] = part[up + SUB : up + SUB + nst, :]


def call(kernel, plan, side, out_shape, args, scratch, name, cost, scalars=0, far=()):
    whole = pl.BlockSpec(memory_space=pltpu.VMEM)
    specs = list(jax.tree.map(lambda _: whole, tuple(args)))
    if scalars:
        specs[0] = pl.BlockSpec(memory_space=pltpu.SMEM)
    scratches = [arrays(scratch, pltpu.VMEM)]
    limit = VMEM_SPARE + sum(int(np.prod(x.shape)) * x.dtype.itemsize for x in jax.tree.leaves(arrays(scratch)))
    if far:
        args = [pltpu.with_memory_space_constraint(a, pltpu.HBM) if k in far else a for k, a in enumerate(args)]
        for k in far:
            specs[k] = pl.BlockSpec(memory_space=pltpu.HBM)
        scratches += [[(pltpu.SMEM if args[k].ndim == 1 else pltpu.VMEM)(args[k].shape, args[k].dtype) for k in far], pltpu.SemaphoreType.DMA((len(far),))]
    return pl.pallas_call(
        functools.partial(kernel, plan, side), out_shape=out_shape, in_specs=tuple(specs),
        out_specs=jax.tree.map(lambda _: whole, out_shape), scratch_shapes=scratches,
        name=name, cost_estimate=pl.CostEstimate(flops=cost * 10**6, bytes_accessed=4 * 10**6, transcendentals=0),
        compiler_params=pltpu.CompilerParams(vmem_limit_bytes=limit),
    )(*args)


def arrays(shapes, make=jax.ShapeDtypeStruct):
    def one(shape):
        return make(shape, F32) if isinstance(shape[-1], int) else make(shape[:-1], shape[-1])

    return jax.tree.map(one, shapes, is_leaf=lambda x: isinstance(x, tuple))


def swap(x, axis, step):
    return lax.ppermute(x, axis, [(i, i ^ step) for i in range(lax.axis_size(axis))])


def exchange(x, axis, step):
    return (x.astype(F32) + swap(x, axis, step).astype(F32)).astype(BF16)


def deliver(blocks, rows):
    bands = lax.axis_size("band")
    if len(blocks) == 1:
        block = blocks[0].reshape(bands, rows // bands, -1)
        return [lax.all_to_all(block, "band", split_axis=0, concat_axis=0, tiled=True).reshape(rows, -1)]
    got = {s: swap(blocks[s], "band", s) for s in reversed(range(1, bands))}
    return [blocks[0]] + [got[s] for s in range(1, bands)]


def shards(features, tissue, cotangent, x_proj, dt_proj, dt_bias, a_log, d_skip):
    _, _, width, channels = features.shape
    _, height, cols_here, _ = cotangent.shape
    bands = lax.axis_size("band")
    dirs, rank, states = dt_proj.shape[0], dt_proj.shape[1], a_log.shape[1]
    rows_plan = Plan(width // SUB, SUB, True, channels, states, rank)
    cols_plan = Plan(height, cols_here, False, channels, states, rank)
    weights = [jnp.transpose(x_proj, (2, 0, 1)), jnp.transpose(dt_proj, (1, 0, 2)), dt_bias, a_log, d_skip]
    feat = jnp.transpose(features.reshape(width, channels))
    keep = tissue.reshape(-1)
    packed = -(-(rank + 2 * states) // SUB) * SUB + SUB + states
    grads_shape = jax.ShapeDtypeStruct((packed, 3 * LANES), BF16)

    perm, back = rows_plan.perm()
    w_kept, w_own = weight_shapes(rows_plan)
    kept, own, grads = token_shapes(rows_plan)
    count = bands if bands in (2, 4) else 1
    tokens = height * cols_here

    def blocks(rows, lanes):
        return [jax.ShapeDtypeStruct((rows // count, lanes), BF16)] * count

    send, w_rows, t_rows = call(
        rows_forward_kernel, rows_plan, 0, (blocks(width, 2 * LANES), arrays(w_kept), arrays(kept)),
        [keep, feat, perm, back] + weights, own | w_own, "rows_forward", 4000, 0, tuple(range(9)))
    moved = deliver(send, width)
    w_kept, w_own = weight_shapes(cols_plan)
    kept_c, own_c, grads_c = token_shapes(cols_plan)
    mixed, grad_carried, grads_v = call(
        columns_kernel, cols_plan, 1,
        (jax.ShapeDtypeStruct((tokens, channels), BF16), blocks(tokens, channels), grads_shape),
        [moved, cotangent.reshape(tokens, channels)] + weights,
        kept_c | own_c | grads_c | w_kept | w_own, "columns", 8000)
    returned = deliver(grad_carried, tokens)
    grad_features, mine, theirs = call(
        rows_backward_kernel, rows_plan, 0, (jax.ShapeDtypeStruct((width, channels), BF16), grads_shape, grads_shape),
        [keep, returned, perm, back, w_rows, t_rows, grads_v], grads, "rows_backward", 8000, 1)
    mine = (mine.astype(F32) + swap(theirs, "slide", 1).astype(F32)).astype(BF16)
    for axis in ("slide", "band"):
        step = 2 if axis == "slide" else 1
        if axis == "band" and lax.axis_size(axis) == 4:
            far = [swap(mine, axis, s).astype(F32) for s in (3, 2, 1)]
            mine = ((mine.astype(F32) + far[2]) + (far[1] + far[0])).astype(BF16)
            continue
        while step < lax.axis_size(axis):
            mine = exchange(mine, axis, step)
            step *= 2
    theirs = swap(mine, "slide", 1)
    shapes = [(rank + 2 * states, dirs, channels), (rank, dirs, channels), (dirs, channels), (dirs, states, channels), (dirs, channels)]
    gx, gd, gb, ga, gs = pl.pallas_call(
        functools.partial(unpack_kernel, rows_plan), out_shape=[jax.ShapeDtypeStruct(s, F32) for s in shapes], name="unpack",
        compiler_params=pltpu.CompilerParams(vmem_limit_bytes=VMEM_LIMIT),
    )(mine, theirs)
    return (mixed.reshape(cotangent.shape), grad_features.reshape(features.shape), jnp.transpose(gx, (1, 2, 0)),
            jnp.transpose(gd, (1, 0, 2)), gb, ga, gs)


def solution(mesh):
    in_specs = (
        P(("groups", "slide"), "band", None, None),
        P(("groups", "slide"), "band", None),
        P(("groups", "slide"), None, "band", None),
        P(), P(), P(), P(), P(),
    )
    out_specs = (
        P(("groups", "slide"), None, "band", None),
        P(("groups", "slide"), "band", None, None),
        P("groups", None, None),
        P("groups", None, None),
        P("groups", None),
        P("groups", None, None),
        P("groups", None),
    )
    return jax.shard_map(shards, mesh=mesh, in_specs=in_specs, out_specs=out_specs, check_vma=False)
```

```python
import functools

import jax
import jax.numpy as jnp
import numpy as np
from jax import lax
from jax.experimental import pallas as pl
from jax.experimental.pallas import tpu as pltpu
from jax.sharding import PartitionSpec as P

F32 = jnp.float32
BF16 = jnp.bfloat16
LANES = 128
SUB = 8
LOG2E = 1.4426950408889634
LN2 = 0.6931471805599453
VMEM_LIMIT = 8 * 2**20
VMEM_SPARE = 4 * 2**20
PER = 8
HOPS = 2


def dot(a, b, dims=((1,), (0,))):
    return lax.dot_general(a, b, (dims, ((), ())), preferred_element_type=F32)


def split(x):
    hi = x.astype(BF16)
    return hi, (x - hi.astype(F32)).astype(BF16)


def lane_tile(k):
    return slice(k * LANES, (k + 1) * LANES)


def swap64(x):
    return pltpu.roll(x, LANES // 2, axis=1)


def lane_iota(rows):
    return lax.broadcasted_iota(jnp.int32, (rows, LANES), 1)


def pack_tiles(a0, b0, a1, b1):
    low = lane_iota(a0.shape[0]) < LANES // 2
    return [a0, jnp.where(low, b0, swap64(b1)), a1]


class Plan:
    def __init__(self, steps, lines, chunked, channels, states, rank):
        self.steps, self.lines, self.chunked = steps, lines, chunked
        self.rows = steps * lines
        self.groups = lines // SUB
        self.channels, self.states, self.rank = channels, states, rank
        self.half = LANES // 2
        self.unroll = next(k for k in (8, 4, 2, 1) if steps % k == 0)

    def reverse(self, x):
        return jnp.concatenate([x[s * self.lines : (s + 1) * self.lines] for s in reversed(range(self.steps))], axis=0)

    def perm(self):
        r = np.arange(self.rows)
        s, j = r // self.lines, r % self.lines
        first = j * self.steps + s
        second = self.rows - 1 - first
        hot = np.zeros((self.rows, 2 * self.rows), np.float32)
        hot[r, first] = 1.0
        hot[r, self.rows + second] = 1.0
        back = np.concatenate([hot[:, : self.rows].T, hot[:, self.rows :].T], axis=1)
        return jnp.asarray(hot, BF16), jnp.asarray(back, BF16)


def load_weights(plan, side, x_ref, dtp_ref, bias_ref, alog_ref, skip_ref, w):
    ch, nst = plan.channels, plan.states
    pad, half = w["pad"], plan.half
    pad[:, :, ch:] = jnp.zeros((2, pad.shape[1], 2 * LANES - ch), F32)

    def halves(rows):
        first, second = pad[0, 0:rows, :], pad[1, 0:rows, :]
        return first[:, :LANES], first[:, LANES:], second[:, :LANES], second[:, LANES:]

    def diagonal(ref, dst):
        count = ref.shape[0]
        rows = -(-count // SUB) * SUB
        dst[...] = jnp.zeros_like(dst)
        for d in range(2):
            pad[d, rows - SUB : rows, 0:ch] = jnp.zeros((SUB, ch), F32)
            pad[d, 0:count, 0:ch] = ref[:, 2 * side + d, :]
        a0, b0, a1, b1 = halves(rows)
        dst[0:rows, 0:LANES] = a0
        dst[0:rows, LANES : 2 * LANES] = b0
        dst[half : half + rows, LANES : 2 * LANES] = swap64(b1)
        dst[half : half + rows, 2 * LANES :] = a1

    diagonal(x_ref, w["x"])
    diagonal(dtp_ref, w["dtp"])
    for d in range(2):
        pad[d, 0:1, 0:ch] = bias_ref[2 * side + d : 2 * side + d + 1, :]
        pad[d, SUB : SUB + 1, 0:ch] = skip_ref[2 * side + d : 2 * side + d + 1, :]
        pad[d, 2 * SUB : 2 * SUB + nst, 0:ch] = alog_ref[2 * side + d]
    tiles = pack_tiles(*halves(2 * SUB + nst))
    for k in range(3):
        at = slice(k * LANES, (k + 1) * LANES)
        w["small"][0 : 2 * SUB, at] = tiles[k][0 : 2 * SUB]
        rates = -jnp.exp(tiles[k][2 * SUB :])
        w["small"][2 * SUB :, at] = rates
        for n in range(nst):
            w["rate"][n, :, at] = jnp.broadcast_to(rates[n : n + 1, :] * LOG2E, (SUB, LANES))


def place(plan, perm_ref, x, dst, tall=False):
    if plan.chunked:
        dims = ((1,), (1,)) if tall else ((1,), (0,))
        first = dot(perm_ref[:, : plan.rows], x, dims)
        second = dot(perm_ref[:, plan.rows :], x, dims)
    else:
        first, second = x, plan.reverse(x)
    a0, b0, a1, b1 = first[:, :LANES], first[:, LANES:], second[:, :LANES], second[:, LANES:]
    for k, tile in enumerate(pack_tiles(a0, b0, a1, b1)):
        dst[:, k * LANES : (k + 1) * LANES] = tile
    return b0, b1


def unplace(plan, back_ref, packed, stack):
    t0, t1, t2 = packed
    if not plan.chunked:
        return t0 + plan.reverse(t2), t1 + plan.reverse(swap64(t1))
    stack[0 : plan.rows, 0:LANES] = t0
    stack[0 : plan.rows, LANES:] = t1
    stack[plan.rows :, 0:LANES] = t2
    stack[plan.rows :, LANES:] = swap64(t1)
    hi, lo = split(stack[...])
    out = dot(back_ref[...], hi) + dot(back_ref[...], lo)
    return out[:, :LANES], out[:, LANES:]


def prepare(plan, perm_ref, x256, w, t):
    b0, b1 = place(plan, perm_ref, x256, t["u"], plan.chunked)
    low = lane_iota(plan.rows) < plan.half
    m0 = jnp.where(low, swap64(b0), b0)
    m1 = jnp.where(low, swap64(b1), b1)
    masks = [m0, jnp.where(low, m0, m1), m1]
    for k in range(3):
        t["m"][:, k * LANES : (k + 1) * LANES] = masks[k]
    u = t["u"][...].astype(BF16)
    x_hi, x_lo = split(w["x"][...])
    proj = dot(u, x_hi, ((1,), (1,))) + dot(u, x_lo, ((1,), (1,)))
    t["p"][...] = proj
    p_hi, p_lo = split(proj)
    d_hi, d_lo = split(w["dtp"][...])
    z = dot(p_hi, d_hi) + dot(p_lo, d_hi) + dot(p_hi, d_lo) + w["small"][0:1, :]
    t["z"][...] = z
    soft = jnp.maximum(z, 0.0) + jnp.log1p(jnp.exp(-jnp.abs(z)))
    dt = soft * t["m"][...]
    t["dt"][...] = dt
    t["dtu"][...] = dt * t["u"][...]


def own_lanes(plan, r, width):
    lane = lax.broadcasted_iota(jnp.int32, (plan.rows, width), 1) % plan.half
    return lane == plan.rank + r


def spread(plan, t):
    k = lax.broadcasted_iota(jnp.int32, (2 * LANES, 2 * LANES), 0) % LANES
    l = lax.broadcasted_iota(jnp.int32, (2 * LANES, 2 * LANES), 1)
    ones = jnp.where((k < plan.half) == (l < LANES), 1.0, 0.0).astype(BF16)
    hi = t["p"][...].astype(BF16).astype(F32)
    both = jnp.concatenate([hi, t["p"][...] - hi], axis=1)
    for r in range(2 * plan.states):
        t["bc"][r] = dot(jnp.where(own_lanes(plan, r, 2 * LANES), both, 0.0).astype(BF16), ones)


def fold(x):
    low = lane_iota(SUB) < LANES // 2
    t0, t1, t2 = x[:, :LANES], x[:, LANES : 2 * LANES], x[:, 2 * LANES :]
    return jnp.concatenate([jnp.where(low, t0, t2) + t1, jnp.where(low, t2, t0)], axis=1)


def gather(plan, t):
    k = lax.broadcasted_iota(jnp.int32, (2 * LANES, LANES), 0)
    l = lax.broadcasted_iota(jnp.int32, (2 * LANES, LANES), 1)
    first = (k < plan.half) | (k >= LANES + plan.half)
    ones = jnp.where(first == (l < plan.half), 1.0, 0.0).astype(BF16)
    out = jnp.zeros((plan.rows, LANES), F32)
    for r in range(2 * plan.states):
        out = jnp.where(own_lanes(plan, r, LANES), dot(t["prod"][r].astype(BF16), ones), out)
    return out


def coefs(plan, t, row, n, which):
    lo = t["bc"][which * plan.states + n, pl.ds(row, SUB), 0:LANES]
    hi = t["bc"][which * plan.states + n, pl.ds(row, SUB), LANES:]
    mid = jnp.where(lane_iota(SUB) < plan.half, lo, hi)
    return jnp.concatenate([lo, mid, hi], axis=1)


def over_steps(plan, g, body, carry, backwards=False):
    u = plan.unroll

    def chunk(i, carry):
        for k in range(u):
            s = i * u + k
            if backwards:
                s = plan.steps - 1 - s
            row = s * plan.lines + g * SUB
            if not isinstance(row, int):
                row = pl.multiple_of(row, SUB)
            carry = body(s, row, carry)
        return carry

    if plan.steps == u:
        return chunk(0, carry)
    return lax.fori_loop(0, plan.steps // u, chunk, carry)


def over_groups(plan, body):
    if plan.groups == 1:
        body(0)
    else:
        lax.fori_loop(0, plan.groups, lambda g, c: (body(g), c)[1], 0)


def chunk_scan(decay, end, backwards):
    at = lax.broadcasted_iota(jnp.int32, end.shape, 0)
    for shift in (1, 2, 4):
        if backwards:
            inside, amount = at < SUB - shift, SUB - shift
        else:
            inside, amount = at >= shift, shift
        prev_end, prev_decay = pltpu.roll(end, amount, axis=0), pltpu.roll(decay, amount, axis=0)
        end = jnp.where(inside, decay * prev_end + end, end)
        decay = jnp.where(inside, decay * prev_decay, decay)
    if backwards:
        return jnp.where(at < SUB - 1, pltpu.roll(end, SUB - 1, axis=0), 0.0)
    return jnp.where(at >= 1, pltpu.roll(end, 1, axis=0), 0.0)


def chunk_decay(plan, w, t, n):
    total = functools.reduce(lambda a, b: a + b, [t["dt"][s * SUB : (s + 1) * SUB, :] for s in range(plan.steps)])
    return [jnp.exp2(total * w["rate"][k]) for k in n]


def forward(plan, w, t, keep_states):
    nst = plan.states
    zero = jnp.zeros((SUB, 3 * LANES), F32)
    spread(plan, t)
    for n0 in range(0, nst, PER):
        ns = list(range(n0, n0 + PER))

        def group(g, ns=ns, n0=n0):
            start = tuple(zero for _ in ns)
            if plan.chunked:

                def local(s, row, hs):
                    dt, dtu = t["dt"][pl.ds(row, SUB), :], t["dtu"][pl.ds(row, SUB), :]
                    new = []
                    for n, h in zip(ns, hs):
                        a = jnp.exp2(dt * w["rate"][n])
                        t["a"][s, n] = a
                        new.append(a * h + coefs(plan, t, row, n, 0) * dtu)
                    return tuple(new)

                ends = over_steps(plan, g, local, start)
                start = tuple(chunk_scan(d, e, False) for d, e in zip(chunk_decay(plan, w, t, ns), ends))
            if keep_states:
                for n, h in zip(ns, start):
                    t["h"][0, n, pl.ds(g * SUB, SUB), :] = h

            def full(s, row, hs):
                dt, dtu = t["dt"][pl.ds(row, SUB), :], t["dtu"][pl.ds(row, SUB), :]
                y = t["u"][pl.ds(row, SUB), :] * w["small"][SUB : SUB + 1, :] if n0 == 0 else t["y"][pl.ds(row, SUB), :]
                new = []
                for n, h in zip(ns, hs):
                    a = t["a"][s, n] if plan.chunked else jnp.exp2(dt * w["rate"][n])
                    h = a * h + coefs(plan, t, row, n, 0) * dtu
                    y = y + coefs(plan, t, row, n, 1) * h
                    if keep_states:
                        t["h"][s + 1, n, pl.ds(g * SUB, SUB), :] = h
                    new.append(h)
                t["y"][pl.ds(row, SUB), :] = y
                return tuple(new)

            over_steps(plan, g, full, start)

        over_groups(plan, group)


def backward(plan, w, t):
    nst, per = plan.states, 4
    zero = jnp.zeros((SUB, 3 * LANES), F32)
    for n0 in range(0, nst, per):
        ns = list(range(n0, n0 + per))

        def group(g, ns=ns, n0=n0):
            start = tuple(zero for _ in ns)
            if plan.chunked:

                def local(s, row, gs):
                    gy = t["gy"][pl.ds(row, SUB), :]
                    return tuple(t["a"][s, n] * (coefs(plan, t, row, n, 1) * gy + c) for n, c in zip(ns, gs))

                ends = over_steps(plan, g, local, start, backwards=True)
                start = tuple(chunk_scan(d, e, True) for d, e in zip(chunk_decay(plan, w, t, ns), ends))

            def full(s, row, carry):
                gs, rs = carry
                dt, dtu = t["dt"][pl.ds(row, SUB), :], t["dtu"][pl.ds(row, SUB), :]
                gy = t["gy"][pl.ds(row, SUB), :]
                if n0 == 0:
                    sb, wq = zero, zero
                else:
                    sb, wq = t["sb"][pl.ds(row, SUB), :], t["wq"][pl.ds(row, SUB), :]
                new_g, new_r = [], []
                for n, c, r in zip(ns, gs, rs):
                    h_now = t["h"][s + 1, n, pl.ds(g * SUB, SUB), :]
                    h_prev = t["h"][s, n, pl.ds(g * SUB, SUB), :]
                    gh = coefs(plan, t, row, n, 1) * gy + c
                    t["prod"][n, pl.ds(row, SUB), :] = fold(gh * dtu)
                    t["prod"][nst + n, pl.ds(row, SUB), :] = fold(gy * h_now)
                    sb = sb + gh * coefs(plan, t, row, n, 0)
                    a = t["a"][s, n] if plan.chunked else jnp.exp2(dt * w["rate"][n])
                    c = a * gh
                    q = c * h_prev
                    wq = wq + q * w["rate"][n]
                    new_g.append(c)
                    new_r.append(r + q * dt)
                t["sb"][pl.ds(row, SUB), :] = sb
                t["wq"][pl.ds(row, SUB), :] = wq
                return tuple(new_g), tuple(new_r)

            _, rs = over_steps(plan, g, full, (start, tuple(zero for _ in ns)), backwards=True)
            for n, r in zip(ns, rs):
                t["gr"][n] = r if plan.groups == 1 else t["gr"][n] + r

        if plan.groups > 1:
            for n in ns:
                t["gr"][n] = zero
        over_groups(plan, group)


def finish(plan, w, t):
    nst, rank = plan.states, plan.rank
    u, dt, gy, sb = t["u"][...], t["dt"][...], t["gy"][...], t["sb"][...]
    g_dt = t["wq"][...] * LN2 + sb * u
    gz = g_dt * t["m"][...] * (1.0 / (1.0 + jnp.exp(-t["z"][...])))
    gz_b = gz.astype(BF16)
    dtp_b = w["dtp"][...].astype(BF16)
    gp = gather(plan, t) + dot(gz_b, dtp_b, ((1,), (1,)))
    gp_b = gp.astype(BF16)
    u_b = u.astype(BF16)
    g_x = dot(gp_b, u_b, ((0,), (0,)))
    g_d = dot(t["p"][...].astype(BF16), gz_b, ((0,), (0,)))
    lane = lax.broadcasted_iota(jnp.int32, (SUB, 3 * LANES), 1)
    first = lane < plan.channels
    wide = -(-(rank + 2 * nst) // SUB) * SUB
    blocks = [jnp.where(first, g_x[r : r + SUB, :], g_x[plan.half + r : plan.half + r + SUB, :]) for r in range(0, wide, SUB)]
    row = lax.broadcasted_iota(jnp.int32, (SUB, 3 * LANES), 0)
    small = jnp.where(first, g_d[0:SUB, :], g_d[plan.half : plan.half + SUB, :])
    small = jnp.where(row == SUB - 2, jnp.sum(gz, axis=0, keepdims=True), small)
    blocks.append(jnp.where(row == SUB - 1, jnp.sum(gy * u, axis=0, keepdims=True), small))
    for n0 in range(0, nst, SUB):
        part = jnp.zeros((SUB, 3 * LANES), F32)
        for n in range(n0, n0 + SUB):
            part = jnp.where(row == n - n0, jnp.sum(t["gr"][n], axis=0, keepdims=True), part)
        blocks.append(part * w["small"][2 * SUB + n0 : 3 * SUB + n0, :])
    grads = jnp.concatenate(blocks, axis=0)
    return grads, gp_b


def input_gradient(plan, back_ref, w, t, gp_b, stack):
    gu = t["sb"][...] * t["dt"][...] + t["gy"][...] * w["small"][SUB : SUB + 1, :] + dot(gp_b, w["x"][...].astype(BF16))
    return unplace(plan, back_ref, [gu[:, lane_tile(k)] for k in range(3)], stack)


def weight_shapes(plan):
    up = -(-(plan.rank + 2 * plan.states) // SUB) * SUB
    return {
        "x": (LANES, 3 * LANES),
        "small": (2 * SUB + plan.states, 3 * LANES),
        "rate": (plan.states, SUB, 3 * LANES),
        "dtp": (LANES, 3 * LANES),
    }, {"pad": (2, max(2 * SUB + plan.states, up), 2 * LANES)}


def token_shapes(plan):
    wide, narrow, double = (plan.rows, 3 * LANES), (plan.rows, LANES), (plan.rows, 2 * LANES)
    kept = {"u": wide, "m": wide, "z": wide, "dt": wide, "dtu": wide, "p": narrow,
            "bc": (2 * plan.states,) + double,
            "h": (plan.steps + 1, plan.states, plan.lines, 3 * LANES)}
    if plan.chunked:
        kept["a"] = (plan.steps, plan.states, plan.lines, 3 * LANES)
    own = {"y": wide, "x256": double}
    grads = {"gy": wide, "sb": wide, "wq": wide, "prod": (2 * plan.states,) + double,
             "gr": (plan.states, SUB, 3 * LANES), "x256": double}
    if plan.chunked:
        own["stack"] = (2 * plan.rows, 2 * LANES)
    return kept, own, grads


def token_mask(plan, tissue_ref, shape, axis):
    per = plan.rows // tissue_ref.shape[0]
    token = lax.broadcasted_iota(jnp.int32, shape, axis)
    mask = jnp.zeros(shape, F32)
    for k in range(tissue_ref.shape[0]):
        mask = jnp.where((token >= k * per) & (token < (k + 1) * per), tissue_ref[k].astype(F32), mask)
    return mask


def masked_rows(plan, tissue_ref, feat_ref):
    ch = plan.channels
    mask = token_mask(plan, tissue_ref, (SUB, plan.rows), 1)
    tall = jnp.concatenate([mask] * (ch // SUB), axis=0)
    fill = jnp.concatenate([mask] * ((2 * LANES - ch) // SUB), axis=0)
    return jnp.concatenate([feat_ref[...].astype(F32) * tall, fill], axis=0).astype(BF16)


def partner_rows(count, rows, s):
    return pl.ds(pl.multiple_of((lax.axis_index("band") ^ s) * (rows // count), SUB), rows // count)


def send_blocks(refs, tiles, scratch, width):
    scratch[:, :LANES], scratch[:, LANES:] = tiles
    send_from(refs, scratch, width)


def send_from(refs, scratch, width):
    if len(refs) == 1:
        refs[0][...] = scratch[:, :width].astype(BF16)
        return
    for s, ref in enumerate(refs):
        ref[...] = scratch[partner_rows(len(refs), scratch.shape[0], s), :width].astype(BF16)


def receive_blocks(refs, scratch):
    width = refs[0].shape[1]
    if len(refs) == 1:
        scratch[:, :width] = refs[0][...].astype(F32)
        return
    for s, ref in enumerate(refs):
        scratch[partner_rows(len(refs), scratch.shape[0], s), :width] = ref[...].astype(F32)


def rows_forward_kernel(plan, side, *refs):
    count = 9
    far, (send_refs, w, kept, rest, near, sems) = refs[:count], refs[count:]
    copies = [pltpu.make_async_copy(a, b, sems.at[k]) for k, (a, b) in enumerate(zip(far, near))]
    for copy in copies:
        copy.start()
    for copy in copies:
        copy.wait()
    tissue_ref, feat_ref, perm_ref, back_ref, x_ref, dtp_ref, bias_ref, alog_ref, skip_ref = near
    t = kept | rest
    w = w | rest
    load_weights(plan, side, x_ref, dtp_ref, bias_ref, alog_ref, skip_ref, w)
    prepare(plan, perm_ref, masked_rows(plan, tissue_ref, feat_ref), w, t)
    forward(plan, w, t, True)
    tiles = [t["y"][:, k * LANES : (k + 1) * LANES] for k in range(3)]
    a, b = unplace(plan, back_ref, tiles, t.get("stack"))
    mask = token_mask(plan, tissue_ref, (plan.rows, LANES), 0)
    send_blocks(send_refs, (a, jnp.where(lane_iota(plan.rows) < plan.half, b, mask)), t["x256"], 2 * LANES)


def rows_backward_kernel(plan, side, gy_refs, perm_ref, w, kept, grads_v_ref, mine_ref, theirs_ref, late, rest):
    t = kept | rest | late
    receive_blocks(gy_refs, t["x256"])
    place(plan, perm_ref, t["x256"][...].astype(BF16), t["gy"])
    backward(plan, w, t)
    grads, gp_b = finish(plan, w, t)
    late["gp"][...] = gp_b
    other = grads_v_ref[...].astype(F32)
    odd = lax.axis_index("slide") % 2 == 1
    mine_ref[...] = jnp.where(odd, other, grads).astype(BF16)
    theirs_ref[...] = jnp.where(odd, grads, other).astype(BF16)


def rows_output_kernel(plan, side, tissue_ref, back_ref, w, kept, late, out_ref, own):
    a, b = input_gradient(plan, back_ref, w, kept | late, late["gp"][...], own["stack"])
    own["x256"][:, :LANES], own["x256"][:, LANES:] = a, b
    mask = token_mask(plan, tissue_ref, (SUB, plan.rows), 1)
    turned = jnp.transpose(own["x256"][...])[: plan.channels]
    out_ref[...] = (turned * jnp.concatenate([mask] * (plan.channels // SUB), axis=0)).astype(BF16)


def columns_kernel(plan, side, recv_refs, gy_ref, x_ref, dtp_ref, bias_ref, alog_ref, skip_ref,
                   mixed_ref, out_refs, grads_ref, t):
    ch = plan.channels
    w = t
    load_weights(plan, side, x_ref, dtp_ref, bias_ref, alog_ref, skip_ref, w)
    receive_blocks(recv_refs, t["x256"])
    low = lane_iota(plan.rows) < plan.half
    last = t["x256"][:, LANES:]
    mask = jnp.where(low, swap64(last), last)
    prepare(plan, None, jnp.concatenate([t["x256"][:, :LANES] * mask, last * mask], axis=1), w, t)
    t["x256"][:, 0:ch] = gy_ref[...].astype(F32)
    place(plan, None, t["x256"][...], t["gy"])
    forward(plan, w, t, True)
    tiles = [t["y"][:, k * LANES : (k + 1) * LANES] for k in range(3)]
    a, b = unplace(plan, None, tiles, None)
    mixed_ref[:, :LANES] = a.astype(BF16)
    mixed_ref[:, LANES:] = b[:, : ch - LANES].astype(BF16)
    backward(plan, w, t)
    grads, gp_b = finish(plan, w, t)
    grads_ref[...] = grads.astype(BF16)
    a, b = input_gradient(plan, None, w, t, gp_b, None)
    mask = t["m"][:, :LANES]
    send_blocks(out_refs, (a * mask, b * mask), t["x256"], ch)


def tall_shapes(plan):
    steps, ch, nst = plan.steps, plan.channels, plan.states
    up = -(-(plan.rank + 2 * nst) // SUB) * SUB
    field = (steps, ch, LANES)
    ready = {"xs": (2 * up, ch), "ds": (2 * SUB, ch), "al": (2 * (nst + SUB), ch), "rb": (nst + 1, ch, LANES), "gy": field}
    kept = {"u": field, "bc": (steps, 2 * nst, SUB, LANES), "h": (steps, nst, ch, LANES)}
    rest = {
        "z": field, "dt": field, "dtu": field, "sb": field, "wq": field,
        "m": (steps, SUB, LANES), "p": (steps, up, LANES), "acc": (steps, 2 * nst, SUB, LANES),
        "a": (steps, nst, ch, LANES), "gr": (nst, ch, LANES),
        "x256": (plan.rows, 2 * LANES), "pad": (2, up + SUB + nst, 2 * LANES),
    }
    return ready, kept, rest


def tall_hot(plan):
    part = plan.states + SUB
    hot = np.zeros((6 * part, (plan.states + 1) * LANES), np.float32)
    for k in range(6 * part):
        d, n = k % (2 * part) // part, k % part
        if n <= plan.states:
            at = n * LANES + d * plan.half
            hot[k, at : at + plan.half] = 1.0
    return jnp.asarray(hot, BF16)


def by_step(plan, tiles):
    low = lane_iota(tiles[0].shape[0]) < plan.half
    out = []
    for s in range(plan.steps):
        mine, other = tiles[s // 2], tiles[(plan.steps - 1 - s) // 2]
        out.append(jnp.where(low, mine, other) if s % 2 == 0 else swap64(jnp.where(low, other, mine)))
    return out


def by_row(plan, fields):
    low = lane_iota(fields[0].shape[0]) < plan.half
    sums = []
    for s in range(0, plan.steps, 2):
        other = plan.steps - 1 - s
        even = fields[s] + swap64(fields[other])
        odd = swap64(fields[s + 1]) + fields[other - 1]
        sums.append(jnp.where(low, even, odd))
    return jnp.transpose(jnp.concatenate(sums, axis=1))


def tall_setup_kernel(plan, side, after_ref, gy_ref, hot_ref, x_ref, dtp_ref, bias_ref, alog_ref, skip_ref, t, own):
    ch, nst, rank = plan.channels, plan.states, plan.rank
    wide = rank + 2 * nst
    up = t["xs"].shape[0] // 2
    part = nst + SUB
    t["xs"][...] = jnp.zeros_like(t["xs"])
    t["ds"][...] = jnp.zeros_like(t["ds"])
    t["al"][...] = jnp.zeros_like(t["al"])
    for d in range(2):
        k = 2 * side + d
        t["xs"][d * up : d * up + wide, :] = x_ref[:, k, :]
        t["ds"][d * SUB : d * SUB + rank, :] = dtp_ref[:, k, :]
        t["ds"][d * SUB + rank : d * SUB + rank + 1, :] = bias_ref[k : k + 1, :]
        t["al"][d * part : d * part + nst, :] = -jnp.exp(alog_ref[k])
        t["al"][d * part + nst : d * part + nst + 1, :] = skip_ref[k : k + 1, :]
    scale = jnp.where(lax.broadcasted_iota(jnp.int32, (2 * part, ch), 0) % part < nst, LOG2E, 1.0)
    rest = t["al"][...] * scale
    parts = []
    for _ in range(3):
        parts.append(rest.astype(BF16))
        rest = rest - parts[-1].astype(F32)
    spread_rates = dot(jnp.concatenate(parts, axis=0), hot_ref[...], ((0,), (0,)))
    for n in range(nst + 1):
        t["rb"][n] = spread_rates[:, lane_tile(n)]
    own["x256"][:, 0:ch] = gy_ref[...].astype(F32)
    turned = jnp.transpose(own["x256"][...])
    for s, field in enumerate(by_step(plan, [turned[:ch, lane_tile(k)] for k in range(plan.steps // 2)])):
        t["gy"][s] = field


def tall_output_kernel(plan, side, kept, gain, mixed_ref, own):
    steps, ch, nst = plan.steps, plan.channels, plan.states

    def channels(c, carry):
        at = pl.ds(pl.multiple_of(c * SUB, SUB), SUB)
        for s in range(steps):
            terms = [gain[nst, at, :] * kept["u"][s, at, :]]
            terms += [kept["bc"][s, nst + n] * kept["h"][s, n, at, :] for n in range(nst)]
            while len(terms) > 1:
                terms = [a + b for a, b in zip(terms[::2], terms[1::2])] + terms[len(terms) // 2 * 2 :]
            own["y"][s, at, :] = terms[0]
        return carry

    lax.fori_loop(0, ch // SUB, channels, 0)
    mixed_ref[...] = by_row(plan, [own["y"][s] for s in range(steps)]).astype(BF16)


def tall_columns_kernel(plan, side, recv_refs, ready, out_refs, grads_ref, kept, rest):
    steps, ch, nst, rank = plan.steps, plan.channels, plan.states, plan.rank
    t = ready | kept | rest
    up = t["p"].shape[1]
    part = nst + SUB
    rows0 = ((0,), (0,))
    lanes1 = ((1,), (1,))
    lanes = lane_tile
    x_hi, x_lo = split(t["xs"][...])
    d_hi, d_lo = split(t["ds"][...])

    low8 = lane_iota(SUB) < plan.half
    row8 = lax.broadcasted_iota(jnp.int32, (SUB, LANES), 0)
    receive_blocks(recv_refs, t["x256"])
    turned = jnp.transpose(t["x256"][...])
    for s, field in enumerate(by_step(plan, [turned[: ch + SUB, lanes(k)] for k in range(steps // 2)])):
        t["m"][s] = field[ch:]
        t["u"][s] = field[:ch] * jnp.concatenate([field[ch:]] * (ch // SUB), axis=0)
    u_b = jnp.concatenate([t["u"][s].astype(BF16) for s in range(steps)], axis=1)
    proj = dot(x_hi, u_b) + dot(x_lo, u_b)
    low_up = lane_iota(up) < plan.half
    ranks = []
    for s in range(steps):
        p = jnp.where(low_up, proj[:up, lanes(s)], proj[up:, lanes(s)])
        t["p"][s] = p
        one = jnp.where(row8 < rank, p[:SUB], jnp.where(row8 == rank, 1.0, 0.0))
        ranks.append(jnp.concatenate([jnp.where(low8, one, 0.0), jnp.where(low8, 0.0, one)], axis=0))
        for r in range(2 * nst):
            t["bc"][s, r] = jnp.broadcast_to(p[rank + r : rank + r + 1, :], (SUB, LANES))
    r_hi, r_lo = split(jnp.concatenate(ranks, axis=1))
    z = dot(d_hi, r_hi, rows0) + dot(d_lo, r_hi, rows0) + dot(d_hi, r_lo, rows0)
    for s in range(steps):
        z_s = z[:, lanes(s)]
        t["z"][s] = z_s
        soft = jnp.maximum(z_s, 0.0) + jnp.log1p(jnp.exp(-jnp.abs(z_s)))
        dt = soft * jnp.concatenate([t["m"][s]] * (ch // SUB), axis=0)
        t["dt"][s] = dt
        t["dtu"][s] = dt * t["u"][s]

    each = 2 if ch % (2 * SUB) == 0 else 1

    def channels_at(c):
        return [pl.ds(pl.multiple_of((c * each + k) * SUB, SUB), SUB) for k in range(each)]

    def scan_forward(c, carry):
        ats = channels_at(c)
        dts = [[t["dt"][s, at, :] for s in range(steps)] for at in ats]
        dtus = [[t["dtu"][s, at, :] for s in range(steps)] for at in ats]
        for n in range(nst):
            hs = [None] * each
            for s in range(steps):
                b = t["bc"][s, n]
                for k, at in enumerate(ats):
                    h = b * dtus[k][s]
                    if s:
                        a = jnp.exp2(dts[k][s] * t["rb"][n, at, :])
                        t["a"][s, n, at, :] = a
                        h = a * hs[k] + h
                    t["h"][s, n, at, :] = h
                    hs[k] = h
        return carry

    lax.fori_loop(0, ch // (each * SUB), scan_forward, 0)
    t["acc"][...] = jnp.zeros_like(t["acc"])

    def scan_backward(c, carry):
        ats = channels_at(c)
        zero = jnp.zeros((SUB, LANES), F32)
        sbs, wqs = [[zero] * steps for _ in ats], [[zero] * steps for _ in ats]
        for n in range(nst):
            after, g_rates = [None] * each, [None] * each
            for s in reversed(range(steps)):
                b, c_now = t["bc"][s, n], t["bc"][s, nst + n]
                to_b, to_c = t["acc"][s, n], t["acc"][s, nst + n]
                for k, at in enumerate(ats):
                    gy = t["gy"][s, at, :]
                    gh = c_now * gy
                    if after[k] is not None:
                        gh = gh + after[k]
                    to_b = to_b + gh * t["dtu"][s, at, :]
                    to_c = to_c + gy * t["h"][s, n, at, :]
                    sbs[k][s] = sbs[k][s] + gh * b
                    if s:
                        after[k] = t["a"][s, n, at, :] * gh
                        q = after[k] * t["h"][s - 1, n, at, :]
                        wqs[k][s] = wqs[k][s] + q * t["rb"][n, at, :]
                        more = q * t["dt"][s, at, :]
                        g_rates[k] = more if g_rates[k] is None else g_rates[k] + more
                t["acc"][s, n], t["acc"][s, nst + n] = to_b, to_c
            for k, at in enumerate(ats):
                t["gr"][n, at, :] = g_rates[k]
        for k, at in enumerate(ats):
            for s in range(steps):
                t["sb"][s, at, :] = sbs[k][s]
                t["wq"][s, at, :] = wqs[k][s]
        return carry

    lax.fori_loop(0, ch // (each * SUB), scan_backward, 0)

    gzs, gyus = [], []
    for s in range(steps):
        mask = jnp.concatenate([t["m"][s]] * (ch // SUB), axis=0)
        g_dt = t["wq"][s] * LN2 + t["sb"][s] * t["u"][s]
        gzs.append((g_dt * mask * (1.0 / (1.0 + jnp.exp(-t["z"][s])))).astype(BF16))
        gyus.append((t["gy"][s] * t["u"][s]).astype(BF16))
    gz_b, gyu_b = jnp.concatenate(gzs, axis=1), jnp.concatenate(gyus, axis=1)
    g_rank = dot(d_hi, gz_b)
    row_up = lax.broadcasted_iota(jnp.int32, (SUB, LANES), 0)
    g_ps = []
    for s in range(steps):
        tiles = [jnp.where(low8, g_rank[:SUB, lanes(s)], g_rank[SUB:, lanes(s)])]
        tiles += [jnp.zeros((SUB, LANES), F32)] * (up // SUB - 1)
        tiles[0] = jnp.where(row_up < rank, tiles[0], 0.0)
        for r in range(2 * nst):
            k, j = divmod(rank + r, SUB)
            tiles[k] = jnp.where(row_up == j, jnp.sum(t["acc"][s, r], axis=0, keepdims=True), tiles[k])
        g_p = jnp.concatenate(tiles, axis=0)
        g_ps.append(jnp.concatenate([jnp.where(low_up, g_p, 0.0), jnp.where(low_up, 0.0, g_p)], axis=0))
    gp_b = jnp.concatenate(g_ps, axis=1).astype(BF16)
    through = dot(x_hi, gp_b, rows0)
    gus = []
    for s in range(steps):
        mask = jnp.concatenate([t["m"][s]] * (ch // SUB), axis=0)
        gus.append((t["sb"][s] * t["dt"][s] + t["rb"][nst] * t["gy"][s] + through[:, lanes(s)]) * mask)
    t["x256"][:, 0:ch] = by_row(plan, gus)
    send_from(out_refs, t["x256"], ch)
    g_x = dot(gp_b, u_b, lanes1)
    g_d = dot(r_hi, gz_b, lanes1)
    halves = jnp.where(row8 == 0, jnp.where(low8, 1.0, 0.0), jnp.where(row8 == 1, jnp.where(low8, 0.0, 1.0), 0.0)).astype(BF16)
    g_skip = dot(jnp.concatenate([halves] * steps, axis=1), gyu_b, lanes1)
    pad = t["pad"]
    row_d = lax.broadcasted_iota(jnp.int32, (SUB, ch), 0)
    for d in range(2):
        pad[d, 0:up, 0:ch] = g_x[d * up : (d + 1) * up]
        pad[d, up : up + SUB, 0:ch] = jnp.where(row_d == SUB - 1, g_skip[d : d + 1], g_d[d * SUB : (d + 1) * SUB])
    for n0 in range(0, nst, SUB):
        both = [jnp.zeros((SUB, ch), F32)] * 2
        for n in range(n0, n0 + SUB):
            sums = dot(halves, t["gr"][n].astype(BF16), lanes1)
            both = [jnp.where(row_d == n - n0, sums[d : d + 1], both[d]) for d in range(2)]
        for d in range(2):
            pad[d, up + SUB + n0 : up + 2 * SUB + n0, 0:ch] = both[d] * t["al"][d * part + n0 : d * part + n0 + SUB, :]
    first, second = pad[0], pad[1]
    tiles = pack_tiles(first[:, :LANES], first[:, LANES:], second[:, :LANES], second[:, LANES:])
    for k in range(3):
        grads_ref[:, lanes(k)] = tiles[k].astype(BF16)


def unpack_kernel(plan, mine_ref, theirs_ref, gx_ref, gd_ref, gb_ref, ga_ref, gs_ref):
    nst, rank, ch = plan.states, plan.rank, plan.channels
    wide = rank + 2 * nst
    up = -(-wide // SUB) * SUB
    odd = lax.axis_index("slide") % 2 == 1
    mine, theirs = mine_ref[...].astype(F32), theirs_ref[...].astype(F32)
    for side, total in enumerate((jnp.where(odd, theirs, mine), jnp.where(odd, mine, theirs))):
        tiles = [total[:, k * LANES : (k + 1) * LANES] for k in range(3)]
        for d, (a, b) in enumerate(((tiles[0], tiles[1]), (tiles[2], swap64(tiles[1])))):
            k = 2 * side + d
            for lo, hi, part in ((0, LANES, a), (LANES, ch, b[:, : ch - LANES])):
                gx_ref[:, k, lo:hi] = part[0:wide, :]
                gd_ref[:, k, lo:hi] = part[up : up + rank, :]
                gb_ref[k : k + 1, lo:hi] = part[up + SUB - 2 : up + SUB - 1, :]
                gs_ref[k : k + 1, lo:hi] = part[up + SUB - 1 : up + SUB, :]
                ga_ref[k, :, lo:hi] = part[up + SUB : up + SUB + nst, :]


def call(kernel, plan, side, out_shape, args, scratch, name, cost, scalars=0, far=()):
    whole = pl.BlockSpec(memory_space=pltpu.VMEM)
    specs = list(jax.tree.map(lambda _: whole, tuple(args)))
    if scalars:
        specs[0] = pl.BlockSpec(memory_space=pltpu.SMEM)
    scratches = [arrays(scratch, pltpu.VMEM)]
    limit = VMEM_SPARE + sum(int(np.prod(x.shape)) * x.dtype.itemsize for x in jax.tree.leaves(arrays(scratch)))
    if far:
        args = [pltpu.with_memory_space_constraint(a, pltpu.HBM) if k in far else a for k, a in enumerate(args)]
        for k in far:
            specs[k] = pl.BlockSpec(memory_space=pltpu.HBM)
        scratches += [[(pltpu.SMEM if args[k].ndim == 1 else pltpu.VMEM)(args[k].shape, args[k].dtype) for k in far], pltpu.SemaphoreType.DMA((len(far),))]
    return pl.pallas_call(
        functools.partial(kernel, plan, side), out_shape=out_shape, in_specs=tuple(specs),
        out_specs=jax.tree.map(lambda _: whole, out_shape), scratch_shapes=scratches,
        name=name, cost_estimate=pl.CostEstimate(flops=cost * 10**6, bytes_accessed=4 * 10**6, transcendentals=0),
        compiler_params=pltpu.CompilerParams(vmem_limit_bytes=limit),
    )(*args)


def arrays(shapes, make=jax.ShapeDtypeStruct):
    def one(shape):
        return make(shape, F32) if isinstance(shape[-1], int) else make(shape[:-1], shape[-1])

    return jax.tree.map(one, shapes, is_leaf=lambda x: isinstance(x, tuple))


def swap(x, axis, step):
    return lax.ppermute(x, axis, [(i, i ^ step) for i in range(lax.axis_size(axis))])


def cross(x, mask):
    axes = ("slide", "band")
    return lax.ppermute(x, axes, [(i, i ^ mask) for i in range(lax.axis_size(axes))])


def deliver(blocks, rows):
    bands = lax.axis_size("band")
    if len(blocks) == 1:
        block = blocks[0].reshape(bands, rows // bands, -1)
        return [lax.all_to_all(block, "band", split_axis=0, concat_axis=0, tiled=True).reshape(rows, -1)]
    got = {s: swap(blocks[s], "band", s) for s in reversed(range(1, bands))}
    return [blocks[0]] + [got[s] for s in range(1, bands)]


def shards(features, tissue, cotangent, x_proj, dt_proj, dt_bias, a_log, d_skip):
    _, _, width, channels = features.shape
    _, height, cols_here, _ = cotangent.shape
    bands = lax.axis_size("band")
    dirs, rank, states = dt_proj.shape[0], dt_proj.shape[1], a_log.shape[1]
    rows_plan = Plan(width // SUB, SUB, True, channels, states, rank)
    cols_plan = Plan(height, cols_here, False, channels, states, rank)
    weights = [jnp.transpose(x_proj, (2, 0, 1)), jnp.transpose(dt_proj, (1, 0, 2)), dt_bias, a_log, d_skip]
    feat = jnp.transpose(features.reshape(width, channels))
    keep = tissue.reshape(-1)
    packed = -(-(rank + 2 * states) // SUB) * SUB + SUB + states
    grads_shape = jax.ShapeDtypeStruct((packed, 3 * LANES), BF16)

    perm, back = rows_plan.perm()
    w_kept, w_own = weight_shapes(rows_plan)
    kept, own, grads = token_shapes(rows_plan)
    count = bands if bands in (2, 4) else 1
    tokens = height * cols_here

    def blocks(rows, lanes):
        return [jax.ShapeDtypeStruct((rows // count, lanes), BF16)] * count

    send, w_rows, t_rows = call(
        rows_forward_kernel, rows_plan, 0, (blocks(width, 2 * LANES), arrays(w_kept), arrays(kept)),
        [keep, feat, perm, back] + weights, own | w_own, "rows_forward", 4000, 0, tuple(range(9)))
    moved = deliver(send, width)
    cols_out = (jax.ShapeDtypeStruct((tokens, channels), BF16), blocks(tokens, channels), grads_shape)
    cols_in = [moved, cotangent.reshape(tokens, channels)]
    if 2 * cols_here == LANES and height % 2 == 0 and rank < SUB - 1:
        ready, kept_c, own_c = tall_shapes(cols_plan)
        ready = call(tall_setup_kernel, cols_plan, 1, arrays(ready),
                     [w_rows["small"], cols_in[1], tall_hot(cols_plan)] + weights, {"x256": own_c["x256"]}, "columns_setup", 1000)
        grad_carried, grads_v, kept_c = call(
            tall_columns_kernel, cols_plan, 1, (*cols_out[1:], arrays(kept_c)), [moved, ready], own_c, "columns", 8000)
        mixed = call(tall_output_kernel, cols_plan, 1, cols_out[0], [kept_c, ready["rb"]], {"y": own_c["z"]}, "columns_output", 1000)
    else:
        w_kept, w_own = weight_shapes(cols_plan)
        kept_c, own_c, grads_c = token_shapes(cols_plan)
        mixed, grad_carried, grads_v = call(
            columns_kernel, cols_plan, 1, cols_out, cols_in + weights,
            kept_c | own_c | grads_c | w_kept | w_own, "columns", 8000)
    returned = deliver(grad_carried, tokens)
    late = {k: grads.pop(k) for k in ("sb", "gy")} | {"gp": (width, LANES, BF16)}
    mine, theirs, late = call(
        rows_backward_kernel, rows_plan, 0, (grads_shape, grads_shape, arrays(late)),
        [returned, perm, w_rows, t_rows, grads_v], grads, "rows_backward", 8000)
    needed = {k: t_rows[k] for k in ("dt",)}
    grad_features = call(
        rows_output_kernel, rows_plan, 0, jax.ShapeDtypeStruct((channels, width), BF16),
        [keep, back, {k: w_rows[k] for k in ("small", "x")}, needed, late], {k: own[k] for k in ("stack", "x256")}, "rows_output", 1000, 1)
    mine = (mine.astype(F32) + swap(theirs, "slide", 1).astype(F32)).astype(BF16)
    hops = [bands << k for k in range(1, (lax.axis_size("slide") - 1).bit_length())]
    hops += [1 << k for k in range((bands - 1).bit_length())]
    late = [mixed, grad_features]
    while hops:
        first, hops = hops[:HOPS], hops[HOPS:]
        masks = [0]
        for hop in first:
            masks += [mask ^ hop for mask in masks]
        got = {mask: cross(mine, mask) for mask in reversed(masks[1:])}
        if late:
            hidden = late.pop(0)
            got, hidden = lax.optimization_barrier((got, hidden))
            if late:
                mixed = hidden
            else:
                grad_features = hidden
        terms = [mine.astype(F32)] + [got[mask].astype(F32) for mask in masks[1:]]
        while len(terms) > 1:
            terms = [a + b for a, b in zip(terms[::2], terms[1::2])]
        mine = terms[0].astype(BF16)
    theirs = swap(mine, "slide", 1)
    shapes = [(rank + 2 * states, dirs, channels), (rank, dirs, channels), (dirs, channels), (dirs, states, channels), (dirs, channels)]
    gx, gd, gb, ga, gs = pl.pallas_call(
        functools.partial(unpack_kernel, rows_plan), out_shape=[jax.ShapeDtypeStruct(s, F32) for s in shapes], name="unpack",
        compiler_params=pltpu.CompilerParams(vmem_limit_bytes=VMEM_LIMIT),
    )(mine, theirs)
    return (mixed.reshape(cotangent.shape), jnp.transpose(grad_features).reshape(features.shape), jnp.transpose(gx, (1, 2, 0)),
            jnp.transpose(gd, (1, 0, 2)), gb, ga, gs)


def solution(mesh):
    in_specs = (
        P(("groups", "slide"), "band", None, None),
        P(("groups", "slide"), "band", None),
        P(("groups", "slide"), None, "band", None),
        P(), P(), P(), P(), P(),
    )
    out_specs = (
        P(("groups", "slide"), None, "band", None),
        P(("groups", "slide"), "band", None, None),
        P("groups", None, None),
        P("groups", None, None),
        P("groups", None),
        P("groups", None, None),
        P("groups", None),
    )
    return jax.shard_map(shards, mesh=mesh, in_specs=in_specs, out_specs=out_specs, check_vma=False)
```

```python
import functools

import jax
import jax.numpy as jnp
import numpy as np
from jax import lax
from jax.experimental import pallas as pl
from jax.experimental.pallas import tpu as pltpu
from jax.sharding import PartitionSpec as P

F32 = jnp.float32
BF16 = jnp.bfloat16
LANES = 128
SUB = 8
LOG2E = 1.4426950408889634
LN2 = 0.6931471805599453
VMEM_LIMIT = 8 * 2**20
VMEM_SPARE = 2 * 2**20
PER = 8
SPREAD_EVERY = 4
GATHER_EVERY = 3
HOPS = 2


def dot(a, b, dims=((1,), (0,))):
    return lax.dot_general(a, b, (dims, ((), ())), preferred_element_type=F32)


def split(x):
    hi = x.astype(BF16)
    return hi, (x - hi.astype(F32)).astype(BF16)


def lane_tile(k):
    return slice(k * LANES, (k + 1) * LANES)


def swap64(x):
    return pltpu.roll(x, LANES // 2, axis=1)


def lane_iota(rows):
    return lax.broadcasted_iota(jnp.int32, (rows, LANES), 1)


def pack_tiles(a0, b0, a1, b1):
    low = lane_iota(a0.shape[0]) < LANES // 2
    return [a0, jnp.where(low, b0, swap64(b1)), a1]


class Plan:
    def __init__(self, steps, lines, chunked, channels, states, rank):
        self.steps, self.lines, self.chunked = steps, lines, chunked
        self.rows = steps * lines
        self.groups = lines // SUB
        self.channels, self.states, self.rank = channels, states, rank
        self.half = LANES // 2
        self.unroll = next(k for k in (8, 4, 2, 1) if steps % k == 0)

    def reverse(self, x):
        return jnp.concatenate([x[s * self.lines : (s + 1) * self.lines] for s in reversed(range(self.steps))], axis=0)

    def perm(self):
        r = np.arange(self.rows)
        s, j = r // self.lines, r % self.lines
        first = j * self.steps + s
        second = self.rows - 1 - first
        hot = np.zeros((self.rows, 2 * self.rows), np.float32)
        hot[r, first] = 1.0
        hot[r, self.rows + second] = 1.0
        back = np.concatenate([hot[:, : self.rows].T, hot[:, self.rows :].T], axis=1)
        return jnp.asarray(hot, BF16), jnp.asarray(back, BF16)


def load_weights(plan, side, x_ref, dtp_ref, bias_ref, alog_ref, skip_ref, w):
    ch, nst = plan.channels, plan.states
    pad, half = w["pad"], plan.half
    pad[:, :, ch:] = jnp.zeros((2, pad.shape[1], 2 * LANES - ch), F32)

    def halves(rows):
        first, second = pad[0, 0:rows, :], pad[1, 0:rows, :]
        return first[:, :LANES], first[:, LANES:], second[:, :LANES], second[:, LANES:]

    def diagonal(ref, dst):
        count = ref.shape[0]
        rows = -(-count // SUB) * SUB
        dst[...] = jnp.zeros_like(dst)
        for d in range(2):
            pad[d, rows - SUB : rows, 0:ch] = jnp.zeros((SUB, ch), F32)
            pad[d, 0:count, 0:ch] = ref[:, 2 * side + d, :]
        a0, b0, a1, b1 = halves(rows)
        dst[0:rows, 0:LANES] = a0
        dst[0:rows, LANES : 2 * LANES] = b0
        dst[half : half + rows, LANES : 2 * LANES] = swap64(b1)
        dst[half : half + rows, 2 * LANES :] = a1

    diagonal(x_ref, w["x"])
    diagonal(dtp_ref, w["dtp"])
    for d in range(2):
        pad[d, 0:1, 0:ch] = bias_ref[2 * side + d : 2 * side + d + 1, :]
        pad[d, SUB : SUB + 1, 0:ch] = skip_ref[2 * side + d : 2 * side + d + 1, :]
        pad[d, 2 * SUB : 2 * SUB + nst, 0:ch] = alog_ref[2 * side + d]
    tiles = pack_tiles(*halves(2 * SUB + nst))
    for k in range(3):
        at = slice(k * LANES, (k + 1) * LANES)
        w["small"][0 : 2 * SUB, at] = tiles[k][0 : 2 * SUB]
        rates = -jnp.exp(tiles[k][2 * SUB :])
        w["small"][2 * SUB :, at] = rates
        for n in range(nst):
            w["rate"][n, :, at] = jnp.broadcast_to(rates[n : n + 1, :] * LOG2E, (SUB, LANES))


def place(plan, perm_ref, x, dst, tall=False):
    if plan.chunked:
        dims = ((1,), (1,)) if tall else ((1,), (0,))
        first = dot(perm_ref[:, : plan.rows], x, dims)
        second = dot(perm_ref[:, plan.rows :], x, dims)
    else:
        first, second = x, plan.reverse(x)
    a0, b0, a1, b1 = first[:, :LANES], first[:, LANES:], second[:, :LANES], second[:, LANES:]
    for k, tile in enumerate(pack_tiles(a0, b0, a1, b1)):
        dst[:, k * LANES : (k + 1) * LANES] = tile
    return b0, b1


def unplace(plan, back_ref, packed, stack):
    t0, t1, t2 = packed
    if not plan.chunked:
        return t0 + plan.reverse(t2), t1 + plan.reverse(swap64(t1))
    stack[0 : plan.rows, 0:LANES] = t0
    stack[0 : plan.rows, LANES:] = t1
    stack[plan.rows :, 0:LANES] = t2
    stack[plan.rows :, LANES:] = swap64(t1)
    hi, lo = split(stack[...])
    out = dot(back_ref[...], hi) + dot(back_ref[...], lo)
    return out[:, :LANES], out[:, LANES:]


def prepare(plan, placed, w, t):
    b0, b1 = placed
    low = lane_iota(plan.rows) < plan.half
    m0 = jnp.where(low, swap64(b0), b0)
    m1 = jnp.where(low, swap64(b1), b1)
    masks = [m0, jnp.where(low, m0, m1), m1]
    for k in range(3):
        t["m"][:, k * LANES : (k + 1) * LANES] = masks[k]
    u = t["u"][...].astype(BF16)
    x_hi, x_lo = split(w["x"][...])
    proj = dot(u, x_hi, ((1,), (1,))) + dot(u, x_lo, ((1,), (1,)))
    t["p"][...] = proj
    p_hi, p_lo = split(proj)
    d_hi, d_lo = split(w["dtp"][...])
    z = dot(p_hi, d_hi) + dot(p_lo, d_hi) + dot(p_hi, d_lo) + w["small"][0:1, :]
    t["z"][...] = z
    soft = jnp.maximum(z, 0.0) + jnp.log1p(jnp.exp(-jnp.abs(z)))
    dt = soft * t["m"][...]
    t["dt"][...] = dt
    t["dtu"][...] = dt * t["u"][...]


def own_lanes(plan, r, width):
    lane = lax.broadcasted_iota(jnp.int32, (plan.rows, width), 1) % plan.half
    return lane == plan.rank + r


def spread(plan, t):
    k = lax.broadcasted_iota(jnp.int32, (2 * LANES, 2 * LANES), 0) % LANES
    l = lax.broadcasted_iota(jnp.int32, (2 * LANES, 2 * LANES), 1)
    ones = jnp.where((k < plan.half) == (l < LANES), 1.0, 0.0).astype(BF16)
    hi = t["p"][...].astype(BF16).astype(F32)
    both = jnp.concatenate([hi, t["p"][...] - hi], axis=1)
    for r in range(2 * plan.states):
        if r % SPREAD_EVERY == SPREAD_EVERY - 1:
            at = plan.rank + r
            t["bc"][r, :, :LANES] = jnp.broadcast_to(t["p"][:, at : at + 1], (plan.rows, LANES))
            t["bc"][r, :, LANES:] = jnp.broadcast_to(t["p"][:, plan.half + at : plan.half + at + 1], (plan.rows, LANES))
            continue
        t["bc"][r] = dot(jnp.where(own_lanes(plan, r, 2 * LANES), both, 0.0).astype(BF16), ones)


def fold(x):
    low = lane_iota(SUB) < LANES // 2
    t0, t1, t2 = x[:, :LANES], x[:, LANES : 2 * LANES], x[:, 2 * LANES :]
    return jnp.concatenate([jnp.where(low, t0, t2) + t1, jnp.where(low, t2, t0)], axis=1)


def gather(plan, t):
    k = lax.broadcasted_iota(jnp.int32, (2 * LANES, LANES), 0)
    l = lax.broadcasted_iota(jnp.int32, (2 * LANES, LANES), 1)
    first = (k < plan.half) | (k >= LANES + plan.half)
    ones = jnp.where(first == (l < plan.half), 1.0, 0.0).astype(BF16)
    out = jnp.zeros((plan.rows, LANES), F32)
    lane = lane_iota(plan.rows)
    low = lane < plan.half
    for r in range(2 * plan.states):
        if r % GATHER_EVERY == GATHER_EVERY - 1:
            a, b = t["prod"][r, :, :LANES], t["prod"][r, :, LANES:]
            out = jnp.where(lane == plan.rank + r, jnp.sum(jnp.where(low, a, b), axis=1, keepdims=True), out)
            out = jnp.where(lane == plan.half + plan.rank + r, jnp.sum(jnp.where(low, b, a), axis=1, keepdims=True), out)
            continue
        out = jnp.where(own_lanes(plan, r, LANES), dot(t["prod"][r].astype(BF16), ones), out)
    return out


def coefs(plan, t, row, n, which):
    lo = t["bc"][which * plan.states + n, pl.ds(row, SUB), 0:LANES]
    hi = t["bc"][which * plan.states + n, pl.ds(row, SUB), LANES:]
    mid = jnp.where(lane_iota(SUB) < plan.half, lo, hi)
    return jnp.concatenate([lo, mid, hi], axis=1)


def over_steps(plan, g, body, carry, backwards=False):
    u = plan.unroll

    def chunk(i, carry):
        for k in range(u):
            s = i * u + k
            if backwards:
                s = plan.steps - 1 - s
            row = s * plan.lines + g * SUB
            if not isinstance(row, int):
                row = pl.multiple_of(row, SUB)
            carry = body(s, row, carry)
        return carry

    if plan.steps == u:
        return chunk(0, carry)
    return lax.fori_loop(0, plan.steps // u, chunk, carry)


def over_groups(plan, body):
    if plan.groups == 1:
        body(0)
    else:
        lax.fori_loop(0, plan.groups, lambda g, c: (body(g), c)[1], 0)


def chunk_scan(decay, end, backwards):
    at = lax.broadcasted_iota(jnp.int32, end.shape, 0)
    for shift in (1, 2, 4):
        if backwards:
            inside, amount = at < SUB - shift, SUB - shift
        else:
            inside, amount = at >= shift, shift
        prev_end, prev_decay = pltpu.roll(end, amount, axis=0), pltpu.roll(decay, amount, axis=0)
        end = jnp.where(inside, decay * prev_end + end, end)
        decay = jnp.where(inside, decay * prev_decay, decay)
    if backwards:
        return jnp.where(at < SUB - 1, pltpu.roll(end, SUB - 1, axis=0), 0.0)
    return jnp.where(at >= 1, pltpu.roll(end, 1, axis=0), 0.0)


def keep_chunk_decay(plan, w, t):
    total = functools.reduce(lambda a, b: a + b, [t["dt"][s * SUB : (s + 1) * SUB, :] for s in range(plan.steps)])
    for n in range(plan.states):
        t["decay"][n] = jnp.exp2(total * w["rate"][n])


def forward(plan, w, t, keep_states):
    nst = plan.states
    zero = jnp.zeros((SUB, 3 * LANES), F32)
    spread(plan, t)
    if plan.chunked:
        keep_chunk_decay(plan, w, t)
    for n0 in range(0, nst, PER):
        ns = list(range(n0, n0 + PER))

        def group(g, ns=ns, n0=n0):
            start = tuple(zero for _ in ns)
            if plan.chunked:

                def local(s, row, hs):
                    dt, dtu = t["dt"][pl.ds(row, SUB), :], t["dtu"][pl.ds(row, SUB), :]
                    new = []
                    for n, h in zip(ns, hs):
                        a = jnp.exp2(dt * w["rate"][n])
                        t["a"][s, n] = a
                        new.append(a * h + coefs(plan, t, row, n, 0) * dtu)
                    return tuple(new)

                ends = over_steps(plan, g, local, start)
                start = tuple(chunk_scan(t["decay"][n], e, False) for n, e in zip(ns, ends))
            if keep_states:
                for n, h in zip(ns, start):
                    t["h"][0, n, pl.ds(g * SUB, SUB), :] = h

            def full(s, row, hs):
                dt, dtu = t["dt"][pl.ds(row, SUB), :], t["dtu"][pl.ds(row, SUB), :]
                y = t["u"][pl.ds(row, SUB), :] * w["small"][SUB : SUB + 1, :] if n0 == 0 else t["y"][pl.ds(row, SUB), :]
                new = []
                for n, h in zip(ns, hs):
                    a = t["a"][s, n] if plan.chunked else jnp.exp2(dt * w["rate"][n])
                    h = a * h + coefs(plan, t, row, n, 0) * dtu
                    y = y + coefs(plan, t, row, n, 1) * h
                    if keep_states:
                        t["h"][s + 1, n, pl.ds(g * SUB, SUB), :] = h
                    new.append(h)
                t["y"][pl.ds(row, SUB), :] = y
                return tuple(new)

            over_steps(plan, g, full, start)

        over_groups(plan, group)


def backward(plan, w, t):
    nst, per = plan.states, 4
    zero = jnp.zeros((SUB, 3 * LANES), F32)
    for n0 in range(0, nst, per):
        ns = list(range(n0, n0 + per))

        def group(g, ns=ns, n0=n0):
            start = tuple(zero for _ in ns)
            if plan.chunked:

                def local(s, row, gs):
                    gy = t["gy"][pl.ds(row, SUB), :]
                    return tuple(t["a"][s, n] * (coefs(plan, t, row, n, 1) * gy + c) for n, c in zip(ns, gs))

                ends = over_steps(plan, g, local, start, backwards=True)
                start = tuple(chunk_scan(t["decay"][n], e, True) for n, e in zip(ns, ends))

            def full(s, row, carry):
                gs, rs = carry
                dt, dtu = t["dt"][pl.ds(row, SUB), :], t["dtu"][pl.ds(row, SUB), :]
                gy = t["gy"][pl.ds(row, SUB), :]
                if n0 == 0:
                    sb, wq = zero, zero
                else:
                    sb, wq = t["sb"][pl.ds(row, SUB), :], t["wq"][pl.ds(row, SUB), :]
                new_g, new_r = [], []
                for n, c, r in zip(ns, gs, rs):
                    h_now = t["h"][s + 1, n, pl.ds(g * SUB, SUB), :]
                    h_prev = t["h"][s, n, pl.ds(g * SUB, SUB), :]
                    gh = coefs(plan, t, row, n, 1) * gy + c
                    t["prod"][n, pl.ds(row, SUB), :] = fold(gh * dtu)
                    t["prod"][nst + n, pl.ds(row, SUB), :] = fold(gy * h_now)
                    sb = sb + gh * coefs(plan, t, row, n, 0)
                    a = t["a"][s, n] if plan.chunked else jnp.exp2(dt * w["rate"][n])
                    c = a * gh
                    q = c * h_prev
                    wq = wq + q * w["rate"][n]
                    new_g.append(c)
                    new_r.append(r + q * dt)
                t["sb"][pl.ds(row, SUB), :] = sb
                t["wq"][pl.ds(row, SUB), :] = wq
                return tuple(new_g), tuple(new_r)

            _, rs = over_steps(plan, g, full, (start, tuple(zero for _ in ns)), backwards=True)
            for n, r in zip(ns, rs):
                t["gr"][n] = r if plan.groups == 1 else t["gr"][n] + r

        if plan.groups > 1:
            for n in ns:
                t["gr"][n] = zero
        over_groups(plan, group)


def finish(plan, w, t):
    nst, rank = plan.states, plan.rank
    u, dt, gy, sb = t["u"][...], t["dt"][...], t["gy"][...], t["sb"][...]
    g_dt = t["wq"][...] * LN2 + sb * u
    gz = g_dt * t["m"][...] * (1.0 / (1.0 + jnp.exp(-t["z"][...])))
    gz_b = gz.astype(BF16)
    dtp_b = w["dtp"][...].astype(BF16)
    gp = gather(plan, t) + dot(gz_b, dtp_b, ((1,), (1,)))
    gp_b = gp.astype(BF16)
    u_b = u.astype(BF16)
    g_x = dot(gp_b, u_b, ((0,), (0,)))
    g_d = dot(t["p"][...].astype(BF16), gz_b, ((0,), (0,)))
    lane = lax.broadcasted_iota(jnp.int32, (SUB, 3 * LANES), 1)
    first = lane < plan.channels
    wide = -(-(rank + 2 * nst) // SUB) * SUB
    blocks = [jnp.where(first, g_x[r : r + SUB, :], g_x[plan.half + r : plan.half + r + SUB, :]) for r in range(0, wide, SUB)]
    row = lax.broadcasted_iota(jnp.int32, (SUB, 3 * LANES), 0)
    small = jnp.where(first, g_d[0:SUB, :], g_d[plan.half : plan.half + SUB, :])
    small = jnp.where(row == SUB - 2, jnp.sum(gz, axis=0, keepdims=True), small)
    blocks.append(jnp.where(row == SUB - 1, jnp.sum(gy * u, axis=0, keepdims=True), small))
    for n0 in range(0, nst, SUB):
        part = jnp.zeros((SUB, 3 * LANES), F32)
        for n in range(n0, n0 + SUB):
            part = jnp.where(row == n - n0, jnp.sum(t["gr"][n], axis=0, keepdims=True), part)
        blocks.append(part * w["small"][2 * SUB + n0 : 3 * SUB + n0, :])
    grads = jnp.concatenate(blocks, axis=0)
    return grads, gp_b


def input_gradient(plan, back_ref, w, t, gp_b, stack):
    gu = t["sb"][...] * t["dt"][...] + t["gy"][...] * w["small"][SUB : SUB + 1, :] + dot(gp_b, w["x"][...].astype(BF16))
    return unplace(plan, back_ref, [gu[:, lane_tile(k)] for k in range(3)], stack)


def weight_shapes(plan):
    up = -(-(plan.rank + 2 * plan.states) // SUB) * SUB
    return {
        "x": (LANES, 3 * LANES),
        "small": (2 * SUB + plan.states, 3 * LANES),
        "rate": (plan.states, SUB, 3 * LANES),
        "dtp": (LANES, 3 * LANES),
    }, {"pad": (2, max(2 * SUB + plan.states, up), 2 * LANES)}


def token_shapes(plan):
    wide, narrow, double = (plan.rows, 3 * LANES), (plan.rows, LANES), (plan.rows, 2 * LANES)
    kept = {"u": wide, "m": wide, "z": wide, "dt": wide, "dtu": wide, "p": narrow,
            "bc": (2 * plan.states,) + double,
            "h": (plan.steps + 1, plan.states, plan.lines, 3 * LANES)}
    if plan.chunked:
        kept["a"] = (plan.steps, plan.states, plan.lines, 3 * LANES)
        kept["decay"] = (plan.states, SUB, 3 * LANES)
    own = {"y": wide, "x256": double}
    grads = {"gy": wide, "sb": wide, "wq": wide, "prod": (2 * plan.states,) + double,
             "gr": (plan.states, SUB, 3 * LANES), "x256": double}
    if plan.chunked:
        own["stack"] = (2 * plan.rows, 2 * LANES)
    return kept, own, grads


def token_mask(plan, tissue_ref, shape, axis):
    per = plan.rows // tissue_ref.shape[0]
    token = lax.broadcasted_iota(jnp.int32, shape, axis)
    mask = jnp.zeros(shape, F32)
    for k in range(tissue_ref.shape[0]):
        mask = jnp.where((token >= k * per) & (token < (k + 1) * per), tissue_ref[k].astype(F32), mask)
    return mask


def masked_rows(plan, tissue_ref, feat_ref):
    ch = plan.channels
    mask = token_mask(plan, tissue_ref, (SUB, plan.rows), 1)
    tall = jnp.concatenate([mask] * (ch // SUB), axis=0)
    fill = jnp.concatenate([mask] * ((2 * LANES - ch) // SUB), axis=0)
    return jnp.concatenate([feat_ref[...].astype(F32) * tall, fill], axis=0).astype(BF16)


def partner_rows(count, rows, s):
    return pl.ds(pl.multiple_of((lax.axis_index("band") ^ s) * (rows // count), SUB), rows // count)


def send_blocks(refs, tiles, scratch, width):
    scratch[:, :LANES], scratch[:, LANES:] = tiles
    send_from(refs, scratch, width)


def send_from(refs, scratch, width):
    if len(refs) == 1:
        refs[0][...] = scratch[:, :width].astype(BF16)
        return
    for s, ref in enumerate(refs):
        ref[...] = scratch[partner_rows(len(refs), scratch.shape[0], s), :width].astype(BF16)


def receive_blocks(refs, scratch):
    width = refs[0].shape[1]
    if len(refs) == 1:
        scratch[:, :width] = refs[0][...].astype(F32)
        return
    for s, ref in enumerate(refs):
        scratch[partner_rows(len(refs), scratch.shape[0], s), :width] = ref[...].astype(F32)


def rows_forward_kernel(plan, side, *refs):
    count = 9
    far, (send_refs, w, kept, rest, near, sems) = refs[:count], refs[count:]
    copies = [pltpu.make_async_copy(a, b, sems.at[k]) for k, (a, b) in enumerate(zip(far, near))]
    for copy in copies:
        copy.start()
    for copy in copies[:3]:
        copy.wait()
    tissue_ref, feat_ref, perm_ref, back_ref, x_ref, dtp_ref, bias_ref, alog_ref, skip_ref = near
    t = kept | rest
    w = w | rest
    placed = place(plan, perm_ref, masked_rows(plan, tissue_ref, feat_ref), t["u"], True)
    for copy in copies[4:]:
        copy.wait()
    load_weights(plan, side, x_ref, dtp_ref, bias_ref, alog_ref, skip_ref, w)
    prepare(plan, placed, w, t)
    forward(plan, w, t, True)
    copies[3].wait()
    tiles = [t["y"][:, k * LANES : (k + 1) * LANES] for k in range(3)]
    a, b = unplace(plan, back_ref, tiles, t.get("stack"))
    mask = token_mask(plan, tissue_ref, (plan.rows, LANES), 0)
    send_blocks(send_refs, (a, jnp.where(lane_iota(plan.rows) < plan.half, b, mask)), t["x256"], 2 * LANES)


def rows_backward_kernel(plan, side, gy_refs, perm_ref, w, kept, grads_v_ref, mine_ref, theirs_ref, late, rest):
    t = kept | rest | late
    receive_blocks(gy_refs, t["x256"])
    place(plan, perm_ref, t["x256"][...].astype(BF16), t["gy"])
    backward(plan, w, t)
    grads, gp_b = finish(plan, w, t)
    late["gp"][...] = gp_b
    other = grads_v_ref[...].astype(F32)
    odd = lax.axis_index("slide") % 2 == 1
    mine_ref[...] = jnp.where(odd, other, grads).astype(BF16)
    theirs_ref[...] = jnp.where(odd, grads, other).astype(BF16)


def rows_output_kernel(plan, side, tissue_ref, back_ref, w, kept, late, out_ref, own):
    a, b = input_gradient(plan, back_ref, w, kept | late, late["gp"][...], own["stack"])
    own["x256"][:, :LANES], own["x256"][:, LANES:] = a, b
    mask = token_mask(plan, tissue_ref, (SUB, plan.rows), 1)
    turned = jnp.transpose(own["x256"][...])[: plan.channels]
    out_ref[...] = (turned * jnp.concatenate([mask] * (plan.channels // SUB), axis=0)).astype(BF16)


def columns_kernel(plan, side, recv_refs, gy_ref, x_ref, dtp_ref, bias_ref, alog_ref, skip_ref,
                   mixed_ref, out_refs, grads_ref, t):
    ch = plan.channels
    w = t
    load_weights(plan, side, x_ref, dtp_ref, bias_ref, alog_ref, skip_ref, w)
    receive_blocks(recv_refs, t["x256"])
    low = lane_iota(plan.rows) < plan.half
    last = t["x256"][:, LANES:]
    mask = jnp.where(low, swap64(last), last)
    both = jnp.concatenate([t["x256"][:, :LANES] * mask, last * mask], axis=1)
    prepare(plan, place(plan, None, both, t["u"]), w, t)
    t["x256"][:, 0:ch] = gy_ref[...].astype(F32)
    place(plan, None, t["x256"][...], t["gy"])
    forward(plan, w, t, True)
    tiles = [t["y"][:, k * LANES : (k + 1) * LANES] for k in range(3)]
    a, b = unplace(plan, None, tiles, None)
    mixed_ref[:, :LANES] = a.astype(BF16)
    mixed_ref[:, LANES:] = b[:, : ch - LANES].astype(BF16)
    backward(plan, w, t)
    grads, gp_b = finish(plan, w, t)
    grads_ref[...] = grads.astype(BF16)
    a, b = input_gradient(plan, None, w, t, gp_b, None)
    mask = t["m"][:, :LANES]
    send_blocks(out_refs, (a * mask, b * mask), t["x256"], ch)


def tall_shapes(plan):
    steps, ch, nst = plan.steps, plan.channels, plan.states
    up = -(-(plan.rank + 2 * nst) // SUB) * SUB
    field = (steps, ch, LANES)
    ready = {"xs": (2 * up, ch), "ds": (2 * SUB, ch), "al": (2 * (nst + SUB), ch), "rb": (nst + 1, ch, LANES), "gy": field}
    kept = {"u": field, "bc": (steps, 2 * nst, SUB, LANES), "h": (steps, nst, ch, LANES)}
    rest = {
        "z": field, "dt": field, "dtu": field, "sb": field, "wq": field,
        "m": (steps, SUB, LANES), "p": (steps, up, LANES), "acc": (steps, 2 * nst, SUB, LANES),
        "a": (steps, nst, ch, LANES), "x256": (plan.rows, 2 * LANES),
    }
    every = steps * LANES
    late = {"gr": (nst, ch, LANES), "gpb": (2 * up, every, BF16), "rk": (2 * SUB, every, BF16),
            "gzb": (ch, every, BF16), "gyu": (ch, every, BF16), "ub": (ch, every, BF16)}
    return ready, kept, late, rest, {"pad": (2, up + SUB + nst, 2 * LANES)}


def tall_hot(plan):
    part = plan.states + SUB
    hot = np.zeros((6 * part, (plan.states + 1) * LANES), np.float32)
    for k in range(6 * part):
        d, n = k % (2 * part) // part, k % part
        if n <= plan.states:
            at = n * LANES + d * plan.half
            hot[k, at : at + plan.half] = 1.0
    return jnp.asarray(hot, BF16)


def by_step(plan, tiles):
    low = lane_iota(tiles[0].shape[0]) < plan.half
    out = []
    for s in range(plan.steps):
        mine, other = tiles[s // 2], tiles[(plan.steps - 1 - s) // 2]
        out.append(jnp.where(low, mine, other) if s % 2 == 0 else swap64(jnp.where(low, other, mine)))
    return out


def by_row(plan, fields):
    low = lane_iota(fields[0].shape[0]) < plan.half
    sums = []
    for s in range(0, plan.steps, 2):
        other = plan.steps - 1 - s
        even = fields[s] + swap64(fields[other])
        odd = swap64(fields[s + 1]) + fields[other - 1]
        sums.append(jnp.where(low, even, odd))
    return jnp.transpose(jnp.concatenate(sums, axis=1))


def tall_setup_kernel(plan, side, after_ref, gy_ref, hot_ref, x_ref, dtp_ref, bias_ref, alog_ref, skip_ref, t, own):
    ch, nst, rank = plan.channels, plan.states, plan.rank
    wide = rank + 2 * nst
    up = t["xs"].shape[0] // 2
    part = nst + SUB
    t["xs"][...] = jnp.zeros_like(t["xs"])
    t["ds"][...] = jnp.zeros_like(t["ds"])
    t["al"][...] = jnp.zeros_like(t["al"])
    for d in range(2):
        k = 2 * side + d
        t["xs"][d * up : d * up + wide, :] = x_ref[:, k, :]
        t["ds"][d * SUB : d * SUB + rank, :] = dtp_ref[:, k, :]
        t["ds"][d * SUB + rank : d * SUB + rank + 1, :] = bias_ref[k : k + 1, :]
        t["al"][d * part : d * part + nst, :] = -jnp.exp(alog_ref[k])
        t["al"][d * part + nst : d * part + nst + 1, :] = skip_ref[k : k + 1, :]
    scale = jnp.where(lax.broadcasted_iota(jnp.int32, (2 * part, ch), 0) % part < nst, LOG2E, 1.0)
    rest = t["al"][...] * scale
    parts = []
    for _ in range(3):
        parts.append(rest.astype(BF16))
        rest = rest - parts[-1].astype(F32)
    spread_rates = dot(jnp.concatenate(parts, axis=0), hot_ref[...], ((0,), (0,)))
    for n in range(nst + 1):
        t["rb"][n] = spread_rates[:, lane_tile(n)]
    own["x256"][:, 0:ch] = gy_ref[...].astype(F32)
    turned = jnp.transpose(own["x256"][...])
    for s, field in enumerate(by_step(plan, [turned[:ch, lane_tile(k)] for k in range(plan.steps // 2)])):
        t["gy"][s] = field


def tall_output_kernel(plan, side, kept, gain, mixed_ref, own):
    steps, ch, nst = plan.steps, plan.channels, plan.states

    each = 2 if ch % (2 * SUB) == 0 else 1

    def channels(c, carry):
        ats = [pl.ds(pl.multiple_of((c * each + k) * SUB, SUB), SUB) for k in range(each)]
        for s in range(steps):
            ys = [[gain[nst, at, :] * kept["u"][s, at, :], None] for at in ats]
            for n in range(nst):
                weight = kept["bc"][s, nst + n]
                for y, at in zip(ys, ats):
                    more = weight * kept["h"][s, n, at, :]
                    y[n % 2] = more if y[n % 2] is None else y[n % 2] + more
            for y, at in zip(ys, ats):
                own["y"][s, at, :] = y[0] + y[1]
        return carry

    lax.fori_loop(0, ch // (each * SUB), channels, 0)
    mixed_ref[...] = by_row(plan, [own["y"][s] for s in range(steps)]).astype(BF16)


def tall_columns_kernel(plan, side, recv_refs, ready, out_refs, kept, late, rest):
    steps, ch, nst, rank = plan.steps, plan.channels, plan.states, plan.rank
    t = ready | kept | late | rest
    up = t["p"].shape[1]
    part = nst + SUB
    rows0 = ((0,), (0,))
    lanes1 = ((1,), (1,))
    lanes = lane_tile
    x_hi, x_lo = split(t["xs"][...])
    d_hi, d_lo = split(t["ds"][...])

    low8 = lane_iota(SUB) < plan.half
    row8 = lax.broadcasted_iota(jnp.int32, (SUB, LANES), 0)
    receive_blocks(recv_refs, t["x256"])
    turned = jnp.transpose(t["x256"][...])
    for s, field in enumerate(by_step(plan, [turned[: ch + SUB, lanes(k)] for k in range(steps // 2)])):
        t["m"][s] = field[ch:]
        t["u"][s] = field[:ch] * jnp.concatenate([field[ch:]] * (ch // SUB), axis=0)
    u_b = jnp.concatenate([t["u"][s].astype(BF16) for s in range(steps)], axis=1)
    proj = dot(x_hi, u_b) + dot(x_lo, u_b)
    low_up = lane_iota(up) < plan.half
    ranks = []
    for s in range(steps):
        p = jnp.where(low_up, proj[:up, lanes(s)], proj[up:, lanes(s)])
        t["p"][s] = p
        one = jnp.where(row8 < rank, p[:SUB], jnp.where(row8 == rank, 1.0, 0.0))
        ranks.append(jnp.concatenate([jnp.where(low8, one, 0.0), jnp.where(low8, 0.0, one)], axis=0))
        for r in range(2 * nst):
            t["bc"][s, r] = jnp.broadcast_to(p[rank + r : rank + r + 1, :], (SUB, LANES))
    r_hi, r_lo = split(jnp.concatenate(ranks, axis=1))
    z = dot(d_hi, r_hi, rows0) + dot(d_lo, r_hi, rows0) + dot(d_hi, r_lo, rows0)
    for s in range(steps):
        z_s = z[:, lanes(s)]
        t["z"][s] = z_s
        soft = jnp.maximum(z_s, 0.0) + jnp.log1p(jnp.exp(-jnp.abs(z_s)))
        dt = soft * jnp.concatenate([t["m"][s]] * (ch // SUB), axis=0)
        t["dt"][s] = dt
        t["dtu"][s] = dt * t["u"][s]

    each = 2 if ch % (2 * SUB) == 0 else 1

    def channels_at(c):
        return [pl.ds(pl.multiple_of((c * each + k) * SUB, SUB), SUB) for k in range(each)]

    def scan_forward(c, carry):
        ats = channels_at(c)
        dts = [[t["dt"][s, at, :] for s in range(steps)] for at in ats]
        dtus = [[t["dtu"][s, at, :] for s in range(steps)] for at in ats]
        for n in range(nst):
            hs = [None] * each
            for s in range(steps):
                b = t["bc"][s, n]
                for k, at in enumerate(ats):
                    h = b * dtus[k][s]
                    if s:
                        a = jnp.exp2(dts[k][s] * t["rb"][n, at, :])
                        t["a"][s, n, at, :] = a
                        h = a * hs[k] + h
                    t["h"][s, n, at, :] = h
                    hs[k] = h
        return carry

    lax.fori_loop(0, ch // (each * SUB), scan_forward, 0)
    t["acc"][...] = jnp.zeros_like(t["acc"])

    def scan_backward(c, carry):
        ats = channels_at(c)
        zero = jnp.zeros((SUB, LANES), F32)
        sbs, wqs = [[zero] * steps for _ in ats], [[zero] * steps for _ in ats]
        for n in range(nst):
            after, g_rates = [None] * each, [None] * each
            for s in reversed(range(steps)):
                b, c_now = t["bc"][s, n], t["bc"][s, nst + n]
                to_b, to_c = t["acc"][s, n], t["acc"][s, nst + n]
                for k, at in enumerate(ats):
                    gy = t["gy"][s, at, :]
                    gh = c_now * gy
                    if after[k] is not None:
                        gh = gh + after[k]
                    to_b = to_b + gh * t["dtu"][s, at, :]
                    to_c = to_c + gy * t["h"][s, n, at, :]
                    sbs[k][s] = sbs[k][s] + gh * b
                    if s:
                        after[k] = t["a"][s, n, at, :] * gh
                        q = after[k] * t["h"][s - 1, n, at, :]
                        wqs[k][s] = wqs[k][s] + q * t["rb"][n, at, :]
                        more = q * t["dt"][s, at, :]
                        g_rates[k] = more if g_rates[k] is None else g_rates[k] + more
                t["acc"][s, n], t["acc"][s, nst + n] = to_b, to_c
            for k, at in enumerate(ats):
                t["gr"][n, at, :] = g_rates[k]
        for k, at in enumerate(ats):
            for s in range(steps):
                t["sb"][s, at, :] = sbs[k][s]
                t["wq"][s, at, :] = wqs[k][s]
        return carry

    lax.fori_loop(0, ch // (each * SUB), scan_backward, 0)

    gzs, gyus = [], []
    for s in range(steps):
        mask = jnp.concatenate([t["m"][s]] * (ch // SUB), axis=0)
        g_dt = t["wq"][s] * LN2 + t["sb"][s] * t["u"][s]
        gzs.append((g_dt * mask * (1.0 / (1.0 + jnp.exp(-t["z"][s])))).astype(BF16))
        gyus.append((t["gy"][s] * t["u"][s]).astype(BF16))
    gz_b = jnp.concatenate(gzs, axis=1)
    t["gzb"][...], t["gyu"][...], t["ub"][...], t["rk"][...] = gz_b, jnp.concatenate(gyus, axis=1), u_b, r_hi
    g_rank = dot(d_hi, gz_b)
    row_up = lax.broadcasted_iota(jnp.int32, (SUB, LANES), 0)
    g_ps = []
    for s in range(steps):
        tiles = [jnp.where(low8, g_rank[:SUB, lanes(s)], g_rank[SUB:, lanes(s)])]
        tiles += [jnp.zeros((SUB, LANES), F32)] * (up // SUB - 1)
        tiles[0] = jnp.where(row_up < rank, tiles[0], 0.0)
        for r in range(2 * nst):
            k, j = divmod(rank + r, SUB)
            tiles[k] = jnp.where(row_up == j, jnp.sum(t["acc"][s, r], axis=0, keepdims=True), tiles[k])
        g_p = jnp.concatenate(tiles, axis=0)
        g_ps.append(jnp.concatenate([jnp.where(low_up, g_p, 0.0), jnp.where(low_up, 0.0, g_p)], axis=0))
    gp_b = jnp.concatenate(g_ps, axis=1).astype(BF16)
    t["gpb"][...] = gp_b
    through = dot(x_hi, gp_b, rows0)
    gus = []
    for s in range(steps):
        mask = jnp.concatenate([t["m"][s]] * (ch // SUB), axis=0)
        gus.append((t["sb"][s] * t["dt"][s] + t["rb"][nst] * t["gy"][s] + through[:, lanes(s)]) * mask)
    t["x256"][:, 0:ch] = by_row(plan, gus)
    send_from(out_refs, t["x256"], ch)


def tall_grads_kernel(plan, side, t, al_ref, grads_ref, own):
    steps, ch, nst = plan.steps, plan.channels, plan.states
    part = nst + SUB
    lanes1 = ((1,), (1,))
    gp_b, u_b, r_hi, gz_b, gyu_b = t["gpb"][...], t["ub"][...], t["rk"][...], t["gzb"][...], t["gyu"][...]
    up = gp_b.shape[0] // 2
    low8 = lane_iota(SUB) < plan.half
    row8 = lax.broadcasted_iota(jnp.int32, (SUB, LANES), 0)
    g_x = dot(gp_b, u_b, lanes1)
    g_d = dot(r_hi, gz_b, lanes1)
    halves = jnp.where(row8 == 0, jnp.where(low8, 1.0, 0.0), jnp.where(row8 == 1, jnp.where(low8, 0.0, 1.0), 0.0)).astype(BF16)
    g_skip = dot(jnp.concatenate([halves] * steps, axis=1), gyu_b, lanes1)
    pad = own["pad"]
    row_d = lax.broadcasted_iota(jnp.int32, (SUB, ch), 0)
    for d in range(2):
        pad[d, 0:up, 0:ch] = g_x[d * up : (d + 1) * up]
        pad[d, up : up + SUB, 0:ch] = jnp.where(row_d == SUB - 1, g_skip[d : d + 1], g_d[d * SUB : (d + 1) * SUB])
    for n0 in range(0, nst, SUB):
        both = [jnp.zeros((SUB, ch), F32)] * 2
        for n in range(n0, n0 + SUB):
            sums = dot(halves, t["gr"][n].astype(BF16), lanes1)
            both = [jnp.where(row_d == n - n0, sums[d : d + 1], both[d]) for d in range(2)]
        for d in range(2):
            pad[d, up + SUB + n0 : up + 2 * SUB + n0, 0:ch] = both[d] * al_ref[d * part + n0 : d * part + n0 + SUB, :]
    first, second = pad[0], pad[1]
    tiles = pack_tiles(first[:, :LANES], first[:, LANES:], second[:, :LANES], second[:, LANES:])
    for k in range(3):
        grads_ref[:, lane_tile(k)] = tiles[k].astype(BF16)


def unpack_kernel(plan, mine_ref, theirs_ref, gx_ref, gd_ref, gb_ref, ga_ref, gs_ref):
    nst, rank, ch = plan.states, plan.rank, plan.channels
    wide = rank + 2 * nst
    up = -(-wide // SUB) * SUB
    odd = lax.axis_index("slide") % 2 == 1
    mine, theirs = mine_ref[...].astype(F32), theirs_ref[...].astype(F32)
    for side, total in enumerate((jnp.where(odd, theirs, mine), jnp.where(odd, mine, theirs))):
        tiles = [total[:, k * LANES : (k + 1) * LANES] for k in range(3)]
        for d, (a, b) in enumerate(((tiles[0], tiles[1]), (tiles[2], swap64(tiles[1])))):
            k = 2 * side + d
            for lo, hi, part in ((0, LANES, a), (LANES, ch, b[:, : ch - LANES])):
                gx_ref[:, k, lo:hi] = part[0:wide, :]
                gd_ref[:, k, lo:hi] = part[up : up + rank, :]
                gb_ref[k : k + 1, lo:hi] = part[up + SUB - 2 : up + SUB - 1, :]
                gs_ref[k : k + 1, lo:hi] = part[up + SUB - 1 : up + SUB, :]
                ga_ref[k, :, lo:hi] = part[up + SUB : up + SUB + nst, :]


def call(kernel, plan, side, out_shape, args, scratch, name, cost, scalars=0, far=()):
    whole = pl.BlockSpec(memory_space=pltpu.VMEM)
    specs = list(jax.tree.map(lambda _: whole, tuple(args)))
    if scalars:
        specs[0] = pl.BlockSpec(memory_space=pltpu.SMEM)
    scratches = [arrays(scratch, pltpu.VMEM)]
    limit = VMEM_SPARE + sum(int(np.prod(x.shape)) * x.dtype.itemsize for x in jax.tree.leaves(arrays(scratch)))
    if far:
        args = [pltpu.with_memory_space_constraint(a, pltpu.HBM) if k in far else a for k, a in enumerate(args)]
        for k in far:
            specs[k] = pl.BlockSpec(memory_space=pltpu.HBM)
        limit += sum(int(np.prod(args[k].shape)) * 4 for k in far)
        scratches += [[(pltpu.SMEM if args[k].ndim == 1 else pltpu.VMEM)(args[k].shape, args[k].dtype) for k in far], pltpu.SemaphoreType.DMA((len(far),))]
    return pl.pallas_call(
        functools.partial(kernel, plan, side), out_shape=out_shape, in_specs=tuple(specs),
        out_specs=jax.tree.map(lambda _: whole, out_shape), scratch_shapes=scratches,
        name=name, cost_estimate=pl.CostEstimate(flops=cost * 10**6, bytes_accessed=4 * 10**6, transcendentals=0),
        compiler_params=pltpu.CompilerParams(vmem_limit_bytes=limit),
    )(*args)


def arrays(shapes, make=jax.ShapeDtypeStruct):
    def one(shape):
        return make(shape, F32) if isinstance(shape[-1], int) else make(shape[:-1], shape[-1])

    return jax.tree.map(one, shapes, is_leaf=lambda x: isinstance(x, tuple))


def swap(x, axis, step):
    return lax.ppermute(x, axis, [(i, i ^ step) for i in range(lax.axis_size(axis))])


def cross(x, mask):
    axes = ("slide", "band")
    return lax.ppermute(x, axes, [(i, i ^ mask) for i in range(lax.axis_size(axes))])


def deliver(blocks, rows):
    bands = lax.axis_size("band")
    if len(blocks) == 1:
        block = blocks[0].reshape(bands, rows // bands, -1)
        return [lax.all_to_all(block, "band", split_axis=0, concat_axis=0, tiled=True).reshape(rows, -1)]
    got = {s: swap(blocks[s], "band", s) for s in reversed(range(1, bands))}
    return [blocks[0]] + [got[s] for s in range(1, bands)]


def shards(features, tissue, cotangent, x_proj, dt_proj, dt_bias, a_log, d_skip):
    _, _, width, channels = features.shape
    _, height, cols_here, _ = cotangent.shape
    bands = lax.axis_size("band")
    dirs, rank, states = dt_proj.shape[0], dt_proj.shape[1], a_log.shape[1]
    rows_plan = Plan(width // SUB, SUB, True, channels, states, rank)
    cols_plan = Plan(height, cols_here, False, channels, states, rank)
    weights = [jnp.transpose(x_proj, (2, 0, 1)), jnp.transpose(dt_proj, (1, 0, 2)), dt_bias, a_log, d_skip]
    feat = jnp.transpose(features.reshape(width, channels))
    keep = tissue.reshape(-1)
    packed = -(-(rank + 2 * states) // SUB) * SUB + SUB + states
    grads_shape = jax.ShapeDtypeStruct((packed, 3 * LANES), BF16)

    perm, back = rows_plan.perm()
    w_kept, w_own = weight_shapes(rows_plan)
    kept, own, grads = token_shapes(rows_plan)
    count = bands if bands in (2, 4) else 1
    tokens = height * cols_here

    def blocks(rows, lanes):
        return [jax.ShapeDtypeStruct((rows // count, lanes), BF16)] * count

    send, w_rows, t_rows = call(
        rows_forward_kernel, rows_plan, 0, (blocks(width, 2 * LANES), arrays(w_kept), arrays(kept)),
        [keep, feat, perm, back] + weights, own | w_own, "rows_forward", 4000, 0, tuple(range(9)))
    moved = deliver(send, width)
    cols_out = (jax.ShapeDtypeStruct((tokens, channels), BF16), blocks(tokens, channels), grads_shape)
    cols_in = [moved, cotangent.reshape(tokens, channels)]
    if 2 * cols_here == LANES and height % 2 == 0 and rank < SUB - 1:
        ready, kept_c, late_c, own_c, pad_c = tall_shapes(cols_plan)
        ready = call(tall_setup_kernel, cols_plan, 1, arrays(ready),
                     [w_rows["small"], cols_in[1], tall_hot(cols_plan)] + weights, {"x256": own_c["x256"]}, "columns_setup", 1000)
        grad_carried, kept_c, late_c = call(
            tall_columns_kernel, cols_plan, 1, (cols_out[1], arrays(kept_c), arrays(late_c)), [moved, ready], own_c, "columns", 8000)
        grads_v = call(tall_grads_kernel, cols_plan, 1, grads_shape, [late_c, ready["al"]], pad_c, "columns_grads", 1000)
        mixed = call(tall_output_kernel, cols_plan, 1, cols_out[0], [kept_c, ready["rb"]], {"y": own_c["z"]}, "columns_output", 1000)
    else:
        w_kept, w_own = weight_shapes(cols_plan)
        kept_c, own_c, grads_c = token_shapes(cols_plan)
        mixed, grad_carried, grads_v = call(
            columns_kernel, cols_plan, 1, cols_out, cols_in + weights,
            kept_c | own_c | grads_c | w_kept | w_own, "columns", 8000)
    returned = deliver(grad_carried, tokens)
    late = {k: grads.pop(k) for k in ("sb", "gy")} | {"gp": (width, LANES, BF16)}
    mine, theirs, late = call(
        rows_backward_kernel, rows_plan, 0, (grads_shape, grads_shape, arrays(late)),
        [returned, perm, w_rows, t_rows, grads_v], grads, "rows_backward", 8000)
    needed = {k: t_rows[k] for k in ("dt",)}
    grad_features = call(
        rows_output_kernel, rows_plan, 0, jax.ShapeDtypeStruct((channels, width), BF16),
        [keep, back, {k: w_rows[k] for k in ("small", "x")}, needed, late], {k: own[k] for k in ("stack", "x256")}, "rows_output", 1000, 1)
    mine = (mine.astype(F32) + swap(theirs, "slide", 1).astype(F32)).astype(BF16)
    hops = [bands << k for k in range(1, (lax.axis_size("slide") - 1).bit_length())]
    hops += [1 << k for k in range((bands - 1).bit_length())]
    late = [mixed, grad_features]
    while hops:
        first, hops = hops[:HOPS], hops[HOPS:]
        masks = [0]
        for hop in first:
            masks += [mask ^ hop for mask in masks]
        got = {mask: cross(mine, mask) for mask in reversed(masks[1:])}
        if late:
            hidden = late.pop(0)
            got, hidden = lax.optimization_barrier((got, hidden))
            if late:
                mixed = hidden
            else:
                grad_features = hidden
        terms = [mine.astype(F32)] + [got[mask].astype(F32) for mask in masks[1:]]
        while len(terms) > 1:
            terms = [a + b for a, b in zip(terms[::2], terms[1::2])]
        mine = terms[0].astype(BF16)
    theirs = swap(mine, "slide", 1)
    shapes = [(rank + 2 * states, dirs, channels), (rank, dirs, channels), (dirs, channels), (dirs, states, channels), (dirs, channels)]
    gx, gd, gb, ga, gs = pl.pallas_call(
        functools.partial(unpack_kernel, rows_plan), out_shape=[jax.ShapeDtypeStruct(s, F32) for s in shapes], name="unpack",
        compiler_params=pltpu.CompilerParams(vmem_limit_bytes=VMEM_LIMIT),
    )(mine, theirs)
    return (mixed.reshape(cotangent.shape), jnp.transpose(grad_features).reshape(features.shape), jnp.transpose(gx, (1, 2, 0)),
            jnp.transpose(gd, (1, 0, 2)), gb, ga, gs)


def solution(mesh):
    in_specs = (
        P(("groups", "slide"), "band", None, None),
        P(("groups", "slide"), "band", None),
        P(("groups", "slide"), None, "band", None),
        P(), P(), P(), P(), P(),
    )
    out_specs = (
        P(("groups", "slide"), None, "band", None),
        P(("groups", "slide"), "band", None, None),
        P("groups", None, None),
        P("groups", None, None),
        P("groups", None),
        P("groups", None, None),
        P("groups", None),
    )
    return jax.shard_map(shards, mesh=mesh, in_specs=in_specs, out_specs=out_specs, check_vma=False)
```

```python
import functools

import jax
import jax.numpy as jnp
import numpy as np
from jax import lax
from jax.experimental import pallas as pl
from jax.experimental.pallas import tpu as pltpu
from jax.sharding import PartitionSpec as P

F32 = jnp.float32
BF16 = jnp.bfloat16
LANES = 128
SUB = 8
LOG2E = 1.4426950408889634
LN2 = 0.6931471805599453
VMEM_LIMIT = 8 * 2**20
VMEM_SPARE = 2 * 2**20
PER = 8
SPREAD_EVERY = 4
GATHER_EVERY = 3
HOPS = 2


def dot(a, b, dims=((1,), (0,))):
    return lax.dot_general(a, b, (dims, ((), ())), preferred_element_type=F32)


def split(x):
    hi = x.astype(BF16)
    return hi, (x - hi.astype(F32)).astype(BF16)


def lane_tile(k):
    return slice(k * LANES, (k + 1) * LANES)


def swap64(x):
    return pltpu.roll(x, LANES // 2, axis=1)


def lane_iota(rows):
    return lax.broadcasted_iota(jnp.int32, (rows, LANES), 1)


def pack_tiles(a0, b0, a1, b1):
    low = lane_iota(a0.shape[0]) < LANES // 2
    return [a0, jnp.where(low, b0, swap64(b1)), a1]


class Plan:
    def __init__(self, steps, lines, chunked, channels, states, rank):
        self.steps, self.lines, self.chunked = steps, lines, chunked
        self.rows = steps * lines
        self.groups = lines // SUB
        self.channels, self.states, self.rank = channels, states, rank
        self.half = LANES // 2
        self.unroll = next(k for k in (8, 4, 2, 1) if steps % k == 0)

    def reverse(self, x):
        return jnp.concatenate([x[s * self.lines : (s + 1) * self.lines] for s in reversed(range(self.steps))], axis=0)

    def perm(self):
        r = np.arange(self.rows)
        s, j = r // self.lines, r % self.lines
        first = j * self.steps + s
        second = self.rows - 1 - first
        hot = np.zeros((self.rows, 2 * self.rows), np.float32)
        hot[r, first] = 1.0
        hot[r, self.rows + second] = 1.0
        back = np.concatenate([hot[:, : self.rows].T, hot[:, self.rows :].T], axis=1)
        return jnp.asarray(hot, BF16), jnp.asarray(back, BF16)


def load_weights(plan, side, x_ref, dtp_ref, bias_ref, alog_ref, skip_ref, w):
    ch, nst = plan.channels, plan.states
    pad, half = w["pad"], plan.half
    pad[:, :, ch:] = jnp.zeros((2, pad.shape[1], 2 * LANES - ch), F32)

    def halves(rows):
        first, second = pad[0, 0:rows, :], pad[1, 0:rows, :]
        return first[:, :LANES], first[:, LANES:], second[:, :LANES], second[:, LANES:]

    def diagonal(ref, dst):
        count = ref.shape[0]
        rows = -(-count // SUB) * SUB
        dst[...] = jnp.zeros_like(dst)
        for d in range(2):
            pad[d, rows - SUB : rows, 0:ch] = jnp.zeros((SUB, ch), F32)
            pad[d, 0:count, 0:ch] = ref[:, 2 * side + d, :]
        a0, b0, a1, b1 = halves(rows)
        dst[0:rows, 0:LANES] = a0
        dst[0:rows, LANES : 2 * LANES] = b0
        dst[half : half + rows, LANES : 2 * LANES] = swap64(b1)
        dst[half : half + rows, 2 * LANES :] = a1

    diagonal(x_ref, w["x"])
    diagonal(dtp_ref, w["dtp"])
    for d in range(2):
        pad[d, 0:1, 0:ch] = bias_ref[2 * side + d : 2 * side + d + 1, :]
        pad[d, SUB : SUB + 1, 0:ch] = skip_ref[2 * side + d : 2 * side + d + 1, :]
        pad[d, 2 * SUB : 2 * SUB + nst, 0:ch] = alog_ref[2 * side + d]
    tiles = pack_tiles(*halves(2 * SUB + nst))
    for k in range(3):
        at = slice(k * LANES, (k + 1) * LANES)
        w["small"][0 : 2 * SUB, at] = tiles[k][0 : 2 * SUB]
        rates = -jnp.exp(tiles[k][2 * SUB :])
        w["small"][2 * SUB :, at] = rates
        for n in range(nst):
            w["rate"][n, :, at] = jnp.broadcast_to(rates[n : n + 1, :] * LOG2E, (SUB, LANES))


def place(plan, perm_ref, x, dst, tall=False):
    if plan.chunked:
        dims = ((1,), (1,)) if tall else ((1,), (0,))
        first = dot(perm_ref[:, : plan.rows], x, dims)
        second = dot(perm_ref[:, plan.rows :], x, dims)
    else:
        first, second = x, plan.reverse(x)
    a0, b0, a1, b1 = first[:, :LANES], first[:, LANES:], second[:, :LANES], second[:, LANES:]
    for k, tile in enumerate(pack_tiles(a0, b0, a1, b1)):
        dst[:, k * LANES : (k + 1) * LANES] = tile
    return b0, b1


def unplace(plan, back_ref, packed, stack):
    t0, t1, t2 = packed
    if not plan.chunked:
        return t0 + plan.reverse(t2), t1 + plan.reverse(swap64(t1))
    stack[0 : plan.rows, 0:LANES] = t0
    stack[0 : plan.rows, LANES:] = t1
    stack[plan.rows :, 0:LANES] = t2
    stack[plan.rows :, LANES:] = swap64(t1)
    hi, lo = split(stack[...])
    out = dot(back_ref[...], hi) + dot(back_ref[...], lo)
    return out[:, :LANES], out[:, LANES:]


def prepare(plan, placed, w, t):
    b0, b1 = placed
    low = lane_iota(plan.rows) < plan.half
    m0 = jnp.where(low, swap64(b0), b0)
    m1 = jnp.where(low, swap64(b1), b1)
    masks = [m0, jnp.where(low, m0, m1), m1]
    for k in range(3):
        t["m"][:, k * LANES : (k + 1) * LANES] = masks[k]
    u = t["u"][...].astype(BF16)
    x_hi, x_lo = split(w["x"][...])
    proj = dot(u, x_hi, ((1,), (1,))) + dot(u, x_lo, ((1,), (1,)))
    t["p"][...] = proj
    p_hi, p_lo = split(proj)
    d_hi, d_lo = split(w["dtp"][...])
    z = dot(p_hi, d_hi) + dot(p_lo, d_hi) + dot(p_hi, d_lo) + w["small"][0:1, :]
    t["z"][...] = z
    soft = jnp.maximum(z, 0.0) + jnp.log1p(jnp.exp(-jnp.abs(z)))
    dt = soft * t["m"][...]
    t["dt"][...] = dt
    t["dtu"][...] = dt * t["u"][...]


def own_lanes(plan, r, width):
    lane = lax.broadcasted_iota(jnp.int32, (plan.rows, width), 1) % plan.half
    return lane == plan.rank + r


def spread(plan, t):
    k = lax.broadcasted_iota(jnp.int32, (2 * LANES, 2 * LANES), 0) % LANES
    l = lax.broadcasted_iota(jnp.int32, (2 * LANES, 2 * LANES), 1)
    ones = jnp.where((k < plan.half) == (l < LANES), 1.0, 0.0).astype(BF16)
    hi = t["p"][...].astype(BF16).astype(F32)
    both = jnp.concatenate([hi, t["p"][...] - hi], axis=1)
    for r in range(2 * plan.states):
        if r % SPREAD_EVERY == SPREAD_EVERY - 1:
            at = plan.rank + r
            t["bc"][r, :, :LANES] = jnp.broadcast_to(t["p"][:, at : at + 1], (plan.rows, LANES))
            t["bc"][r, :, LANES:] = jnp.broadcast_to(t["p"][:, plan.half + at : plan.half + at + 1], (plan.rows, LANES))
            continue
        t["bc"][r] = dot(jnp.where(own_lanes(plan, r, 2 * LANES), both, 0.0).astype(BF16), ones)


def fold(x):
    low = lane_iota(SUB) < LANES // 2
    t0, t1, t2 = x[:, :LANES], x[:, LANES : 2 * LANES], x[:, 2 * LANES :]
    return jnp.concatenate([jnp.where(low, t0, t2) + t1, jnp.where(low, t2, t0)], axis=1)


def gather(plan, t):
    k = lax.broadcasted_iota(jnp.int32, (2 * LANES, LANES), 0)
    l = lax.broadcasted_iota(jnp.int32, (2 * LANES, LANES), 1)
    first = (k < plan.half) | (k >= LANES + plan.half)
    ones = jnp.where(first == (l < plan.half), 1.0, 0.0).astype(BF16)
    out = jnp.zeros((plan.rows, LANES), F32)
    lane = lane_iota(plan.rows)
    low = lane < plan.half
    for r in range(2 * plan.states):
        if r % GATHER_EVERY == GATHER_EVERY - 1:
            a, b = t["prod"][r, :, :LANES], t["prod"][r, :, LANES:]
            out = jnp.where(lane == plan.rank + r, jnp.sum(jnp.where(low, a, b), axis=1, keepdims=True), out)
            out = jnp.where(lane == plan.half + plan.rank + r, jnp.sum(jnp.where(low, b, a), axis=1, keepdims=True), out)
            continue
        out = jnp.where(own_lanes(plan, r, LANES), dot(t["prod"][r].astype(BF16), ones), out)
    return out


def coefs(plan, t, row, n, which):
    lo = t["bc"][which * plan.states + n, pl.ds(row, SUB), 0:LANES]
    hi = t["bc"][which * plan.states + n, pl.ds(row, SUB), LANES:]
    mid = jnp.where(lane_iota(SUB) < plan.half, lo, hi)
    return jnp.concatenate([lo, mid, hi], axis=1)


def over_steps(plan, g, body, carry, backwards=False):
    u = plan.unroll

    def chunk(i, carry):
        for k in range(u):
            s = i * u + k
            if backwards:
                s = plan.steps - 1 - s
            row = s * plan.lines + g * SUB
            if not isinstance(row, int):
                row = pl.multiple_of(row, SUB)
            carry = body(s, row, carry)
        return carry

    if plan.steps == u:
        return chunk(0, carry)
    return lax.fori_loop(0, plan.steps // u, chunk, carry)


def over_groups(plan, body):
    if plan.groups == 1:
        body(0)
    else:
        lax.fori_loop(0, plan.groups, lambda g, c: (body(g), c)[1], 0)


def chunk_scan(decay, end, backwards):
    at = lax.broadcasted_iota(jnp.int32, end.shape, 0)
    for shift in (1, 2, 4):
        if backwards:
            inside, amount = at < SUB - shift, SUB - shift
        else:
            inside, amount = at >= shift, shift
        prev_end, prev_decay = pltpu.roll(end, amount, axis=0), pltpu.roll(decay, amount, axis=0)
        end = jnp.where(inside, decay * prev_end + end, end)
        decay = jnp.where(inside, decay * prev_decay, decay)
    if backwards:
        return jnp.where(at < SUB - 1, pltpu.roll(end, SUB - 1, axis=0), 0.0)
    return jnp.where(at >= 1, pltpu.roll(end, 1, axis=0), 0.0)


def keep_chunk_decay(plan, w, t):
    total = functools.reduce(lambda a, b: a + b, [t["dt"][s * SUB : (s + 1) * SUB, :] for s in range(plan.steps)])
    for n in range(plan.states):
        t["decay"][n] = jnp.exp2(total * w["rate"][n])


def forward(plan, w, t, keep_states):
    nst = plan.states
    zero = jnp.zeros((SUB, 3 * LANES), F32)
    spread(plan, t)
    if plan.chunked:
        keep_chunk_decay(plan, w, t)
    for n0 in range(0, nst, PER):
        ns = list(range(n0, n0 + PER))

        def group(g, ns=ns, n0=n0):
            start = tuple(zero for _ in ns)
            if plan.chunked:

                def local(s, row, hs):
                    dt, dtu = t["dt"][pl.ds(row, SUB), :], t["dtu"][pl.ds(row, SUB), :]
                    new = []
                    for n, h in zip(ns, hs):
                        a = jnp.exp2(dt * w["rate"][n])
                        t["a"][s, n] = a
                        new.append(a * h + coefs(plan, t, row, n, 0) * dtu)
                    return tuple(new)

                ends = over_steps(plan, g, local, start)
                start = tuple(chunk_scan(t["decay"][n], e, False) for n, e in zip(ns, ends))
            if keep_states:
                for n, h in zip(ns, start):
                    t["h"][0, n, pl.ds(g * SUB, SUB), :] = h

            def full(s, row, hs):
                dt, dtu = t["dt"][pl.ds(row, SUB), :], t["dtu"][pl.ds(row, SUB), :]
                y = t["u"][pl.ds(row, SUB), :] * w["small"][SUB : SUB + 1, :] if n0 == 0 else t["y"][pl.ds(row, SUB), :]
                new = []
                for n, h in zip(ns, hs):
                    a = t["a"][s, n] if plan.chunked else jnp.exp2(dt * w["rate"][n])
                    h = a * h + coefs(plan, t, row, n, 0) * dtu
                    y = y + coefs(plan, t, row, n, 1) * h
                    if keep_states:
                        t["h"][s + 1, n, pl.ds(g * SUB, SUB), :] = h
                    new.append(h)
                t["y"][pl.ds(row, SUB), :] = y
                return tuple(new)

            over_steps(plan, g, full, start)

        over_groups(plan, group)


def backward(plan, w, t):
    nst, per = plan.states, 4
    zero = jnp.zeros((SUB, 3 * LANES), F32)
    for n0 in range(0, nst, per):
        ns = list(range(n0, n0 + per))

        def group(g, ns=ns, n0=n0):
            start = tuple(zero for _ in ns)
            if plan.chunked:

                def local(s, row, gs):
                    gy = t["gy"][pl.ds(row, SUB), :]
                    return tuple(t["a"][s, n] * (coefs(plan, t, row, n, 1) * gy + c) for n, c in zip(ns, gs))

                ends = over_steps(plan, g, local, start, backwards=True)
                start = tuple(chunk_scan(t["decay"][n], e, True) for n, e in zip(ns, ends))

            def full(s, row, carry):
                gs, rs = carry
                dt, dtu = t["dt"][pl.ds(row, SUB), :], t["dtu"][pl.ds(row, SUB), :]
                gy = t["gy"][pl.ds(row, SUB), :]
                if n0 == 0:
                    sb, wq = zero, zero
                else:
                    sb, wq = t["sb"][pl.ds(row, SUB), :], t["wq"][pl.ds(row, SUB), :]
                new_g, new_r = [], []
                for n, c, r in zip(ns, gs, rs):
                    h_now = t["h"][s + 1, n, pl.ds(g * SUB, SUB), :]
                    h_prev = t["h"][s, n, pl.ds(g * SUB, SUB), :]
                    gh = coefs(plan, t, row, n, 1) * gy + c
                    t["prod"][n, pl.ds(row, SUB), :] = fold(gh * dtu)
                    t["prod"][nst + n, pl.ds(row, SUB), :] = fold(gy * h_now)
                    sb = sb + gh * coefs(plan, t, row, n, 0)
                    a = t["a"][s, n] if plan.chunked else jnp.exp2(dt * w["rate"][n])
                    c = a * gh
                    q = c * h_prev
                    wq = wq + q * w["rate"][n]
                    new_g.append(c)
                    new_r.append(r + q * dt)
                t["sb"][pl.ds(row, SUB), :] = sb
                t["wq"][pl.ds(row, SUB), :] = wq
                return tuple(new_g), tuple(new_r)

            _, rs = over_steps(plan, g, full, (start, tuple(zero for _ in ns)), backwards=True)
            for n, r in zip(ns, rs):
                t["gr"][n] = r if plan.groups == 1 else t["gr"][n] + r

        if plan.groups > 1:
            for n in ns:
                t["gr"][n] = zero
        over_groups(plan, group)


def finish(plan, w, t):
    nst, rank = plan.states, plan.rank
    u, dt, gy, sb = t["u"][...], t["dt"][...], t["gy"][...], t["sb"][...]
    g_dt = t["wq"][...] * LN2 + sb * u
    gz = g_dt * t["m"][...] * (1.0 / (1.0 + jnp.exp(-t["z"][...])))
    gz_b = gz.astype(BF16)
    dtp_b = w["dtp"][...].astype(BF16)
    gp = gather(plan, t) + dot(gz_b, dtp_b, ((1,), (1,)))
    gp_b = gp.astype(BF16)
    u_b = u.astype(BF16)
    g_x = dot(gp_b, u_b, ((0,), (0,)))
    g_d = dot(t["p"][...].astype(BF16), gz_b, ((0,), (0,)))
    lane = lax.broadcasted_iota(jnp.int32, (SUB, 3 * LANES), 1)
    first = lane < plan.channels
    wide = -(-(rank + 2 * nst) // SUB) * SUB
    blocks = [jnp.where(first, g_x[r : r + SUB, :], g_x[plan.half + r : plan.half + r + SUB, :]) for r in range(0, wide, SUB)]
    row = lax.broadcasted_iota(jnp.int32, (SUB, 3 * LANES), 0)
    small = jnp.where(first, g_d[0:SUB, :], g_d[plan.half : plan.half + SUB, :])
    small = jnp.where(row == SUB - 2, jnp.sum(gz, axis=0, keepdims=True), small)
    blocks.append(jnp.where(row == SUB - 1, jnp.sum(gy * u, axis=0, keepdims=True), small))
    for n0 in range(0, nst, SUB):
        part = jnp.zeros((SUB, 3 * LANES), F32)
        for n in range(n0, n0 + SUB):
            part = jnp.where(row == n - n0, jnp.sum(t["gr"][n], axis=0, keepdims=True), part)
        blocks.append(part * w["small"][2 * SUB + n0 : 3 * SUB + n0, :])
    grads = jnp.concatenate(blocks, axis=0)
    return grads, gp_b


def input_gradient(plan, back_ref, w, t, gp_b, stack):
    gu = t["sb"][...] * t["dt"][...] + t["gy"][...] * w["small"][SUB : SUB + 1, :] + dot(gp_b, w["x"][...].astype(BF16))
    return unplace(plan, back_ref, [gu[:, lane_tile(k)] for k in range(3)], stack)


def weight_shapes(plan):
    up = -(-(plan.rank + 2 * plan.states) // SUB) * SUB
    return {
        "x": (LANES, 3 * LANES),
        "small": (2 * SUB + plan.states, 3 * LANES),
        "rate": (plan.states, SUB, 3 * LANES),
        "dtp": (LANES, 3 * LANES),
    }, {"pad": (2, max(2 * SUB + plan.states, up), 2 * LANES)}


def token_shapes(plan):
    wide, narrow, double = (plan.rows, 3 * LANES), (plan.rows, LANES), (plan.rows, 2 * LANES)
    kept = {"u": wide, "m": wide, "z": wide, "dt": wide, "dtu": wide, "p": narrow,
            "bc": (2 * plan.states,) + double,
            "h": (plan.steps + 1, plan.states, plan.lines, 3 * LANES)}
    if plan.chunked:
        kept["a"] = (plan.steps, plan.states, plan.lines, 3 * LANES)
        kept["decay"] = (plan.states, SUB, 3 * LANES)
    own = {"y": wide, "x256": double}
    grads = {"gy": wide, "sb": wide, "wq": wide, "prod": (2 * plan.states,) + double,
             "gr": (plan.states, SUB, 3 * LANES), "x256": double}
    if plan.chunked:
        own["stack"] = (2 * plan.rows, 2 * LANES)
    return kept, own, grads


def token_mask(plan, tissue_ref, shape, axis):
    per = plan.rows // tissue_ref.shape[0]
    token = lax.broadcasted_iota(jnp.int32, shape, axis)
    mask = jnp.zeros(shape, F32)
    for k in range(tissue_ref.shape[0]):
        mask = jnp.where((token >= k * per) & (token < (k + 1) * per), tissue_ref[k].astype(F32), mask)
    return mask


def masked_rows(plan, tissue_ref, feat_ref):
    ch = plan.channels
    mask = token_mask(plan, tissue_ref, (SUB, plan.rows), 1)
    tall = jnp.concatenate([mask] * (ch // SUB), axis=0)
    fill = jnp.concatenate([mask] * ((2 * LANES - ch) // SUB), axis=0)
    return jnp.concatenate([feat_ref[...].astype(F32) * tall, fill], axis=0).astype(BF16)


def partner_rows(count, rows, s):
    return pl.ds(pl.multiple_of((lax.axis_index("band") ^ s) * (rows // count), SUB), rows // count)


def send_blocks(refs, tiles, scratch, width):
    scratch[:, :LANES], scratch[:, LANES:] = tiles
    send_from(refs, scratch, width)


def send_from(refs, scratch, width):
    if len(refs) == 1:
        refs[0][...] = scratch[:, :width].astype(BF16)
        return
    for s, ref in enumerate(refs):
        ref[...] = scratch[partner_rows(len(refs), scratch.shape[0], s), :width].astype(BF16)


def receive_blocks(refs, scratch):
    width = refs[0].shape[1]
    if len(refs) == 1:
        scratch[:, :width] = refs[0][...].astype(F32)
        return
    for s, ref in enumerate(refs):
        scratch[partner_rows(len(refs), scratch.shape[0], s), :width] = ref[...].astype(F32)


def rows_forward_kernel(plan, side, *refs):
    count = 9
    far, (send_refs, w, kept, rest, near, sems) = refs[:count], refs[count:]
    copies = [pltpu.make_async_copy(a, b, sems.at[k]) for k, (a, b) in enumerate(zip(far, near))]
    for copy in copies:
        copy.start()
    for copy in copies[:3]:
        copy.wait()
    tissue_ref, feat_ref, perm_ref, back_ref, x_ref, dtp_ref, bias_ref, alog_ref, skip_ref = near
    t = kept | rest
    w = w | rest
    placed = place(plan, perm_ref, masked_rows(plan, tissue_ref, feat_ref), t["u"], True)
    for copy in copies[4:]:
        copy.wait()
    load_weights(plan, side, x_ref, dtp_ref, bias_ref, alog_ref, skip_ref, w)
    prepare(plan, placed, w, t)
    forward(plan, w, t, True)
    copies[3].wait()
    tiles = [t["y"][:, k * LANES : (k + 1) * LANES] for k in range(3)]
    a, b = unplace(plan, back_ref, tiles, t.get("stack"))
    mask = token_mask(plan, tissue_ref, (plan.rows, LANES), 0)
    send_blocks(send_refs, (a, jnp.where(lane_iota(plan.rows) < plan.half, b, mask)), t["x256"], 2 * LANES)


def rows_backward_kernel(plan, side, gy_refs, perm_ref, w, kept, grads_v_ref, mine_ref, theirs_ref, late, rest):
    t = kept | rest | late
    receive_blocks(gy_refs, t["x256"])
    place(plan, perm_ref, t["x256"][...].astype(BF16), t["gy"])
    backward(plan, w, t)
    grads, gp_b = finish(plan, w, t)
    late["gp"][...] = gp_b
    other = grads_v_ref[...].astype(F32)
    odd = lax.axis_index("slide") % 2 == 1
    mine_ref[...] = jnp.where(odd, other, grads).astype(BF16)
    theirs_ref[...] = jnp.where(odd, grads, other).astype(BF16)


def rows_output_kernel(plan, side, tissue_ref, back_ref, w, kept, late, out_ref, own):
    a, b = input_gradient(plan, back_ref, w, kept | late, late["gp"][...], own["stack"])
    own["x256"][:, :LANES], own["x256"][:, LANES:] = a, b
    mask = token_mask(plan, tissue_ref, (SUB, plan.rows), 1)
    turned = jnp.transpose(own["x256"][...])[: plan.channels]
    out_ref[...] = (turned * jnp.concatenate([mask] * (plan.channels // SUB), axis=0)).astype(BF16)


def columns_kernel(plan, side, recv_refs, gy_ref, x_ref, dtp_ref, bias_ref, alog_ref, skip_ref,
                   mixed_ref, out_refs, grads_ref, t):
    ch = plan.channels
    w = t
    load_weights(plan, side, x_ref, dtp_ref, bias_ref, alog_ref, skip_ref, w)
    receive_blocks(recv_refs, t["x256"])
    low = lane_iota(plan.rows) < plan.half
    last = t["x256"][:, LANES:]
    mask = jnp.where(low, swap64(last), last)
    both = jnp.concatenate([t["x256"][:, :LANES] * mask, last * mask], axis=1)
    prepare(plan, place(plan, None, both, t["u"]), w, t)
    t["x256"][:, 0:ch] = gy_ref[...].astype(F32)
    place(plan, None, t["x256"][...], t["gy"])
    forward(plan, w, t, True)
    tiles = [t["y"][:, k * LANES : (k + 1) * LANES] for k in range(3)]
    a, b = unplace(plan, None, tiles, None)
    mixed_ref[:, :LANES] = a.astype(BF16)
    mixed_ref[:, LANES:] = b[:, : ch - LANES].astype(BF16)
    backward(plan, w, t)
    grads, gp_b = finish(plan, w, t)
    grads_ref[...] = grads.astype(BF16)
    a, b = input_gradient(plan, None, w, t, gp_b, None)
    mask = t["m"][:, :LANES]
    send_blocks(out_refs, (a * mask, b * mask), t["x256"], ch)


def tall_shapes(plan):
    steps, ch, nst = plan.steps, plan.channels, plan.states
    up = -(-(plan.rank + 2 * nst) // SUB) * SUB
    field = (steps, ch, LANES)
    ready = {"xs": (2 * up, ch), "ds": (2 * SUB, ch), "al": (2 * (nst + SUB), ch), "rb": (nst + 1, ch, LANES), "gy": field}
    kept = {"u": field, "bc": (steps, 2 * nst, SUB, LANES), "h": (steps, nst, ch, LANES)}
    rest = {
        "z": field, "dt": field, "dtu": field, "sb": field, "wq": field,
        "m": (steps, SUB, LANES), "p": (steps, up, LANES), "acc": (steps, 2 * nst, SUB, LANES),
        "a": (steps, nst, ch, LANES), "x256": (plan.rows, 2 * LANES),
    }
    every = steps * LANES
    late = {"gr": (nst, ch, LANES), "gpb": (2 * up, every, BF16), "rk": (2 * SUB, every, BF16),
            "gzb": (ch, every, BF16), "gyu": (ch, every, BF16), "ub": (ch, every, BF16)}
    return ready, kept, late, rest, {"pad": (2, up + SUB + nst, 2 * LANES)}


def tall_hot(plan):
    part = plan.states + SUB
    hot = np.zeros((6 * part, (plan.states + 1) * LANES), np.float32)
    for k in range(6 * part):
        d, n = k % (2 * part) // part, k % part
        if n <= plan.states:
            at = n * LANES + d * plan.half
            hot[k, at : at + plan.half] = 1.0
    return jnp.asarray(hot, BF16)


def by_step(plan, tiles):
    low = lane_iota(tiles[0].shape[0]) < plan.half
    out = []
    for s in range(plan.steps):
        mine, other = tiles[s // 2], tiles[(plan.steps - 1 - s) // 2]
        out.append(jnp.where(low, mine, other) if s % 2 == 0 else swap64(jnp.where(low, other, mine)))
    return out


def by_row(plan, fields):
    low = lane_iota(fields[0].shape[0]) < plan.half
    sums = []
    for s in range(0, plan.steps, 2):
        other = plan.steps - 1 - s
        even = fields[s] + swap64(fields[other])
        odd = swap64(fields[s + 1]) + fields[other - 1]
        sums.append(jnp.where(low, even, odd))
    return jnp.transpose(jnp.concatenate(sums, axis=1))


def tall_setup_kernel(plan, side, after_ref, gy_ref, hot_ref, x_ref, dtp_ref, bias_ref, alog_ref, skip_ref, t, own):
    ch, nst, rank = plan.channels, plan.states, plan.rank
    wide = rank + 2 * nst
    up = t["xs"].shape[0] // 2
    part = nst + SUB
    t["xs"][...] = jnp.zeros_like(t["xs"])
    t["ds"][...] = jnp.zeros_like(t["ds"])
    t["al"][...] = jnp.zeros_like(t["al"])
    for d in range(2):
        k = 2 * side + d
        t["xs"][d * up : d * up + wide, :] = x_ref[:, k, :]
        t["ds"][d * SUB : d * SUB + rank, :] = dtp_ref[:, k, :]
        t["ds"][d * SUB + rank : d * SUB + rank + 1, :] = bias_ref[k : k + 1, :]
        t["al"][d * part : d * part + nst, :] = -jnp.exp(alog_ref[k])
        t["al"][d * part + nst : d * part + nst + 1, :] = skip_ref[k : k + 1, :]
    scale = jnp.where(lax.broadcasted_iota(jnp.int32, (2 * part, ch), 0) % part < nst, LOG2E, 1.0)
    rest = t["al"][...] * scale
    parts = []
    for _ in range(3):
        parts.append(rest.astype(BF16))
        rest = rest - parts[-1].astype(F32)
    spread_rates = dot(jnp.concatenate(parts, axis=0), hot_ref[...], ((0,), (0,)))
    for n in range(nst + 1):
        t["rb"][n] = spread_rates[:, lane_tile(n)]
    own["x256"][:, 0:ch] = gy_ref[...].astype(F32)
    turned = jnp.transpose(own["x256"][...])
    for s, field in enumerate(by_step(plan, [turned[:ch, lane_tile(k)] for k in range(plan.steps // 2)])):
        t["gy"][s] = field


def tall_output_kernel(plan, side, kept, gain, mixed_ref, own):
    steps, ch, nst = plan.steps, plan.channels, plan.states

    each = 2 if ch % (2 * SUB) == 0 else 1

    def channels(c, carry):
        ats = [pl.ds(pl.multiple_of((c * each + k) * SUB, SUB), SUB) for k in range(each)]
        for s in range(steps):
            ys = [[gain[nst, at, :] * kept["u"][s, at, :], None] for at in ats]
            for n in range(nst):
                weight = kept["bc"][s, nst + n]
                for y, at in zip(ys, ats):
                    more = weight * kept["h"][s, n, at, :]
                    y[n % 2] = more if y[n % 2] is None else y[n % 2] + more
            for y, at in zip(ys, ats):
                own["y"][s, at, :] = y[0] + y[1]
        return carry

    lax.fori_loop(0, ch // (each * SUB), channels, 0)
    mixed_ref[...] = by_row(plan, [own["y"][s] for s in range(steps)]).astype(BF16)


def tall_columns_kernel(plan, side, recv_refs, ready, out_refs, kept, late, rest):
    steps, ch, nst, rank = plan.steps, plan.channels, plan.states, plan.rank
    t = ready | kept | late | rest
    up = t["p"].shape[1]
    part = nst + SUB
    rows0 = ((0,), (0,))
    lanes1 = ((1,), (1,))
    lanes = lane_tile
    x_hi, x_lo = split(t["xs"][...])
    d_hi, d_lo = split(t["ds"][...])

    low8 = lane_iota(SUB) < plan.half
    row8 = lax.broadcasted_iota(jnp.int32, (SUB, LANES), 0)
    receive_blocks(recv_refs, t["x256"])
    turned = jnp.transpose(t["x256"][...])
    for s, field in enumerate(by_step(plan, [turned[: ch + SUB, lanes(k)] for k in range(steps // 2)])):
        t["m"][s] = field[ch:]
        t["u"][s] = field[:ch] * jnp.concatenate([field[ch:]] * (ch // SUB), axis=0)
    u_b = jnp.concatenate([t["u"][s].astype(BF16) for s in range(steps)], axis=1)
    proj = dot(x_hi, u_b) + dot(x_lo, u_b)
    low_up = lane_iota(up) < plan.half
    ranks = []
    for s in range(steps):
        p = jnp.where(low_up, proj[:up, lanes(s)], proj[up:, lanes(s)])
        t["p"][s] = p
        one = jnp.where(row8 < rank, p[:SUB], jnp.where(row8 == rank, 1.0, 0.0))
        ranks.append(jnp.concatenate([jnp.where(low8, one, 0.0), jnp.where(low8, 0.0, one)], axis=0))
        for r in range(2 * nst):
            t["bc"][s, r] = jnp.broadcast_to(p[rank + r : rank + r + 1, :], (SUB, LANES))
    r_hi, r_lo = split(jnp.concatenate(ranks, axis=1))
    z = dot(d_hi, r_hi, rows0) + dot(d_lo, r_hi, rows0) + dot(d_hi, r_lo, rows0)
    for s in range(steps):
        z_s = z[:, lanes(s)]
        t["z"][s] = z_s
        soft = jnp.maximum(z_s, 0.0) + jnp.log1p(jnp.exp(-jnp.abs(z_s)))
        dt = soft * jnp.concatenate([t["m"][s]] * (ch // SUB), axis=0)
        t["dt"][s] = dt
        t["dtu"][s] = dt * t["u"][s]

    each = 3 if ch % (3 * SUB) == 0 else 1

    def channels_at(c):
        return [pl.ds(pl.multiple_of((c * each + k) * SUB, SUB), SUB) for k in range(each)]

    def scan_forward(c, carry):
        ats = channels_at(c)
        dts = [[t["dt"][s, at, :] for s in range(steps)] for at in ats]
        dtus = [[t["dtu"][s, at, :] for s in range(steps)] for at in ats]
        for n in range(nst):
            hs = [None] * each
            for s in range(steps):
                b = t["bc"][s, n]
                for k, at in enumerate(ats):
                    h = b * dtus[k][s]
                    if s:
                        a = jnp.exp2(dts[k][s] * t["rb"][n, at, :])
                        t["a"][s, n, at, :] = a
                        h = a * hs[k] + h
                    t["h"][s, n, at, :] = h
                    hs[k] = h
        return carry

    lax.fori_loop(0, ch // (each * SUB), scan_forward, 0)
    t["acc"][...] = jnp.zeros_like(t["acc"])

    def scan_backward(c, carry):
        ats = channels_at(c)
        zero = jnp.zeros((SUB, LANES), F32)
        sbs, wqs = [[zero] * steps for _ in ats], [[zero] * steps for _ in ats]
        for n in range(nst):
            after, g_rates = [None] * each, [None] * each
            for s in reversed(range(steps)):
                b, c_now = t["bc"][s, n], t["bc"][s, nst + n]
                to_b, to_c = t["acc"][s, n], t["acc"][s, nst + n]
                for k, at in enumerate(ats):
                    gy = t["gy"][s, at, :]
                    gh = c_now * gy
                    if after[k] is not None:
                        gh = gh + after[k]
                    to_b = to_b + gh * t["dtu"][s, at, :]
                    to_c = to_c + gy * t["h"][s, n, at, :]
                    sbs[k][s] = sbs[k][s] + gh * b
                    if s:
                        after[k] = t["a"][s, n, at, :] * gh
                        q = after[k] * t["h"][s - 1, n, at, :]
                        wqs[k][s] = wqs[k][s] + q * t["rb"][n, at, :]
                        more = q * t["dt"][s, at, :]
                        g_rates[k] = more if g_rates[k] is None else g_rates[k] + more
                t["acc"][s, n], t["acc"][s, nst + n] = to_b, to_c
            for k, at in enumerate(ats):
                t["gr"][n, at, :] = g_rates[k]
        for k, at in enumerate(ats):
            for s in range(steps):
                t["sb"][s, at, :] = sbs[k][s]
                t["wq"][s, at, :] = wqs[k][s]
        return carry

    lax.fori_loop(0, ch // (each * SUB), scan_backward, 0)

    gzs, gyus = [], []
    for s in range(steps):
        mask = jnp.concatenate([t["m"][s]] * (ch // SUB), axis=0)
        g_dt = t["wq"][s] * LN2 + t["sb"][s] * t["u"][s]
        gzs.append((g_dt * mask * (1.0 / (1.0 + jnp.exp(-t["z"][s])))).astype(BF16))
        gyus.append((t["gy"][s] * t["u"][s]).astype(BF16))
    gz_b = jnp.concatenate(gzs, axis=1)
    t["gzb"][...], t["gyu"][...], t["ub"][...], t["rk"][...] = gz_b, jnp.concatenate(gyus, axis=1), u_b, r_hi
    g_rank = dot(d_hi, gz_b)
    row_up = lax.broadcasted_iota(jnp.int32, (SUB, LANES), 0)
    g_ps = []
    for s in range(steps):
        tiles = [jnp.where(low8, g_rank[:SUB, lanes(s)], g_rank[SUB:, lanes(s)])]
        tiles += [jnp.zeros((SUB, LANES), F32)] * (up // SUB - 1)
        tiles[0] = jnp.where(row_up < rank, tiles[0], 0.0)
        for r in range(2 * nst):
            k, j = divmod(rank + r, SUB)
            tiles[k] = jnp.where(row_up == j, jnp.sum(t["acc"][s, r], axis=0, keepdims=True), tiles[k])
        g_p = jnp.concatenate(tiles, axis=0)
        g_ps.append(jnp.concatenate([jnp.where(low_up, g_p, 0.0), jnp.where(low_up, 0.0, g_p)], axis=0))
    gp_b = jnp.concatenate(g_ps, axis=1).astype(BF16)
    t["gpb"][...] = gp_b
    through = dot(x_hi, gp_b, rows0)
    gus = []
    for s in range(steps):
        mask = jnp.concatenate([t["m"][s]] * (ch // SUB), axis=0)
        gus.append((t["sb"][s] * t["dt"][s] + t["rb"][nst] * t["gy"][s] + through[:, lanes(s)]) * mask)
    t["x256"][:, 0:ch] = by_row(plan, gus)
    send_from(out_refs, t["x256"], ch)


def tall_grads_kernel(plan, side, t, al_ref, grads_ref, own):
    steps, ch, nst = plan.steps, plan.channels, plan.states
    part = nst + SUB
    lanes1 = ((1,), (1,))
    gp_b, u_b, r_hi, gz_b, gyu_b = t["gpb"][...], t["ub"][...], t["rk"][...], t["gzb"][...], t["gyu"][...]
    up = gp_b.shape[0] // 2
    low8 = lane_iota(SUB) < plan.half
    row8 = lax.broadcasted_iota(jnp.int32, (SUB, LANES), 0)
    g_x = dot(gp_b, u_b, lanes1)
    g_d = dot(r_hi, gz_b, lanes1)
    halves = jnp.where(row8 == 0, jnp.where(low8, 1.0, 0.0), jnp.where(row8 == 1, jnp.where(low8, 0.0, 1.0), 0.0)).astype(BF16)
    g_skip = dot(jnp.concatenate([halves] * steps, axis=1), gyu_b, lanes1)
    pad = own["pad"]
    row_d = lax.broadcasted_iota(jnp.int32, (SUB, ch), 0)
    for d in range(2):
        pad[d, 0:up, 0:ch] = g_x[d * up : (d + 1) * up]
        pad[d, up : up + SUB, 0:ch] = jnp.where(row_d == SUB - 1, g_skip[d : d + 1], g_d[d * SUB : (d + 1) * SUB])
    for n0 in range(0, nst, SUB):
        both = [jnp.zeros((SUB, ch), F32)] * 2
        for n in range(n0, n0 + SUB):
            sums = dot(halves, t["gr"][n].astype(BF16), lanes1)
            both = [jnp.where(row_d == n - n0, sums[d : d + 1], both[d]) for d in range(2)]
        for d in range(2):
            pad[d, up + SUB + n0 : up + 2 * SUB + n0, 0:ch] = both[d] * al_ref[d * part + n0 : d * part + n0 + SUB, :]
    first, second = pad[0], pad[1]
    tiles = pack_tiles(first[:, :LANES], first[:, LANES:], second[:, :LANES], second[:, LANES:])
    for k in range(3):
        grads_ref[:, lane_tile(k)] = tiles[k].astype(BF16)


def unpack_kernel(plan, mine_ref, theirs_ref, gx_ref, gd_ref, gb_ref, ga_ref, gs_ref):
    nst, rank, ch = plan.states, plan.rank, plan.channels
    wide = rank + 2 * nst
    up = -(-wide // SUB) * SUB
    odd = lax.axis_index("slide") % 2 == 1
    mine, theirs = mine_ref[...].astype(F32), theirs_ref[...].astype(F32)
    for side, total in enumerate((jnp.where(odd, theirs, mine), jnp.where(odd, mine, theirs))):
        tiles = [total[:, k * LANES : (k + 1) * LANES] for k in range(3)]
        for d, (a, b) in enumerate(((tiles[0], tiles[1]), (tiles[2], swap64(tiles[1])))):
            k = 2 * side + d
            for lo, hi, part in ((0, LANES, a), (LANES, ch, b[:, : ch - LANES])):
                gx_ref[:, k, lo:hi] = part[0:wide, :]
                gd_ref[:, k, lo:hi] = part[up : up + rank, :]
                gb_ref[k : k + 1, lo:hi] = part[up + SUB - 2 : up + SUB - 1, :]
                gs_ref[k : k + 1, lo:hi] = part[up + SUB - 1 : up + SUB, :]
                ga_ref[k, :, lo:hi] = part[up + SUB : up + SUB + nst, :]


def call(kernel, plan, side, out_shape, args, scratch, name, cost, scalars=0, far=()):
    whole = pl.BlockSpec(memory_space=pltpu.VMEM)
    specs = list(jax.tree.map(lambda _: whole, tuple(args)))
    if scalars:
        specs[0] = pl.BlockSpec(memory_space=pltpu.SMEM)
    scratches = [arrays(scratch, pltpu.VMEM)]
    limit = VMEM_SPARE + sum(int(np.prod(x.shape)) * x.dtype.itemsize for x in jax.tree.leaves(arrays(scratch)))
    if far:
        args = [pltpu.with_memory_space_constraint(a, pltpu.HBM) if k in far else a for k, a in enumerate(args)]
        for k in far:
            specs[k] = pl.BlockSpec(memory_space=pltpu.HBM)
        limit += sum(int(np.prod(args[k].shape)) * 4 for k in far)
        scratches += [[(pltpu.SMEM if args[k].ndim == 1 else pltpu.VMEM)(args[k].shape, args[k].dtype) for k in far], pltpu.SemaphoreType.DMA((len(far),))]
    return pl.pallas_call(
        functools.partial(kernel, plan, side), out_shape=out_shape, in_specs=tuple(specs),
        out_specs=jax.tree.map(lambda _: whole, out_shape), scratch_shapes=scratches,
        name=name, cost_estimate=pl.CostEstimate(flops=cost * 10**6, bytes_accessed=4 * 10**6, transcendentals=0),
        compiler_params=pltpu.CompilerParams(vmem_limit_bytes=limit),
    )(*args)


def arrays(shapes, make=jax.ShapeDtypeStruct):
    def one(shape):
        return make(shape, F32) if isinstance(shape[-1], int) else make(shape[:-1], shape[-1])

    return jax.tree.map(one, shapes, is_leaf=lambda x: isinstance(x, tuple))


def swap(x, axis, step):
    return lax.ppermute(x, axis, [(i, i ^ step) for i in range(lax.axis_size(axis))])


def cross(x, mask):
    axes = ("slide", "band")
    return lax.ppermute(x, axes, [(i, i ^ mask) for i in range(lax.axis_size(axes))])


def deliver(blocks, rows):
    bands = lax.axis_size("band")
    if len(blocks) == 1:
        block = blocks[0].reshape(bands, rows // bands, -1)
        return [lax.all_to_all(block, "band", split_axis=0, concat_axis=0, tiled=True).reshape(rows, -1)]
    got = {s: swap(blocks[s], "band", s) for s in reversed(range(1, bands))}
    return [blocks[0]] + [got[s] for s in range(1, bands)]


def shards(features, tissue, cotangent, x_proj, dt_proj, dt_bias, a_log, d_skip):
    _, _, width, channels = features.shape
    _, height, cols_here, _ = cotangent.shape
    bands = lax.axis_size("band")
    dirs, rank, states = dt_proj.shape[0], dt_proj.shape[1], a_log.shape[1]
    rows_plan = Plan(width // SUB, SUB, True, channels, states, rank)
    cols_plan = Plan(height, cols_here, False, channels, states, rank)
    weights = [jnp.transpose(x_proj, (2, 0, 1)), jnp.transpose(dt_proj, (1, 0, 2)), dt_bias, a_log, d_skip]
    feat = jnp.transpose(features.reshape(width, channels))
    keep = tissue.reshape(-1)
    packed = -(-(rank + 2 * states) // SUB) * SUB + SUB + states
    grads_shape = jax.ShapeDtypeStruct((packed, 3 * LANES), BF16)

    perm, back = rows_plan.perm()
    w_kept, w_own = weight_shapes(rows_plan)
    kept, own, grads = token_shapes(rows_plan)
    count = bands if bands in (2, 4) else 1
    tokens = height * cols_here

    def blocks(rows, lanes):
        return [jax.ShapeDtypeStruct((rows // count, lanes), BF16)] * count

    send, w_rows, t_rows = call(
        rows_forward_kernel, rows_plan, 0, (blocks(width, 2 * LANES), arrays(w_kept), arrays(kept)),
        [keep, feat, perm, back] + weights, own | w_own, "rows_forward", 4000, 0, tuple(range(9)))
    moved = deliver(send, width)
    cols_out = (jax.ShapeDtypeStruct((tokens, channels), BF16), blocks(tokens, channels), grads_shape)
    cols_in = [moved, cotangent.reshape(tokens, channels)]
    if 2 * cols_here == LANES and height % 2 == 0 and rank < SUB - 1:
        ready, kept_c, late_c, own_c, pad_c = tall_shapes(cols_plan)
        ready = call(tall_setup_kernel, cols_plan, 1, arrays(ready),
                     [w_rows["small"], cols_in[1], tall_hot(cols_plan)] + weights, {"x256": own_c["x256"]}, "columns_setup", 1000)
        grad_carried, kept_c, late_c = call(
            tall_columns_kernel, cols_plan, 1, (cols_out[1], arrays(kept_c), arrays(late_c)), [moved, ready], own_c, "columns", 8000)
        grads_v = call(tall_grads_kernel, cols_plan, 1, grads_shape, [late_c, ready["al"]], pad_c, "columns_grads", 1000)
        mixed = call(tall_output_kernel, cols_plan, 1, cols_out[0], [kept_c, ready["rb"]], {"y": own_c["z"]}, "columns_output", 1000)
    else:
        w_kept, w_own = weight_shapes(cols_plan)
        kept_c, own_c, grads_c = token_shapes(cols_plan)
        mixed, grad_carried, grads_v = call(
            columns_kernel, cols_plan, 1, cols_out, cols_in + weights,
            kept_c | own_c | grads_c | w_kept | w_own, "columns", 8000)
    returned = deliver(grad_carried, tokens)
    late = {k: grads.pop(k) for k in ("sb", "gy")} | {"gp": (width, LANES, BF16)}
    mine, theirs, late = call(
        rows_backward_kernel, rows_plan, 0, (grads_shape, grads_shape, arrays(late)),
        [returned, perm, w_rows, t_rows, grads_v], grads, "rows_backward", 8000)
    needed = {k: t_rows[k] for k in ("dt",)}
    grad_features = call(
        rows_output_kernel, rows_plan, 0, jax.ShapeDtypeStruct((channels, width), BF16),
        [keep, back, {k: w_rows[k] for k in ("small", "x")}, needed, late], {k: own[k] for k in ("stack", "x256")}, "rows_output", 1000, 1)
    mine = (mine.astype(F32) + swap(theirs, "slide", 1).astype(F32)).astype(BF16)
    hops = [bands << k for k in range(1, (lax.axis_size("slide") - 1).bit_length())]
    hops += [1 << k for k in range((bands - 1).bit_length())]
    late = [mixed, grad_features]
    while hops:
        first, hops = hops[:HOPS], hops[HOPS:]
        masks = [0]
        for hop in first:
            masks += [mask ^ hop for mask in masks]
        got = {mask: cross(mine, mask) for mask in reversed(masks[1:])}
        if late:
            hidden = late.pop(0)
            got, hidden = lax.optimization_barrier((got, hidden))
            if late:
                mixed = hidden
            else:
                grad_features = hidden
        terms = [mine.astype(F32)] + [got[mask].astype(F32) for mask in masks[1:]]
        while len(terms) > 1:
            terms = [a + b for a, b in zip(terms[::2], terms[1::2])]
        mine = terms[0].astype(BF16)
    theirs = swap(mine, "slide", 1)
    shapes = [(rank + 2 * states, dirs, channels), (rank, dirs, channels), (dirs, channels), (dirs, states, channels), (dirs, channels)]
    gx, gd, gb, ga, gs = pl.pallas_call(
        functools.partial(unpack_kernel, rows_plan), out_shape=[jax.ShapeDtypeStruct(s, F32) for s in shapes], name="unpack",
        compiler_params=pltpu.CompilerParams(vmem_limit_bytes=VMEM_LIMIT),
    )(mine, theirs)
    return (mixed.reshape(cotangent.shape), jnp.transpose(grad_features).reshape(features.shape), jnp.transpose(gx, (1, 2, 0)),
            jnp.transpose(gd, (1, 0, 2)), gb, ga, gs)


def solution(mesh):
    in_specs = (
        P(("groups", "slide"), "band", None, None),
        P(("groups", "slide"), "band", None),
        P(("groups", "slide"), None, "band", None),
        P(), P(), P(), P(), P(),
    )
    out_specs = (
        P(("groups", "slide"), None, "band", None),
        P(("groups", "slide"), "band", None, None),
        P("groups", None, None),
        P("groups", None, None),
        P("groups", None),
        P("groups", None, None),
        P("groups", None),
    )
    return jax.shard_map(shards, mesh=mesh, in_specs=in_specs, out_specs=out_specs, check_vma=False)
```
